32 devices in a mesh: gx: 8 (over z, x), gy: 4 (over y, core).
Axes of the slice: x: 2, y: 2, z: 4, core: 2. Of those that a mesh axis runs over, the one named last changes fastest.
Arguments:
- reference_scan: bfloat16 [128, 128, 2048], P('gx', 'gy'), may hold values from -6 to 6
- ref_gradient: bfloat16 [3, 128, 128, 2048], P(None, 'gx', 'gy'), may hold values from -6 to 6
- deformed_scan: bfloat16 [128, 128, 2048], P('gx', 'gy'), may hold values from -6 to 6
- interp_weights: bfloat16 [128, 128, 2048], P('gx', 'gy'), may hold values from 0 to 1
- sample_mask: int32 [128, 128, 2048], P('gx', 'gy'), may hold values from 0 to 1, as said below
- block_list: int32 [8, 16384], P('gx', 'gy'), may hold values from -1 to 8191, as said below
- offsets: int32 [2, 128, 128, 4], P(None, 'gx', 'gy'), may hold values from -4 to 4, as said below
Outputs:
- increment: float32 [3, 128, 128, 5], P(None, 'gx', 'gy')
- cg_residual: float32 [3, 128, 128, 5], P(None, 'gx', 'gy')
The draws below stay inside these ranges and needn't reach their ends.
Inputs may be any that keep to these rules, and one draw needn't show every extreme that they name: sample_mask is 0 in every block of 128 voxels that its device's block_list does not name. `block_list`: each device's 4096 entries are first distinct local block indices, then -1 to the end; some device names exactly 4096 blocks. `offsets`: both ends of the range occur.
All inputs are finite; a program needn't handle non-finite values.
Results may differ from the reference program's by a relative error of at most 0.0045.
Values may be sent and summed in bfloat16 or wider, within the bound.
A program may use at most 320 MiB of HBM per device.

```python
import jax
import jax.numpy as jnp
from jax import lax

EX = 16
EY = 32
EZ = 4
BOUND = 4
ITERS = 3
CAP = 4096
NEX = 128
NEY = 128
N_GX = 8
N_GY = 4


def live_blocks(key):
    base = jax.random.fold_in(key, 4021)
    split_keys = jax.random.split(base, 4)
    devices_total = N_GX * N_GY
    local_blocks = EX * EY * EZ * 4
    counts = jax.random.randint(split_keys[0], (devices_total,), CAP // 8, CAP + 1)
    busiest = jax.random.randint(split_keys[1], (), 0, devices_total)
    counts = jnp.where(jnp.arange(devices_total) == busiest, CAP, counts)
    orders = jax.vmap(lambda inner: jax.random.permutation(inner, local_blocks))(jax.random.split(split_keys[2], devices_total))
    ranks = jnp.argsort(orders, axis=1)
    listed = (ranks < counts[:, None]).astype(jnp.int32)
    chosen = jnp.where(jnp.arange(CAP)[None, :] < counts[:, None], orders[:, :CAP], -1)
    voxels = (jax.random.randint(split_keys[3], (devices_total, local_blocks, 128), 0, 10) < 6).astype(jnp.int32)
    voxels = voxels * listed[:, :, None]
    return (chosen.astype(jnp.int32), voxels)


def draw_sample_mask(key, part):
    chosen, voxels = live_blocks(key)
    grid = jnp.transpose(voxels.reshape(N_GX, N_GY, EX, EY, EZ * 512), (0, 2, 1, 3, 4))
    return grid.reshape(EX * N_GX, EY * N_GY, EZ * 512).astype(jnp.int32)


def draw_block_list(key, part):
    chosen, voxels = live_blocks(key)
    return chosen.reshape(N_GX, N_GY * CAP).astype(jnp.int32)


def draw_offsets(key, part):
    inner = jax.random.fold_in(key, 733)
    values = jax.random.randint(inner, (2, EX * N_GX, EY * N_GY, EZ), -BOUND, BOUND + 1)
    values = values.at[:, 0, 0, 0].set(BOUND)
    values = values.at[:, EX * N_GX - 1, EY * N_GY - 1, EZ - 1].set(-BOUND)
    return values.astype(jnp.int32)


def shard_levels(rng, extent, shards, smallest, top_value):
    level, own = 1.0, jax.random.fold_in(rng, 6)
    for dim, blocks in shards:
        heights = jnp.exp(jax.random.uniform(jax.random.fold_in(own, dim), (blocks,), jnp.float32, smallest / len(shards), top_value / len(shards)))
        level = level * jnp.repeat(heights, extent[dim] // blocks).reshape([-1 if axis == dim else 1 for axis in range(len(extent))])
    return level


def gaussian(stream_key, shape, width, limit, cuts=(), kind=jnp.bfloat16):
    result = jax.random.normal(stream_key, shape, jnp.float32) * width
    if len(cuts) > 0:
        result = shard_levels(stream_key, shape, cuts, -0.22, 0.18) * result
    return jnp.clip(result, min=-limit, max=limit).astype(kind)


def setup_inputs(seed: int = 0) -> dict:
    key_list = jax.random.split(jax.random.key(seed), 8)
    return {
        "reference_scan": gaussian(key_list[0], (NEX, NEY, EZ * 512), 1.0, 6.0, ((0, 8), (1, 4))),
        "ref_gradient": gaussian(key_list[1], (3, NEX, NEY, EZ * 512), 1.0, 6.0, ((1, 8), (2, 4))),
        "deformed_scan": gaussian(key_list[2], (NEX, NEY, EZ * 512), 1.0, 6.0, ((0, 8), (1, 4))),
        "interp_weights": jnp.clip(1.0 * jax.random.uniform(key_list[3], (NEX, NEY, EZ * 512), jnp.float32) ** shard_levels(key_list[3], (NEX, NEY, EZ * 512), ((0, 8), (1, 4)), -0.2, 0.2), 0.0, 1.0).astype(jnp.bfloat16),
        "sample_mask": draw_sample_mask(jax.random.fold_in(key_list[7], 71), 0),
        "block_list": draw_block_list(jax.random.fold_in(key_list[7], 71), 0),
        "offsets": draw_offsets(jax.random.fold_in(key_list[7], 71), 0),
    }


tikhonov = 8.0


def shape_table():
    voxel = jnp.arange(512)
    coords = [((voxel // 64).astype(jnp.float32) + 0.5) / 8.0, (((voxel // 8) % 8).astype(jnp.float32) + 0.5) / 8.0, ((voxel % 8).astype(jnp.float32) + 0.5) / 8.0]
    rows = []
    for node in range(8):
        bits = [(node >> 2) & 1, (node >> 1) & 1, node & 1]
        value = jnp.ones((512,), jnp.float32)
        for axis_pos in range(3):
            value = value * (coords[axis_pos] if bits[axis_pos] else 1.0 - coords[axis_pos])
        rows.append(value)
    return jnp.transpose(jnp.stack(rows).reshape(8, 4, 128), (1, 0, 2))


def reference(reference_scan, ref_gradient, deformed_scan, interp_weights, sample_mask, block_list, offsets):
    margin = BOUND + 1
    total_x = EX * N_GX
    total_y = EY * N_GY
    padded = jnp.pad(deformed_scan, ((margin, margin), (margin, margin), (0, 0)))
    span_y = total_y + 2 * margin
    flat_scan = padded.reshape(-1, EZ, 512)
    pos_x = jnp.arange(total_x)[:, None, None]
    pos_y = jnp.arange(total_y)[None, :, None]
    source = (pos_x + offsets[0] + margin) * span_y + pos_y + offsets[1] + margin
    layer = jnp.broadcast_to(jnp.arange(EZ)[None, None, :], source.shape)
    near = flat_scan[source, layer].astype(jnp.float32)
    far = flat_scan[source + span_y, layer].astype(jnp.float32)
    weights = interp_weights.reshape(total_x, total_y, EZ, 512).astype(jnp.float32)
    warped = weights * near + (1.0 - weights) * far
    residual_image = (reference_scan.reshape(total_x, total_y, EZ, 512).astype(jnp.float32) - warped).astype(jnp.bfloat16)
    devices_total = N_GX * N_GY
    local_blocks = EX * EY * EZ * 4
    elements = EX * EY * EZ

    def to_devices(array):
        moved = jnp.transpose(array.reshape(N_GX, EX, N_GY, EY, EZ * 512), (0, 2, 1, 3, 4))
        return moved.reshape(devices_total, local_blocks, 128)

    resid_dev = to_devices(residual_image.reshape(total_x, total_y, EZ * 512))
    mask_dev = to_devices(sample_mask)
    grad_dev = jnp.stack([to_devices(ref_gradient[comp]) for comp in range(3)], axis=1)
    lists = block_list.reshape(devices_total, CAP)
    table = shape_table()

    def per_device(parts):
        grads, resid, mask, entries = parts
        listed = entries >= 0
        safe = jnp.maximum(entries, 0)
        shapes = table[safe % 4]
        grad_rows = jnp.moveaxis(grads[:, safe], 0, 1).astype(jnp.float32)
        product = (shapes[:, :, None, :] * grad_rows[:, None, :, :]).reshape(CAP, 24, 128)
        jacobian = lax.optimization_barrier(product.astype(jnp.bfloat16)).astype(jnp.float32)
        sampled = mask[safe].astype(jnp.float32) * listed[:, None].astype(jnp.float32)
        weighted = jacobian * sampled[:, None, :]
        hessian = jnp.einsum("bdv,bev->bde", weighted, jacobian, precision=lax.Precision.HIGHEST)
        gradient = jnp.einsum("bdv,bv->bd", weighted, resid[safe].astype(jnp.float32), precision=lax.Precision.HIGHEST)
        elem_hess = jnp.zeros((elements, 24, 24), jnp.float32).at[safe // 4].add(hessian)
        elem_load = jnp.zeros((elements, 24), jnp.float32).at[safe // 4].add(gradient)
        return elem_hess, elem_load

    elem_hess, elem_load = lax.map(per_device, (grad_dev, resid_dev, mask_dev, lists))
    stiffness = jnp.transpose(elem_hess.reshape(N_GX, N_GY, EX, EY, EZ, 24, 24), (0, 2, 1, 3, 4, 5, 6)).reshape(total_x, total_y, EZ, 24, 24)
    loads = jnp.transpose(elem_load.reshape(N_GX, N_GY, EX, EY, EZ, 24), (0, 2, 1, 3, 4, 5)).reshape(total_x, total_y, EZ, 24)

    def spread(field):
        wide = jnp.pad(field, ((0, 0), (0, 1), (0, 1), (0, 0)))
        pieces = []
        for node in range(8):
            i_bit, j_bit, l_bit = (node >> 2) & 1, (node >> 1) & 1, node & 1
            pieces.append(wide[:, i_bit:i_bit + total_x, j_bit:j_bit + total_y, l_bit:l_bit + EZ])
        stacked = jnp.stack(pieces)
        return jnp.transpose(stacked, (2, 3, 4, 0, 1)).reshape(total_x, total_y, EZ, 24)

    def collect(values):
        parts = jnp.transpose(values.reshape(total_x, total_y, EZ, 8, 3), (3, 4, 0, 1, 2))
        total = jnp.zeros((3, total_x + 1, total_y + 1, EZ + 1), jnp.float32)
        for node in range(8):
            i_bit, j_bit, l_bit = (node >> 2) & 1, (node >> 1) & 1, node & 1
            total = total + jnp.pad(parts[node], ((0, 0), (i_bit, 1 - i_bit), (j_bit, 1 - j_bit), (l_bit, 1 - l_bit)))
        return total[:, :total_x, :total_y]

    def operate(field):
        images = jnp.einsum("xyzde,xyze->xyzd", stiffness, spread(field), precision=lax.Precision.HIGHEST)
        return collect(images) + tikhonov * field

    rhs = collect(loads)
    increment = jnp.zeros_like(rhs)
    cg_residual = rhs
    direction = rhs
    norm_now = jnp.sum(cg_residual * cg_residual)
    for sweep in range(ITERS):
        image = operate(direction)
        step_size = norm_now / jnp.sum(direction * image)
        increment = increment + step_size * direction
        cg_residual = cg_residual - step_size * image
        norm_next = jnp.sum(cg_residual * cg_residual)
        direction = cg_residual + (norm_next / norm_now) * direction
        norm_now = norm_next
    return increment, cg_residual
```

```python
import functools

import jax
import jax.numpy as jnp
import ml_dtypes
import numpy as np
from jax import lax
from jax.experimental import pallas as pl
from jax.experimental.pallas import tpu as pltpu
from jax.sharding import PartitionSpec as P

BOUND = 4
ITERS = 3
PHASES = ITERS + 1
EDGE = 8

tikhonov = 8.0
UNIT = 64.0

NODES = [(n >> 2 & 1, n >> 1 & 1, n & 1) for n in range(8)]
PAIRS = [(c, d) for c in range(3) for d in range(c, 3)]
PAIR_OF = {(c, d): PAIRS.index((min(c, d), max(c, d))) for c in range(3) for d in range(3)}
MESH = pl.DeviceIdType.MESH


def split(table, count):
    parts = []
    for _ in range(count):
        part = table.astype(ml_dtypes.bfloat16)
        parts.append(part)
        table = table - part.astype(np.float32)
    return parts


def tables():
    voxel = np.arange(512)
    coords = [
        ((voxel // 64).astype(np.float32) + np.float32(0.5)) / np.float32(8.0),
        ((voxel // 8 % 8).astype(np.float32) + np.float32(0.5)) / np.float32(8.0),
        ((voxel % 8).astype(np.float32) + np.float32(0.5)) / np.float32(8.0),
    ]
    linear = [[np.float32(1.0) - t, t] for t in coords]
    quad = [[s[0] * s[0], s[0] * s[1], s[1] * s[1]] for s in linear]
    shapes = np.stack([linear[0][i] * linear[1][j] * linear[2][l] for i, j, l in NODES])
    squares = np.stack(
        [quad[0][a] * quad[1][b] * quad[2][c] for a in range(3) for b in range(3) for c in range(3)]
    )
    squares = np.pad(squares, ((0, 5), (0, 0))) / np.float32(UNIT)
    square_table = np.concatenate(split(squares.astype(np.float32), 2), axis=0)
    shape_table = np.concatenate(split(shapes.astype(np.float32), 2), axis=0)
    return (square_table, shape_table)


def contract(table, part):
    return lax.dot_general(
        table, part, (((1,), (1,)), ((), ())), preferred_element_type=jnp.float32
    )


def row_of(step, tile_x):
    turn = jnp.maximum(step - tile_x, 0)
    return jnp.where(turn < tile_x - BOUND, turn + BOUND, tile_x - 1 - turn)


def step_kernel(
    sizes,
    tile_x,
    tile_y,
    depth,
    source_ref,
    square_ref,
    shape_ref,
    grad_ref,
    mask_ref,
    own_ref,
    image_ref,
    weight_ref,
    scan_ref,
    inc_ref,
    res_ref,
    before_ref,
    after_ref,
    beyond_ref,
    ahead_ref,
    wide_ref,
    masked_ref,
    part_ref,
    fetched_ref,
    high_ref,
    low_ref,
    hess_ref,
    load_ref,
    field_ref,
    value_ref,
    out_e,
    out_w,
    out_n,
    out_s,
    in_w,
    in_e,
    in_s,
    in_n,
    in_sw,
    in_ne,
    in_nw,
    in_se,
    own_x,
    got_x,
    own_y,
    got_y,
    halo_send,
    halo_recv,
    send_sems,
    recv_sems,
    send_x,
    recv_x,
    send_y,
    recv_y,
):
    step = pl.program_id(0)
    n_gx, n_gy = sizes
    gx = lax.axis_index("gx")
    gy = lax.axis_index("gy")
    not_first_x, not_last_x = (gx > 0, gx < n_gx - 1)
    not_first_y, not_last_y = (gy > 0, gy < n_gy - 1)
    both = jnp.logical_and
    wide = depth * tile_y
    span_x = tile_x + 2 * BOUND + 1
    stride_y = depth * span_x * 4

    def remote(source, target, sends, receives, device):
        return pltpu.make_async_remote_copy(
            src_ref=source,
            dst_ref=target,
            send_sem=sends,
            recv_sem=receives,
            device_id=device,
            device_id_type=MESH,
        )

    def halo(k, source, target, device):
        return remote(source, target, halo_send.at[k], halo_recv.at[k], device)

    every = slice(None)
    low_y, high_y = (pl.ds(0, EDGE), pl.ds(tile_y - EDGE, EDGE))
    near_y, far_y = ((gx, gy - 1), (gx, gy + 1))
    middle = pl.ds(BOUND, tile_x)

    def y_copies():
        return [
            (halo(0, scan_ref.at[every, low_y], beyond_ref.at[middle], near_y), not_first_y, not_last_y),
            (halo(1, scan_ref.at[every, high_y], ahead_ref.at[middle], far_y), not_last_y, not_first_y),
        ]

    def after_copy(k):
        return (halo(2 + k, scan_ref.at[k], after_ref.at[k], (gx - 1, gy)), not_first_x, not_last_x)

    def before_copy(k):
        source = scan_ref.at[tile_x - BOUND + k]
        return (
            halo(3 + BOUND + k, source, before_ref.at[k], (gx + 1, gy)),
            not_last_x,
            not_first_x,
        )

    def corner_copies(first, band, k, row, present):
        return [
            (
                halo(first, band.at[k, low_y], beyond_ref.at[row], near_y),
                both(present, not_first_y),
                both(present, not_last_y),
            ),
            (
                halo(first + 1, band.at[k, high_y], ahead_ref.at[row], far_y),
                both(present, not_last_y),
                both(present, not_first_y),
            ),
        ]

    def after_corners(k):
        first = 3 + 2 * BOUND + 2 * k
        return corner_copies(first, after_ref, k, BOUND + tile_x + k, not_last_x)

    def before_corners(k):
        first = 5 + 4 * BOUND + 2 * k
        return corner_copies(first, before_ref, k, k, not_first_x)

    def begin(copies):
        for one, sends, _ in copies:
            pl.when(sends)(one.start)

    def arrive(copies):
        for one, _, receives in copies:
            pl.when(receives)(one.wait_recv)

    def sent(copies):
        for one, sends, _ in copies:
            pl.when(sends)(one.wait_send)

    def put_wide(value, at_x, at_y):
        count = value.shape[0]
        for layer in range(depth):
            for chunk in range(4):
                lanes = slice(layer * 512 + chunk * 128, layer * 512 + chunk * 128 + 128)
                start = at_y * stride_y + (layer * span_x + at_x) * 4 + chunk
                wide_ref[pl.ds(start, count, stride=stride_y), :] = value[:, lanes]

    def put_sides(row, inside):
        value = beyond_ref[row].astype(jnp.float32)[0:BOUND]
        put_wide(jnp.where(both(inside, not_last_y), value, 0.0), row, BOUND + tile_y)
        value = ahead_ref[row].astype(jnp.float32)[EDGE - BOUND :]
        put_wide(jnp.where(both(inside, not_first_y), value, 0.0), row, 0)

    def put_band(band, k, row, inside):
        for first in range(0, tile_y, 16):
            value = band[k, pl.ds(first, 16), :].astype(jnp.float32)
            put_wide(jnp.where(inside, value, 0.0), row, BOUND + first)
        put_sides(row, inside)

    @pl.when(step == 0)
    def _():
        for buffer in (in_w, in_e, in_s, in_n, in_sw, in_ne, in_nw, in_se):
            buffer[...] = jnp.zeros_like(buffer)
        for buffer in (out_e, out_w, out_n, out_s):
            buffer[...] = jnp.zeros_like(buffer)
        barrier = pltpu.get_barrier_semaphore()
        for k in range(1, n_gx):
            pl.semaphore_signal(
                barrier, inc=1, device_id=((gx + k) % n_gx, gy), device_id_type=MESH
            )
        for k in range(1, n_gy):
            pl.semaphore_signal(
                barrier, inc=1, device_id=(gx, (gy + k) % n_gy), device_id_type=MESH
            )
        corners = 0
        for dx, there_x in ((-1, not_first_x), (1, not_last_x)):
            for dy, there_y in ((-1, not_first_y), (1, not_last_y)):
                present = both(there_x, there_y)
                corners = corners + jnp.where(present, 1, 0)

                @pl.when(present)
                def _(dx=dx, dy=dy):
                    pl.semaphore_signal(
                        barrier, inc=1, device_id=(gx + dx, gy + dy), device_id_type=MESH
                    )

        pl.semaphore_wait(barrier, n_gx - 1 + n_gy - 1 + corners)
        begin(y_copies())
        begin([after_copy(k) for k in range(BOUND + 1)])
        begin([before_copy(BOUND - 1 - k) for k in range(BOUND)])

    @pl.when(step < tile_x)
    def _():
        for first in range(0, tile_y, 16):
            value = own_ref[0, pl.ds(first, 16), :].astype(jnp.float32)
            put_wide(value, BOUND + step, BOUND + first)
        for layer in range(depth):
            lanes = pl.ds(layer * 512, 512)
            mask = mask_ref[0, :, lanes].astype(jnp.float32).astype(jnp.bfloat16)
            grads = [grad_ref[c, 0, :, lanes] for c in range(3)]
            masked = [mask * g for g in grads]
            for c in range(3):
                masked_ref[step, c, :, lanes] = masked[c]
            for q, (c, d) in enumerate(PAIRS):
                part_ref[pl.ds(q * wide + layer * tile_y, tile_y), :] = masked[c] * grads[d]
        table = square_ref[...]
        for q in range(6):
            total = contract(table, part_ref[pl.ds(q * wide, wide), :])
            value = total[0:32] + total[32:64]
            for first in range(0, 32, 8):
                rows = pl.ds((q * 32 + first) * tile_x + step, 8, stride=tile_x)
                hess_ref[rows, :] = value[first : first + 8]

    turn = step - tile_x

    @pl.when(turn == 0)
    def _():
        arrive(y_copies())

        def convert(i, carry):
            put_sides(BOUND + i, gx >= 0)
            return carry

        lax.fori_loop(0, tile_x, convert, 0)

    head = tile_x - 2 * BOUND - 1
    turned = tile_x - BOUND

    @pl.when(both(turn >= head - 2, turn < turned - 2))
    def _():
        k = turn - (head - 2)
        arrive([after_copy(k)])
        begin(after_corners(k))

    @pl.when(both(turn >= turned - 2, turn < tile_x - 2))
    def _():
        k = tile_x - 3 - turn
        arrive([before_copy(k)])
        begin(before_corners(k))

    @pl.when(both(turn >= head, turn < turned))
    def _():
        k = turn - head
        arrive(after_corners(k))
        put_band(after_ref, k, BOUND + tile_x + k, not_last_x)

    @pl.when(turn >= turned)
    def _():
        k = tile_x - 1 - turn
        arrive(before_corners(k))
        put_band(before_ref, k, k, not_first_x)

    @pl.when(turn >= 0)
    def _():
        x = row_of(step, tile_x)

        def fetch(block, carry):
            for inner in range(4):
                y = block * 4 + inner
                for layer in range(depth):
                    row = source_ref[(x * tile_y + y) * depth + layer]
                    rows = pl.ds(pl.multiple_of((y * depth + layer) * 8, 8), 8)
                    fetched_ref[rows, :] = wide_ref[pl.ds(row, 8), :]
            return carry

        lax.fori_loop(0, tile_y // 4, fetch, 0)
        for layer in range(depth):
            for chunk in range(4):
                lanes = pl.ds(layer * 512 + chunk * 128, 128)
                part = pl.ds(chunk * 128, 128)
                near = fetched_ref[pl.ds(layer * 8 + chunk, tile_y, stride=8 * depth), :]
                far = fetched_ref[pl.ds(layer * 8 + 4 + chunk, tile_y, stride=8 * depth), :]
                weight = weight_ref[0, :, lanes].astype(jnp.float32)
                warped = weight * near + (1.0 - weight) * far
                image = image_ref[0, :, lanes].astype(jnp.float32) - warped
                image = image.astype(jnp.bfloat16).astype(jnp.float32)
                for c in range(3):
                    rows = pl.ds(c * wide + layer * tile_y, tile_y)
                    value = image * masked_ref[x, c, :, lanes].astype(jnp.float32)
                    high = value.astype(jnp.bfloat16)
                    high_ref[rows, part] = high
                    low_ref[rows, part] = (value - high.astype(jnp.float32)).astype(jnp.bfloat16)
        table = shape_ref[...]
        for c in range(3):
            rows = pl.ds(c * wide, wide)
            total = contract(table, high_ref[rows, :]) + contract(table, low_ref[rows, :])
            load_ref[pl.ds(c * 8 * tile_x + x, 8, stride=tile_x), :] = total[0:8] + total[8:16]

    @pl.when(step == 2 * tile_x - 1)
    def _():
        width = wide
        lane = lax.broadcasted_iota(jnp.int32, (tile_x, width), 1)
        row = lax.broadcasted_iota(jnp.int32, (tile_x, width), 0)
        in_tile = lane % tile_y
        first_y = in_tile == 0
        last_y = in_tile == tile_y - 1
        first_x = row == 0
        last_x = row == tile_x - 1
        topmost = lane >= width - tile_y
        above = lane >= tile_y
        first_8, last_8 = (first_y[0:8], last_y[0:8])
        turn_y = tile_y - 1
        body, tail = (pl.ds(0, tile_x), pl.ds(tile_x, 8))
        upper, lower = (pl.ds(0, 8), pl.ds(8, 8))

        def roll(value, shift, axis):
            return pltpu.roll(value, shift % value.shape[axis], axis)

        def shift_x(value):
            return jnp.where(first_x, 0.0, roll(value, 1, 0))

        def copies(phase):
            table = [
                (out_e, None, in_w, 1, 0),
                (out_n, None, in_s, 0, 1),
                (out_e, lower, in_sw, 1, 1),
                (out_w, None, in_e, -1, 0),
                (out_s, None, in_n, 0, -1),
                (out_w, upper, in_ne, -1, -1),
                (out_e, upper, in_nw, 1, -1),
                (out_w, lower, in_se, -1, 1),
            ]
            if phase == PHASES - 1:
                table = table[:3]
            found = []
            for k, (src, rows, dst, dx, dy) in enumerate(table):
                send_ok, recv_ok = (gx >= 0, gx >= 0)
                if dx:
                    send_ok = not_last_x if dx > 0 else not_first_x
                    recv_ok = not_first_x if dx > 0 else not_last_x
                if dy:
                    send_ok = both(send_ok, not_last_y if dy > 0 else not_first_y)
                    recv_ok = both(recv_ok, not_first_y if dy > 0 else not_last_y)
                source = src.at[phase] if rows is None else src.at[phase, rows]
                one = remote(
                    source,
                    dst.at[phase],
                    send_sems.at[phase, k],
                    recv_sems.at[phase, k],
                    (gx + dx, gy + dy),
                )
                found.append((one, send_ok, recv_ok))
            return found

        def assemble(phase, partial, meanwhile):
            folded = {}
            for i in range(2):
                for j in range(2):
                    found = []
                    for c in range(3):
                        under = partial((4 * i + 2 * j) * 3 + c)
                        over = partial((4 * i + 2 * j + 1) * 3 + c)
                        found.append(under + jnp.where(above, roll(over, tile_y, 1), 0.0))
                        folded[i, j, 3 + c] = jnp.where(topmost, over, 0.0)
                    for c in range(3):
                        folded[i, j, c] = found[c]
            total, right = ([], [])
            north = jnp.zeros((tile_x, width), jnp.float32)
            south = jnp.zeros((tile_x, width), jnp.float32)
            for a in range(6):
                kept = [
                    folded[i, 0, a] + jnp.where(first_y, 0.0, roll(folded[i, 1, a], 1, 1))
                    for i in range(2)
                ]
                mine = kept[0] + shift_x(kept[1])
                side = folded[0, 1, a] + shift_x(folded[1, 1, a])
                edge_x = kept[1][tile_x - 1 :]
                edge_c = folded[1, 1, a][tile_x - 1 :]
                out_e[phase, a : a + 1, :] = edge_x
                out_e[phase, 8 + a : 9 + a, :] = edge_c
                out_w[phase, a : a + 1, :] = mine[0:1]
                out_w[phase, 8 + a : 9 + a, :] = side[0:1]
                out_n[phase, tile_x + a : tile_x + a + 1, :] = edge_c
                out_s[phase, tile_x + a : tile_x + a + 1, :] = edge_x
                north = jnp.where(in_tile == a, roll(side, a + 1, 1), north)
                south = jnp.where(in_tile == a, roll(mine, a, 1), south)
                total.append(mine)
                right.append(side)
            out_n[phase, body, :] = north
            out_s[phase, body, :] = south
            begin(copies(phase))
            meanwhile()
            arrive(copies(phase))
            line = in_w[phase, upper, :] + jnp.where(
                first_8, roll(in_sw[phase], -turn_y, 1), 0.0
            )
            from_s = in_s[phase, body, :]
            whole = [
                total[a]
                + jnp.where(first_x, line[a : a + 1], 0.0)
                + jnp.where(first_y, roll(from_s, -(tile_y + a), 1), 0.0)
                for a in range(6)
            ]
            if phase == PHASES - 1:
                return whole
            side_x = in_s[phase, tail, :] + in_se[phase]
            side_x = jnp.where(first_8, roll(side_x, -turn_y, 1), 0.0)
            side_x = jnp.where(not_last_x, out_e[phase, upper, :] + in_e[phase, upper, :] + side_x, 0.0)
            line = in_w[phase, lower, :] + roll(in_nw[phase], turn_y, 1)
            corner = in_n[phase, tail, :] + in_ne[phase]
            corner = out_e[phase, lower, :] + in_e[phase, lower, :] + roll(corner, turn_y, 1)
            corner = jnp.where(both(not_last_x, not_last_y), corner, 0.0)
            corner = jnp.where(last_8, corner, roll(side_x, -1, 1))
            from_n = in_n[phase, body, :]
            for a in range(6):
                side = right[a] + jnp.where(first_x, line[a : a + 1], 0.0)
                side = side + roll(from_n, turn_y - a, 1)
                side = jnp.where(not_last_y, side, 0.0)
                next_x = jnp.where(last_x, side_x[a : a + 1], roll(whole[a], -1, 0))
                next_y = jnp.where(last_y, side, roll(whole[a], -1, 1))
                next_c = jnp.where(last_x, corner[a : a + 1], roll(next_y, -1, 0))
                for k, value in enumerate((whole[a], next_y, next_x, next_c)):
                    if a < 3:
                        field_ref[6 * k + a] = value
                        field_ref[6 * k + 3 + a] = roll(value, -tile_y, 1)
                    else:
                        above_it = field_ref[6 * k + a]
                        field_ref[6 * k + a] = jnp.where(topmost, value, above_it)
            return whole

        def apply():
            for half in range(0, tile_x, 8):
                rows = pl.ds(half, 8)
                fields = [field_ref[k, rows, :] for k in range(24)]
                for n, (i, j, l) in enumerate(NODES):
                    for c in range(3):
                        total = None
                        for m, (p, q, r) in enumerate(NODES):
                            kind = (i + p) * 9 + (j + q) * 3 + l + r
                            for d in range(3):
                                index = (PAIR_OF[c, d] * 32 + kind) * tile_x + half
                                term = hess_ref[pl.ds(index, 8), :] * fields[3 * m + d]
                                total = term if total is None else total + term
                        value_ref[3 * n + c, rows, :] = total

        def exchange(own, got, sends, receives, index, count, target):
            return [
                remote(
                    own,
                    got.at[k - 1],
                    sends.at[k - 1],
                    receives.at[k - 1],
                    target((index + k) % count),
                )
                for k in range(1, count)
            ]

        def along_x():
            return exchange(own_x, got_x, send_x, recv_x, gx, n_gx, lambda t: (t, gy))

        def along_y():
            return exchange(own_y, got_y, send_y, recv_y, gy, n_gy, lambda t: (gx, t))

        def gather(found, own, got, count):
            for one in found:
                one.wait_recv()
            total = own[...]
            for k in range(1, count):
                total = total + got[k - 1]
            return total

        def inner(left, right):
            total = left[0] * right[0]
            for one, other in zip(left[1:], right[1:]):
                total = total + one * other
            return jnp.sum(total, axis=0, keepdims=True)

        def nothing():
            return None

        def load_part(k):
            start = ((k % 3) * 8 + k // 3) * tile_x
            return load_ref[pl.ds(start, tile_x), :]

        def value_part(k):
            return value_ref[k]

        base = [assemble(0, load_part, nothing)]
        for phase in range(1, ITERS):
            apply()
            base.append(assemble(phase, value_part, nothing))
        apply()
        last = inner([field_ref[k] for k in range(24)], [value_ref[k] for k in range(24)])
        rows = [
            inner(base[0], base[0]),
            inner(base[0], base[1]),
            inner(base[1], base[1]),
            inner(base[1], base[2]),
            inner(base[2], base[2]),
            last,
        ]
        for k in range(6):
            own_x[k : k + 1, :] = rows[k]
        own_x[6:8, :] = jnp.zeros((2, width), jnp.float32)
        for one in along_x():
            one.start()

        def pass_on():
            own_y[...] = gather(along_x(), own_x, got_x, n_gx)
            for one in along_y():
                one.start()

        base.append(assemble(ITERS, value_part, pass_on))
        sums = gather(along_y(), own_y, got_y, n_gy)
        sums = jnp.sum(sums, axis=1, keepdims=True)
        h = [sums[k : k + 1] for k in range(6)]
        sigma = tikhonov / UNIT
        a0 = h[1] / h[0]
        n1 = h[2] - a0 * h[1]
        a1 = (h[3] - 2.0 * a0 * h[2] + a0 * a0 * h[1]) / n1
        s = a0 + a1
        q = a0 * a1 - n1 / h[0]
        n2 = h[4] - s * h[3] + q * h[2]
        a2 = (h[5] - s * h[4] + q * h[3] - s * n2) / n2
        b2 = n2 / n1
        p2 = -(s + a2)
        p1 = q + a2 * s - b2
        p0 = b2 * a0 - a2 * q
        scale = 1.0 / (sigma * (sigma * (p2 - sigma) - p1) + p0)
        r2, r1, r0 = (p2 * scale, p1 * scale, p0 * scale)
        turn_back = -scale / UNIT
        i1 = (p2 - sigma) * turn_back
        i0 = (p1 - sigma * p2 + sigma * sigma) * turn_back
        for a in range(6):
            inc = turn_back * base[2][a] + i1 * base[1][a] + i0 * base[0][a]
            res = scale * base[3][a] + r2 * base[2][a] + r1 * base[1][a] + r0 * base[0][a]
            for out, value in ((inc_ref, inc), (res_ref, res)):
                if a < 3:
                    for layer in range(depth):
                        out[a, layer] = value[:, layer * tile_y : (layer + 1) * tile_y]
                else:
                    out[a - 3, depth] = value[:, width - tile_y :]
        for phase in range(PHASES):
            sent(copies(phase))
        for one in along_x() + along_y():
            one.wait_send()
        sent(y_copies())
        for k in range(BOUND + 1):
            sent([after_copy(k)] + after_corners(k))
        for k in range(BOUND):
            sent([before_copy(k)] + before_corners(k))


def per_device(
    reference_scan, ref_gradient, deformed_scan, interp_weights, sample_mask, block_list, offsets
):
    tile_x, tile_y, column = reference_scan.shape
    depth = column // 512
    width = depth * tile_y
    square_table, shape_table = tables()
    n_gx, n_gy = (lax.axis_size("gx"), lax.axis_size("gy"))
    span_x, span_y = (tile_x + 2 * BOUND + 1, tile_y + 2 * BOUND)
    pos_x = jnp.arange(tile_x)[:, None, None]
    pos_y = jnp.arange(tile_y)[None, :, None]
    layer = jnp.arange(depth)[None, None, :]
    source = (pos_y + offsets[1] + BOUND) * depth + layer
    source = (source * span_x + pos_x + offsets[0] + BOUND) * 4

    def first_pass(s):
        return jnp.minimum(s, tile_x - 1)

    def second_pass(s):
        return row_of(s, tile_x)

    def block(pick):
        return pl.BlockSpec((1, tile_y, column), lambda s: (pick(s), 0, 0))

    def whole(table):
        return pl.BlockSpec(table.shape, lambda s: (0, 0))

    f32, bf16, vmem, dma = (jnp.float32, jnp.bfloat16, pltpu.VMEM, pltpu.SemaphoreType.DMA)
    part = jax.ShapeDtypeStruct((3, depth + 1, tile_x, tile_y), f32)
    result = pl.BlockSpec(part.shape, lambda s: (0, 0, 0, 0))
    halos = 2 + 3 * (2 * BOUND + 1)
    increment, residual = pl.pallas_call(
        functools.partial(step_kernel, (n_gx, n_gy), tile_x, tile_y, depth),
        grid=(2 * tile_x,),
        out_shape=(part, part),
        in_specs=[
            pl.BlockSpec(memory_space=pltpu.SMEM),
            whole(square_table),
            whole(shape_table),
            pl.BlockSpec((3, 1, tile_y, column), lambda s: (0, first_pass(s), 0, 0)),
            block(first_pass),
            block(first_pass),
            block(second_pass),
            block(second_pass),
            pl.BlockSpec(memory_space=pl.ANY),
        ],
        out_specs=(result, result),
        scratch_shapes=[
            vmem((BOUND, tile_y, column), bf16),
            vmem((BOUND + 1, tile_y, column), bf16),
            vmem((span_x, EDGE, column), bf16),
            vmem((span_x, EDGE, column), bf16),
            vmem((span_y * depth * span_x * 4, 128), f32),
            vmem((tile_x, 3, tile_y, column), bf16),
            vmem((6 * width, 512), bf16),
            vmem((width * 8, 128), f32),
            vmem((3 * width, 512), bf16),
            vmem((3 * width, 512), bf16),
            vmem((6 * 32 * tile_x, width), f32),
            vmem((3 * 8 * tile_x, width), f32),
            vmem((24, tile_x, width), f32),
            vmem((24, tile_x, width), f32),
        ]
        + [
            vmem((PHASES, rows, width), f32)
            for rows in (16, 16, tile_x + 8, tile_x + 8) * 2 + (8, 8, 8, 8)
        ]
        + [
            vmem((8, width), f32),
            vmem((n_gx - 1, 8, width), f32),
            vmem((8, width), f32),
            vmem((n_gy - 1, 8, width), f32),
            dma((halos,)),
            dma((halos,)),
            dma((PHASES, 8)),
            dma((PHASES, 8)),
            dma((n_gx - 1,)),
            dma((n_gx - 1,)),
            dma((n_gy - 1,)),
            dma((n_gy - 1,)),
        ],
        compiler_params=pltpu.CompilerParams(collective_id=0, has_side_effects=True),
        name="step",
    )(
        source.reshape(-1),
        jnp.asarray(square_table),
        jnp.asarray(shape_table),
        ref_gradient,
        sample_mask,
        deformed_scan,
        reference_scan,
        interp_weights,
        deformed_scan,
    )

    def nodal(value):
        return jnp.transpose(value, (0, 2, 3, 1))

    return (nodal(increment), nodal(residual))


def solution(mesh):
    return jax.shard_map(
        per_device,
        mesh=mesh,
        in_specs=(
            P("gx", "gy", None),
            P(None, "gx", "gy", None),
            P("gx", "gy", None),
            P("gx", "gy", None),
            P("gx", "gy", None),
            P("gx", "gy"),
            P(None, "gx", "gy", None),
        ),
        out_specs=(P(None, "gx", "gy", None), P(None, "gx", "gy", None)),
        check_vma=False,
    )
```

```python
import functools

import jax
import jax.numpy as jnp
import ml_dtypes
import numpy as np
from jax import lax
from jax.experimental import pallas as pl
from jax.experimental.pallas import tpu as pltpu
from jax.sharding import PartitionSpec as P

BOUND = 4
ITERS = 3
PHASES = ITERS + 1
EDGE = 8

tikhonov = 8.0
UNIT = 64.0

NODES = [(n >> 2 & 1, n >> 1 & 1, n & 1) for n in range(8)]
PAIRS = [(c, d) for c in range(3) for d in range(c, 3)]
PAIR_OF = {(c, d): PAIRS.index((min(c, d), max(c, d))) for c in range(3) for d in range(3)}
MESH = pl.DeviceIdType.MESH


def split(table, count):
    parts = []
    for _ in range(count):
        part = table.astype(ml_dtypes.bfloat16)
        parts.append(part)
        table = table - part.astype(np.float32)
    return parts


def tables():
    voxel = np.arange(512)
    coords = [
        ((voxel // 64).astype(np.float32) + np.float32(0.5)) / np.float32(8.0),
        ((voxel // 8 % 8).astype(np.float32) + np.float32(0.5)) / np.float32(8.0),
        ((voxel % 8).astype(np.float32) + np.float32(0.5)) / np.float32(8.0),
    ]
    linear = [[np.float32(1.0) - t, t] for t in coords]
    quad = [[s[0] * s[0], s[0] * s[1], s[1] * s[1]] for s in linear]
    shapes = np.stack([linear[0][i] * linear[1][j] * linear[2][l] for i, j, l in NODES])
    squares = np.stack(
        [quad[0][a] * quad[1][b] * quad[2][c] for a in range(3) for b in range(3) for c in range(3)]
    )
    squares = np.pad(squares, ((0, 5), (0, 0))) / np.float32(UNIT)
    square_table = np.concatenate(split(squares.astype(np.float32), 2), axis=0)
    shape_table = np.concatenate(split(shapes.astype(np.float32), 2), axis=0)
    return (square_table, shape_table)


def contract(table, part):
    return lax.dot_general(
        table, part, (((1,), (1,)), ((), ())), preferred_element_type=jnp.float32
    )


def row_of(turn, tile_x):
    return jnp.where(turn < tile_x - BOUND, turn + BOUND, tile_x - 1 - turn)


def step_kernel(
    sizes,
    tile_x,
    tile_y,
    depth,
    offset_ref,
    square_ref,
    shape_ref,
    grad_hbm,
    mask_hbm,
    scan_ref,
    image_hbm,
    weight_hbm,
    out_ref,
    grad_ref,
    mask_ref,
    own_ref,
    image_ref,
    weight_ref,
    before_ref,
    after_ref,
    beyond_ref,
    ahead_ref,
    wide_ref,
    part_ref,
    fetched_ref,
    high_ref,
    low_ref,
    hess_ref,
    load_ref,
    field_ref,
    value_ref,
    out_e,
    out_w,
    out_n,
    out_s,
    in_w,
    in_e,
    in_s,
    in_n,
    in_sw,
    in_ne,
    in_nw,
    in_se,
    own_x,
    got_x,
    own_y,
    got_y,
    table_ref,
    source_ref,
    local_sems,
    halo_send,
    halo_recv,
    send_sems,
    recv_sems,
    send_x,
    recv_x,
    send_y,
    recv_y,
):
    n_gx, n_gy = sizes
    gx = lax.axis_index("gx")
    gy = lax.axis_index("gy")
    not_first_x, not_last_x = (gx > 0, gx < n_gx - 1)
    not_first_y, not_last_y = (gy > 0, gy < n_gy - 1)
    both = jnp.logical_and
    wide = depth * tile_y
    span_x = tile_x + 2 * BOUND + 1
    stride_y = depth * span_x * 4

    def remote(source, target, sends, receives, device):
        return pltpu.make_async_remote_copy(
            src_ref=source,
            dst_ref=target,
            send_sem=sends,
            recv_sem=receives,
            device_id=device,
            device_id_type=MESH,
        )

    def halo(k, source, target, device):
        return remote(source, target, halo_send.at[k], halo_recv.at[k], device)

    every = slice(None)
    low_y, high_y = (pl.ds(0, EDGE), pl.ds(tile_y - EDGE, EDGE))
    near_y, far_y = ((gx, gy - 1), (gx, gy + 1))
    middle = pl.ds(BOUND, tile_x)

    def y_copies():
        return [
            (halo(0, scan_ref.at[every, low_y], beyond_ref.at[middle], near_y), not_first_y, not_last_y),
            (halo(1, scan_ref.at[every, high_y], ahead_ref.at[middle], far_y), not_last_y, not_first_y),
        ]

    def after_copy(k):
        return (halo(2 + k, scan_ref.at[k], after_ref.at[k], (gx - 1, gy)), not_first_x, not_last_x)

    def before_copy(k):
        source = scan_ref.at[tile_x - BOUND + k]
        return (
            halo(3 + BOUND + k, source, before_ref.at[k], (gx + 1, gy)),
            not_last_x,
            not_first_x,
        )

    def corner_copies(first, band, k, row, present):
        return [
            (
                halo(first, band.at[k, low_y], beyond_ref.at[row], near_y),
                both(present, not_first_y),
                both(present, not_last_y),
            ),
            (
                halo(first + 1, band.at[k, high_y], ahead_ref.at[row], far_y),
                both(present, not_last_y),
                both(present, not_first_y),
            ),
        ]

    def after_corners(k):
        first = 3 + 2 * BOUND + 2 * k
        return corner_copies(first, after_ref, k, BOUND + tile_x + k, not_last_x)

    def before_corners(k):
        first = 5 + 4 * BOUND + 2 * k
        return corner_copies(first, before_ref, k, k, not_first_x)

    def begin(copies):
        for one, sends, _ in copies:
            pl.when(sends)(one.start)

    def arrive(copies):
        for one, _, receives in copies:
            pl.when(receives)(one.wait_recv)

    def sent(copies):
        for one, sends, _ in copies:
            pl.when(sends)(one.wait_send)

    def put_wide(value, at_x, at_y):
        count = value.shape[0]
        for layer in range(depth):
            for chunk in range(4):
                lanes = slice(layer * 512 + chunk * 128, layer * 512 + chunk * 128 + 128)
                start = at_y * stride_y + (layer * span_x + at_x) * 4 + chunk
                wide_ref[pl.ds(start, count, stride=stride_y), :] = value[:, lanes]

    def put_sides(row, inside):
        value = beyond_ref[row].astype(jnp.float32)[0:BOUND]
        put_wide(jnp.where(both(inside, not_last_y), value, 0.0), row, BOUND + tile_y)
        value = ahead_ref[row].astype(jnp.float32)[EDGE - BOUND :]
        put_wide(jnp.where(both(inside, not_first_y), value, 0.0), row, 0)

    def put_band(band, k, row, inside):
        for first in range(0, tile_y, 16):
            value = band[k, pl.ds(first, 16), :].astype(jnp.float32)
            put_wide(jnp.where(inside, value, 0.0), row, BOUND + first)
        put_sides(row, inside)

    def first_copies(x):
        return [
            pltpu.make_async_copy(grad_hbm.at[:, x], grad_ref.at[:, x], local_sems.at[0, x]),
            pltpu.make_async_copy(mask_hbm.at[x], mask_ref.at[x], local_sems.at[1, x]),
            pltpu.make_async_copy(scan_ref.at[x], own_ref.at[x], local_sems.at[2, x]),
        ]

    def second_copies(x):
        return [
            pltpu.make_async_copy(image_hbm.at[x], image_ref.at[x], local_sems.at[3, x]),
            pltpu.make_async_copy(weight_hbm.at[x], weight_ref.at[x], local_sems.at[4, x]),
        ]

    def start_first(x, carry):
        for one in first_copies(x):
            one.start()
        return carry

    def start_second(turn, carry):
        for one in second_copies(row_of(turn, tile_x)):
            one.start()
        return carry

    for buffer in (in_w, in_e, in_s, in_n, in_sw, in_ne, in_nw, in_se):
        buffer[...] = jnp.zeros_like(buffer)
    for buffer in (out_e, out_w, out_n, out_s):
        buffer[...] = jnp.zeros_like(buffer)
    barrier = pltpu.get_barrier_semaphore()
    for k in range(1, n_gx):
        pl.semaphore_signal(
            barrier, inc=1, device_id=((gx + k) % n_gx, gy), device_id_type=MESH
        )
    for k in range(1, n_gy):
        pl.semaphore_signal(
            barrier, inc=1, device_id=(gx, (gy + k) % n_gy), device_id_type=MESH
        )
    corners = 0
    for dx, there_x in ((-1, not_first_x), (1, not_last_x)):
        for dy, there_y in ((-1, not_first_y), (1, not_last_y)):
            present = both(there_x, there_y)
            corners = corners + jnp.where(present, 1, 0)

            @pl.when(present)
            def _(dx=dx, dy=dy):
                pl.semaphore_signal(
                    barrier, inc=1, device_id=(gx + dx, gy + dy), device_id_type=MESH
                )

    lax.fori_loop(0, tile_x, start_first, 0)
    extent = (tile_x, depth, tile_y)
    pos_x, layers, pos_y = [lax.broadcasted_iota(jnp.int32, extent, k) for k in range(3)]
    table = (pos_y + offset_ref[1] + BOUND) * depth + layers
    table_ref[...] = (table * span_x + pos_x + offset_ref[0] + BOUND) * 4
    table_copy = pltpu.make_async_copy(table_ref, source_ref, local_sems.at[5, 0])
    table_copy.start()
    pl.semaphore_wait(barrier, n_gx - 1 + n_gy - 1 + corners)
    begin(y_copies())
    begin([after_copy(k) for k in range(BOUND + 1)])
    begin([before_copy(BOUND - 1 - k) for k in range(BOUND)])
    lax.fori_loop(0, tile_x, start_second, 0)

    def hessian_row(x, carry):
        for one in first_copies(x):
            one.wait()
        for first in range(0, tile_y, 16):
            value = own_ref[x, pl.ds(first, 16), :].astype(jnp.float32)
            put_wide(value, BOUND + x, BOUND + first)
        for layer in range(depth):
            lanes = pl.ds(layer * 512, 512)
            mask = mask_ref[x, :, lanes].astype(jnp.float32).astype(jnp.bfloat16)
            grads = [grad_ref[c, x, :, lanes] for c in range(3)]
            masked = [mask * g for g in grads]
            for c in range(3):
                grad_ref[c, x, :, lanes] = masked[c]
            for q, (c, d) in enumerate(PAIRS):
                part_ref[pl.ds(q * wide + layer * tile_y, tile_y), :] = masked[c] * grads[d]
        table = square_ref[...]
        for q in range(6):
            total = contract(table, part_ref[pl.ds(q * wide, wide), :])
            value = total[0:32] + total[32:64]
            for first in range(0, 32, 8):
                rows = pl.ds((q * 32 + first) * tile_x + x, 8, stride=tile_x)
                hess_ref[rows, :] = value[first : first + 8]
        return carry

    lax.fori_loop(0, tile_x, hessian_row, 0)
    table_copy.wait()
    arrive(y_copies())

    def convert(i, carry):
        put_sides(BOUND + i, gx >= 0)
        return carry

    lax.fori_loop(0, tile_x, convert, 0)
    head = tile_x - 2 * BOUND - 1
    turned = tile_x - BOUND

    def load_row(turn, carry):
        @pl.when(both(turn >= head - 2, turn < turned - 2))
        def _():
            k = turn - (head - 2)
            arrive([after_copy(k)])
            begin(after_corners(k))

        @pl.when(both(turn >= turned - 2, turn < tile_x - 2))
        def _():
            k = tile_x - 3 - turn
            arrive([before_copy(k)])
            begin(before_corners(k))

        @pl.when(both(turn >= head, turn < turned))
        def _():
            k = turn - head
            arrive(after_corners(k))
            put_band(after_ref, k, BOUND + tile_x + k, not_last_x)

        @pl.when(turn >= turned)
        def _():
            k = tile_x - 1 - turn
            arrive(before_corners(k))
            put_band(before_ref, k, k, not_first_x)

        x = row_of(turn, tile_x)
        for one in second_copies(x):
            one.wait()

        def fetch(block, inner_carry):
            for inner in range(4):
                y = block * 4 + inner
                for layer in range(depth):
                    row = source_ref[x, layer, y]
                    rows = pl.ds(pl.multiple_of((y * depth + layer) * 8, 8), 8)
                    fetched_ref[rows, :] = wide_ref[pl.ds(row, 8), :]
            return inner_carry

        lax.fori_loop(0, tile_y // 4, fetch, 0)
        for layer in range(depth):
            for chunk in range(4):
                lanes = pl.ds(layer * 512 + chunk * 128, 128)
                part = pl.ds(chunk * 128, 128)
                near = fetched_ref[pl.ds(layer * 8 + chunk, tile_y, stride=8 * depth), :]
                far = fetched_ref[pl.ds(layer * 8 + 4 + chunk, tile_y, stride=8 * depth), :]
                weight = weight_ref[x, :, lanes].astype(jnp.float32)
                warped = weight * near + (1.0 - weight) * far
                image = image_ref[x, :, lanes].astype(jnp.float32) - warped
                image = image.astype(jnp.bfloat16).astype(jnp.float32)
                for c in range(3):
                    rows = pl.ds(c * wide + layer * tile_y, tile_y)
                    value = image * grad_ref[c, x, :, lanes].astype(jnp.float32)
                    high = value.astype(jnp.bfloat16)
                    high_ref[rows, part] = high
                    low_ref[rows, part] = (value - high.astype(jnp.float32)).astype(jnp.bfloat16)
        table = shape_ref[...]
        for c in range(3):
            rows = pl.ds(c * wide, wide)
            total = contract(table, high_ref[rows, :]) + contract(table, low_ref[rows, :])
            load_ref[pl.ds(c * 8 * tile_x + x, 8, stride=tile_x), :] = total[0:8] + total[8:16]
        return carry

    lax.fori_loop(0, tile_x, load_row, 0)

    width = wide
    lane = lax.broadcasted_iota(jnp.int32, (tile_x, width), 1)
    row = lax.broadcasted_iota(jnp.int32, (tile_x, width), 0)
    in_tile = lane % tile_y
    first_y = in_tile == 0
    last_y = in_tile == tile_y - 1
    first_x = row == 0
    last_x = row == tile_x - 1
    topmost = lane >= width - tile_y
    above = lane >= tile_y
    first_8, last_8 = (first_y[0:8], last_y[0:8])
    turn_y = tile_y - 1
    body, tail = (pl.ds(0, tile_x), pl.ds(tile_x, 8))
    upper, lower = (pl.ds(0, 8), pl.ds(8, 8))

    def roll(value, shift, axis):
        return pltpu.roll(value, shift % value.shape[axis], axis)

    def shift_x(value):
        return jnp.where(first_x, 0.0, roll(value, 1, 0))

    def copies(phase):
        table = [
            (out_e, None, in_w, 1, 0),
            (out_n, None, in_s, 0, 1),
            (out_e, lower, in_sw, 1, 1),
            (out_w, None, in_e, -1, 0),
            (out_s, None, in_n, 0, -1),
            (out_w, upper, in_ne, -1, -1),
            (out_e, upper, in_nw, 1, -1),
            (out_w, lower, in_se, -1, 1),
        ]
        if phase == PHASES - 1:
            table = table[:3]
        found = []
        for k, (src, rows, dst, dx, dy) in enumerate(table):
            send_ok, recv_ok = (gx >= 0, gx >= 0)
            if dx:
                send_ok = not_last_x if dx > 0 else not_first_x
                recv_ok = not_first_x if dx > 0 else not_last_x
            if dy:
                send_ok = both(send_ok, not_last_y if dy > 0 else not_first_y)
                recv_ok = both(recv_ok, not_first_y if dy > 0 else not_last_y)
            source = src.at[phase] if rows is None else src.at[phase, rows]
            one = remote(
                source,
                dst.at[phase],
                send_sems.at[phase, k],
                recv_sems.at[phase, k],
                (gx + dx, gy + dy),
            )
            found.append((one, send_ok, recv_ok))
        return found

    def assemble(phase, partial, meanwhile):
        folded = {}
        for i in range(2):
            for j in range(2):
                found = []
                for c in range(3):
                    under = partial((4 * i + 2 * j) * 3 + c)
                    over = partial((4 * i + 2 * j + 1) * 3 + c)
                    found.append(under + jnp.where(above, roll(over, tile_y, 1), 0.0))
                    folded[i, j, 3 + c] = jnp.where(topmost, over, 0.0)
                for c in range(3):
                    folded[i, j, c] = found[c]
        total, right = ([], [])
        north = jnp.zeros((tile_x, width), jnp.float32)
        south = jnp.zeros((tile_x, width), jnp.float32)
        for a in range(6):
            kept = [
                folded[i, 0, a] + jnp.where(first_y, 0.0, roll(folded[i, 1, a], 1, 1))
                for i in range(2)
            ]
            mine = kept[0] + shift_x(kept[1])
            side = folded[0, 1, a] + shift_x(folded[1, 1, a])
            edge_x = kept[1][tile_x - 1 :]
            edge_c = folded[1, 1, a][tile_x - 1 :]
            out_e[phase, a : a + 1, :] = edge_x
            out_e[phase, 8 + a : 9 + a, :] = edge_c
            out_w[phase, a : a + 1, :] = mine[0:1]
            out_w[phase, 8 + a : 9 + a, :] = side[0:1]
            out_n[phase, tile_x + a : tile_x + a + 1, :] = edge_c
            out_s[phase, tile_x + a : tile_x + a + 1, :] = edge_x
            north = jnp.where(in_tile == a, roll(side, a + 1, 1), north)
            south = jnp.where(in_tile == a, roll(mine, a, 1), south)
            total.append(mine)
            right.append(side)
        out_n[phase, body, :] = north
        out_s[phase, body, :] = south
        begin(copies(phase))
        meanwhile()
        arrive(copies(phase))
        line = in_w[phase, upper, :] + jnp.where(
            first_8, roll(in_sw[phase], -turn_y, 1), 0.0
        )
        from_s = in_s[phase, body, :]
        whole = [
            total[a]
            + jnp.where(first_x, line[a : a + 1], 0.0)
            + jnp.where(first_y, roll(from_s, -(tile_y + a), 1), 0.0)
            for a in range(6)
        ]
        if phase == PHASES - 1:
            return whole
        side_x = in_s[phase, tail, :] + in_se[phase]
        side_x = jnp.where(first_8, roll(side_x, -turn_y, 1), 0.0)
        side_x = jnp.where(not_last_x, out_e[phase, upper, :] + in_e[phase, upper, :] + side_x, 0.0)
        line = in_w[phase, lower, :] + roll(in_nw[phase], turn_y, 1)
        corner = in_n[phase, tail, :] + in_ne[phase]
        corner = out_e[phase, lower, :] + in_e[phase, lower, :] + roll(corner, turn_y, 1)
        corner = jnp.where(both(not_last_x, not_last_y), corner, 0.0)
        corner = jnp.where(last_8, corner, roll(side_x, -1, 1))
        from_n = in_n[phase, body, :]
        for a in range(6):
            side = right[a] + jnp.where(first_x, line[a : a + 1], 0.0)
            side = side + roll(from_n, turn_y - a, 1)
            side = jnp.where(not_last_y, side, 0.0)
            next_x = jnp.where(last_x, side_x[a : a + 1], roll(whole[a], -1, 0))
            next_y = jnp.where(last_y, side, roll(whole[a], -1, 1))
            next_c = jnp.where(last_x, corner[a : a + 1], roll(next_y, -1, 0))
            for k, value in enumerate((whole[a], next_y, next_x, next_c)):
                if a < 3:
                    field_ref[6 * k + a] = value
                    field_ref[6 * k + 3 + a] = roll(value, -tile_y, 1)
                else:
                    above_it = field_ref[6 * k + a]
                    field_ref[6 * k + a] = jnp.where(topmost, value, above_it)
        return whole

    def apply():
        for half in range(0, tile_x, 8):
            rows = pl.ds(half, 8)
            fields = [field_ref[k, rows, :] for k in range(24)]
            for n, (i, j, l) in enumerate(NODES):
                for c in range(3):
                    total = None
                    for m, (p, q, r) in enumerate(NODES):
                        kind = (i + p) * 9 + (j + q) * 3 + l + r
                        for d in range(3):
                            index = (PAIR_OF[c, d] * 32 + kind) * tile_x + half
                            term = hess_ref[pl.ds(index, 8), :] * fields[3 * m + d]
                            total = term if total is None else total + term
                    value_ref[3 * n + c, rows, :] = total

    def exchange(own, got, sends, receives, index, count, target):
        return [
            remote(
                own,
                got.at[k - 1],
                sends.at[k - 1],
                receives.at[k - 1],
                target((index + k) % count),
            )
            for k in range(1, count)
        ]

    def along_x():
        return exchange(own_x, got_x, send_x, recv_x, gx, n_gx, lambda t: (t, gy))

    def along_y():
        return exchange(own_y, got_y, send_y, recv_y, gy, n_gy, lambda t: (gx, t))

    def gather(found, own, got, count):
        for one in found:
            one.wait_recv()
        total = own[...]
        for k in range(1, count):
            total = total + got[k - 1]
        return total

    def inner(left, right):
        total = left[0] * right[0]
        for one, other in zip(left[1:], right[1:]):
            total = total + one * other
        return jnp.sum(total, axis=0, keepdims=True)

    def nothing():
        return None

    def load_part(k):
        start = ((k % 3) * 8 + k // 3) * tile_x
        return load_ref[pl.ds(start, tile_x), :]

    def value_part(k):
        return value_ref[k]

    base = [assemble(0, load_part, nothing)]
    for phase in range(1, ITERS):
        apply()
        base.append(assemble(phase, value_part, nothing))
    apply()
    last = inner([field_ref[k] for k in range(24)], [value_ref[k] for k in range(24)])
    rows = [
        inner(base[0], base[0]),
        inner(base[0], base[1]),
        inner(base[1], base[1]),
        inner(base[1], base[2]),
        inner(base[2], base[2]),
        last,
    ]
    for k in range(6):
        own_x[k : k + 1, :] = rows[k]
    own_x[6:8, :] = jnp.zeros((2, width), jnp.float32)
    for one in along_x():
        one.start()

    def pass_on():
        own_y[...] = gather(along_x(), own_x, got_x, n_gx)
        for one in along_y():
            one.start()

    base.append(assemble(ITERS, value_part, pass_on))
    sums = gather(along_y(), own_y, got_y, n_gy)
    sums = jnp.sum(sums, axis=1, keepdims=True)
    h = [sums[k : k + 1] for k in range(6)]
    sigma = tikhonov / UNIT
    a0 = h[1] / h[0]
    n1 = h[2] - a0 * h[1]
    a1 = (h[3] - 2.0 * a0 * h[2] + a0 * a0 * h[1]) / n1
    s = a0 + a1
    q = a0 * a1 - n1 / h[0]
    n2 = h[4] - s * h[3] + q * h[2]
    a2 = (h[5] - s * h[4] + q * h[3] - s * n2) / n2
    b2 = n2 / n1
    p2 = -(s + a2)
    p1 = q + a2 * s - b2
    p0 = b2 * a0 - a2 * q
    scale = 1.0 / (sigma * (sigma * (p2 - sigma) - p1) + p0)
    r2, r1, r0 = (p2 * scale, p1 * scale, p0 * scale)
    turn_back = -scale / UNIT
    i1 = (p2 - sigma) * turn_back
    i0 = (p1 - sigma * p2 + sigma * sigma) * turn_back
    for a in range(6):
        inc = turn_back * base[2][a] + i1 * base[1][a] + i0 * base[0][a]
        res = scale * base[3][a] + r2 * base[2][a] + r1 * base[1][a] + r0 * base[0][a]
        out_ref[a] = inc
        out_ref[6 + a] = res
    for phase in range(PHASES):
        sent(copies(phase))
    for one in along_x() + along_y():
        one.wait_send()
    sent(y_copies())
    for k in range(BOUND + 1):
        sent([after_copy(k)] + after_corners(k))
    for k in range(BOUND):
        sent([before_copy(k)] + before_corners(k))


def format_kernel(depth, value_ref, inc_ref, res_ref):
    tile_y = inc_ref.shape[3]
    width = value_ref.shape[2]
    for out, first in ((inc_ref, 0), (res_ref, 6)):
        for c in range(3):
            value = value_ref[first + c]
            for layer in range(depth):
                out[c, layer] = value[:, layer * tile_y : (layer + 1) * tile_y]
            out[c, depth] = value_ref[first + 3 + c][:, width - tile_y :]


def per_device(
    reference_scan, ref_gradient, deformed_scan, interp_weights, sample_mask, block_list, offsets
):
    tile_x, tile_y, column = reference_scan.shape
    depth = column // 512
    width = depth * tile_y
    square_table, shape_table = tables()
    n_gx, n_gy = (lax.axis_size("gx"), lax.axis_size("gy"))
    span_x, span_y = (tile_x + 2 * BOUND + 1, tile_y + 2 * BOUND)
    f32, bf16, vmem, dma = (jnp.float32, jnp.bfloat16, pltpu.VMEM, pltpu.SemaphoreType.DMA)
    part = jax.ShapeDtypeStruct((3, depth + 1, tile_x, tile_y), f32)
    halos = 2 + 3 * (2 * BOUND + 1)
    whole = pl.BlockSpec(memory_space=pltpu.VMEM)
    anywhere = pl.BlockSpec(memory_space=pl.ANY)
    packed = pl.pallas_call(
        functools.partial(step_kernel, (n_gx, n_gy), tile_x, tile_y, depth),
        out_shape=jax.ShapeDtypeStruct((12, tile_x, width), f32),
        in_specs=[whole] * 3 + [anywhere] * 5,
        out_specs=whole,
        scratch_shapes=[
            vmem((3, tile_x, tile_y, column), bf16),
            vmem((tile_x, tile_y, column), jnp.int32),
            vmem((tile_x, tile_y, column), bf16),
            vmem((tile_x, tile_y, column), bf16),
            vmem((tile_x, tile_y, column), bf16),
            vmem((BOUND, tile_y, column), bf16),
            vmem((BOUND + 1, tile_y, column), bf16),
            vmem((span_x, EDGE, column), bf16),
            vmem((span_x, EDGE, column), bf16),
            vmem((span_y * depth * span_x * 4, 128), f32),
            vmem((6 * width, 512), bf16),
            vmem((width * 8, 128), f32),
            vmem((3 * width, 512), bf16),
            vmem((3 * width, 512), bf16),
            vmem((6 * 32 * tile_x, width), f32),
            vmem((3 * 8 * tile_x, width), f32),
            vmem((24, tile_x, width), f32),
            vmem((24, tile_x, width), f32),
        ]
        + [
            vmem((PHASES, rows, width), f32)
            for rows in (16, 16, tile_x + 8, tile_x + 8) * 2 + (8, 8, 8, 8)
        ]
        + [
            vmem((8, width), f32),
            vmem((n_gx - 1, 8, width), f32),
            vmem((8, width), f32),
            vmem((n_gy - 1, 8, width), f32),
            vmem((tile_x, depth, tile_y), jnp.int32),
            pltpu.SMEM((tile_x, depth, tile_y), jnp.int32),
            dma((6, tile_x)),
            dma((halos,)),
            dma((halos,)),
            dma((PHASES, 8)),
            dma((PHASES, 8)),
            dma((n_gx - 1,)),
            dma((n_gx - 1,)),
            dma((n_gy - 1,)),
            dma((n_gy - 1,)),
        ],
        compiler_params=pltpu.CompilerParams(collective_id=0, has_side_effects=True),
        name="step",
    )(
        jnp.transpose(offsets, (0, 1, 3, 2)),
        jnp.asarray(square_table),
        jnp.asarray(shape_table),
        ref_gradient,
        sample_mask,
        deformed_scan,
        reference_scan,
        interp_weights,
    )
    increment, residual = pl.pallas_call(
        functools.partial(format_kernel, depth),
        out_shape=(part, part),
        in_specs=[whole],
        out_specs=(whole, whole),
        name="format",
    )(packed)

    def nodal(value):
        return jnp.transpose(value, (0, 2, 3, 1))

    return (nodal(increment), nodal(residual))


def solution(mesh):
    return jax.shard_map(
        per_device,
        mesh=mesh,
        in_specs=(
            P("gx", "gy", None),
            P(None, "gx", "gy", None),
            P("gx", "gy", None),
            P("gx", "gy", None),
            P("gx", "gy", None),
            P("gx", "gy"),
            P(None, "gx", "gy", None),
        ),
        out_specs=(P(None, "gx", "gy", None), P(None, "gx", "gy", None)),
        check_vma=False,
    )
```

```python
import functools

import jax
import jax.numpy as jnp
import ml_dtypes
import numpy as np
from jax import lax
from jax.experimental import pallas as pl
from jax.experimental.pallas import tpu as pltpu
from jax.sharding import PartitionSpec as P

BOUND = 4
ITERS = 3
PHASES = ITERS + 1
EDGE = 8

tikhonov = 8.0
UNIT = 64.0

NODES = [(n >> 2 & 1, n >> 1 & 1, n & 1) for n in range(8)]
PAIRS = [(c, d) for c in range(3) for d in range(c, 3)]
PAIR_OF = {(c, d): PAIRS.index((min(c, d), max(c, d))) for c in range(3) for d in range(3)}
MESH = pl.DeviceIdType.MESH


def split(table, count):
    parts = []
    for _ in range(count):
        part = table.astype(ml_dtypes.bfloat16)
        parts.append(part)
        table = table - part.astype(np.float32)
    return parts


def tables():
    voxel = np.arange(512)
    coords = [
        ((voxel // 64).astype(np.float32) + np.float32(0.5)) / np.float32(8.0),
        ((voxel // 8 % 8).astype(np.float32) + np.float32(0.5)) / np.float32(8.0),
        ((voxel % 8).astype(np.float32) + np.float32(0.5)) / np.float32(8.0),
    ]
    linear = [[np.float32(1.0) - t, t] for t in coords]
    quad = [[s[0] * s[0], s[0] * s[1], s[1] * s[1]] for s in linear]
    shapes = np.stack([linear[0][i] * linear[1][j] * linear[2][l] for i, j, l in NODES])
    squares = np.stack(
        [quad[0][a] * quad[1][b] * quad[2][c] for a in range(3) for b in range(3) for c in range(3)]
    )
    squares = np.pad(squares, ((0, 5), (0, 0))) / np.float32(UNIT)
    square_table = np.concatenate(split(squares.astype(np.float32), 2), axis=0)
    shape_table = np.concatenate(split(shapes.astype(np.float32), 2), axis=0)
    return (square_table, shape_table)


def spread_stride(rows):
    return rows + 4 if rows % 8 == 0 else rows


def contract(table, part):
    return lax.dot_general(
        table, part, (((1,), (1,)), ((), ())), preferred_element_type=jnp.float32
    )


def row_of(turn, tile_x):
    return jnp.where(turn < tile_x - BOUND, turn + BOUND, tile_x - 1 - turn)


def step_kernel(
    sizes,
    tile_x,
    tile_y,
    depth,
    offset_ref,
    square_ref,
    shape_ref,
    grad_hbm,
    mask_hbm,
    scan_ref,
    image_hbm,
    weight_hbm,
    out_ref,
    grad_ref,
    mask_ref,
    own_ref,
    image_ref,
    weight_ref,
    before_ref,
    after_ref,
    beyond_ref,
    ahead_ref,
    wide_ref,
    part_ref,
    fetched_ref,
    high_ref,
    low_ref,
    hess_ref,
    load_ref,
    field_ref,
    value_ref,
    out_e,
    out_w,
    out_n,
    out_s,
    in_w,
    in_e,
    in_s,
    in_n,
    in_sw,
    in_ne,
    in_nw,
    in_se,
    own_x,
    got_x,
    own_y,
    got_y,
    table_ref,
    source_ref,
    local_sems,
    halo_send,
    halo_recv,
    send_sems,
    recv_sems,
    send_x,
    recv_x,
    send_y,
    recv_y,
):
    n_gx, n_gy = sizes
    gx = lax.axis_index("gx")
    gy = lax.axis_index("gy")
    not_first_x, not_last_x = (gx > 0, gx < n_gx - 1)
    not_first_y, not_last_y = (gy > 0, gy < n_gy - 1)
    both = jnp.logical_and
    wide = depth * tile_y
    span_x = tile_x + 2 * BOUND + 1
    stride_y = spread_stride(depth * span_x * 4)
    stride_x = spread_stride(tile_x)
    stride_f = spread_stride(8 * depth)

    def remote(source, target, sends, receives, device):
        return pltpu.make_async_remote_copy(
            src_ref=source,
            dst_ref=target,
            send_sem=sends,
            recv_sem=receives,
            device_id=device,
            device_id_type=MESH,
        )

    def halo(k, source, target, device):
        return remote(source, target, halo_send.at[k], halo_recv.at[k], device)

    every = slice(None)
    low_y, high_y = (pl.ds(0, EDGE), pl.ds(tile_y - EDGE, EDGE))
    near_y, far_y = ((gx, gy - 1), (gx, gy + 1))
    middle = pl.ds(BOUND, tile_x)

    def y_copies():
        return [
            (halo(0, scan_ref.at[every, low_y], beyond_ref.at[middle], near_y), not_first_y, not_last_y),
            (halo(1, scan_ref.at[every, high_y], ahead_ref.at[middle], far_y), not_last_y, not_first_y),
        ]

    inner_y = pl.ds(EDGE, tile_y - 2 * EDGE)
    bands = 2 * BOUND + 1

    def after_parts(k, parts):
        return [
            (
                halo(2 + 3 * k + p, scan_ref.at[k, cut], after_ref.at[k, cut], (gx - 1, gy)),
                not_first_x,
                not_last_x,
            )
            for p, cut in enumerate((low_y, high_y, inner_y))
            if p in parts
        ]

    def before_parts(k, parts):
        row = tile_x - BOUND + k
        first = 5 + 3 * BOUND + 3 * k
        return [
            (
                halo(first + p, scan_ref.at[row, cut], before_ref.at[k, cut], (gx + 1, gy)),
                not_last_x,
                not_first_x,
            )
            for p, cut in enumerate((low_y, high_y, inner_y))
            if p in parts
        ]

    edges, rest, whole_row = ((0, 1), (2,), (0, 1, 2))

    def corner_copies(first, band, k, row, present):
        return [
            (
                halo(first, band.at[k, low_y], beyond_ref.at[row], near_y),
                both(present, not_first_y),
                both(present, not_last_y),
            ),
            (
                halo(first + 1, band.at[k, high_y], ahead_ref.at[row], far_y),
                both(present, not_last_y),
                both(present, not_first_y),
            ),
        ]

    def after_corners(k):
        first = 2 + 3 * bands + 2 * k
        return corner_copies(first, after_ref, k, BOUND + tile_x + k, not_last_x)

    def before_corners(k):
        first = 4 + 3 * bands + 2 * BOUND + 2 * k
        return corner_copies(first, before_ref, k, k, not_first_x)

    def begin(copies):
        for one, sends, _ in copies:
            pl.when(sends)(one.start)

    def arrive(copies):
        for one, _, receives in copies:
            pl.when(receives)(one.wait_recv)

    def sent(copies):
        for one, sends, _ in copies:
            pl.when(sends)(one.wait_send)

    def put_wide(value, at_x, at_y):
        count = value.shape[0]
        for layer in range(depth):
            for chunk in range(4):
                lanes = slice(layer * 512 + chunk * 128, layer * 512 + chunk * 128 + 128)
                start = at_y * stride_y + (layer * span_x + at_x) * 4 + chunk
                wide_ref[pl.ds(start, count, stride=stride_y), :] = value[:, lanes]

    def put_sides(row, inside):
        value = beyond_ref[row].astype(jnp.float32)[0:BOUND]
        put_wide(jnp.where(both(inside, not_last_y), value, 0.0), row, BOUND + tile_y)
        value = ahead_ref[row].astype(jnp.float32)[EDGE - BOUND :]
        put_wide(jnp.where(both(inside, not_first_y), value, 0.0), row, 0)

    def put_band(band, k, row, inside):
        for first in range(0, tile_y, 16):
            value = band[k, pl.ds(first, 16), :].astype(jnp.float32)
            put_wide(jnp.where(inside, value, 0.0), row, BOUND + first)
        put_sides(row, inside)

    def first_copies(x):
        return [
            pltpu.make_async_copy(grad_hbm.at[:, x], grad_ref.at[:, x], local_sems.at[0, x]),
            pltpu.make_async_copy(mask_hbm.at[x], mask_ref.at[x], local_sems.at[1, x]),
            pltpu.make_async_copy(scan_ref.at[x], own_ref.at[x], local_sems.at[2, x]),
        ]

    def second_copies(x):
        return [
            pltpu.make_async_copy(image_hbm.at[x], image_ref.at[x], local_sems.at[3, x]),
            pltpu.make_async_copy(weight_hbm.at[x], weight_ref.at[x], local_sems.at[4, x]),
        ]

    def start_first(x, carry):
        for one in first_copies(x):
            one.start()
        return carry

    def start_second(turn, carry):
        for one in second_copies(row_of(turn, tile_x)):
            one.start()
        return carry

    for buffer in (in_w, in_e, in_s, in_n, in_sw, in_ne, in_nw, in_se):
        buffer[...] = jnp.zeros_like(buffer)
    for buffer in (out_e, out_w, out_n, out_s):
        buffer[...] = jnp.zeros_like(buffer)
    barrier = pltpu.get_barrier_semaphore()
    for k in range(1, n_gx):
        pl.semaphore_signal(
            barrier, inc=1, device_id=((gx + k) % n_gx, gy), device_id_type=MESH
        )
    for k in range(1, n_gy):
        pl.semaphore_signal(
            barrier, inc=1, device_id=(gx, (gy + k) % n_gy), device_id_type=MESH
        )
    corners = 0
    for dx, there_x in ((-1, not_first_x), (1, not_last_x)):
        for dy, there_y in ((-1, not_first_y), (1, not_last_y)):
            present = both(there_x, there_y)
            corners = corners + jnp.where(present, 1, 0)

            @pl.when(present)
            def _(dx=dx, dy=dy):
                pl.semaphore_signal(
                    barrier, inc=1, device_id=(gx + dx, gy + dy), device_id_type=MESH
                )

    lax.fori_loop(0, 2, start_first, 0)
    extent = (tile_x, depth, tile_y)
    pos_x, layers, pos_y = [lax.broadcasted_iota(jnp.int32, extent, k) for k in range(3)]
    table = (pos_y + offset_ref[1] + BOUND) * stride_y
    table_ref[...] = table + (layers * span_x + pos_x + offset_ref[0] + BOUND) * 4
    table_copy = pltpu.make_async_copy(table_ref, source_ref, local_sems.at[5, 0])
    table_copy.start()
    pl.semaphore_wait(barrier, n_gx - 1 + n_gy - 1 + corners)
    begin(y_copies())
    for parts in (edges, rest):
        for k in range(BOUND + 1):
            begin(after_parts(k, parts))
        for k in range(BOUND):
            begin(before_parts(BOUND - 1 - k, parts))
    lax.fori_loop(2, tile_x, start_first, 0)
    lax.fori_loop(0, tile_x, start_second, 0)

    def hessian_row(x, carry):
        for one in first_copies(x):
            one.wait()
        for first in range(0, tile_y, 16):
            value = own_ref[x, pl.ds(first, 16), :].astype(jnp.float32)
            put_wide(value, BOUND + x, BOUND + first)
        for layer in range(depth):
            lanes = pl.ds(layer * 512, 512)
            mask = mask_ref[x, :, lanes].astype(jnp.float32).astype(jnp.bfloat16)
            grads = [grad_ref[c, x, :, lanes] for c in range(3)]
            masked = [mask * g for g in grads]
            for c in range(3):
                grad_ref[c, x, :, lanes] = masked[c]
            for q, (c, d) in enumerate(PAIRS):
                part_ref[pl.ds(q * wide + layer * tile_y, tile_y), :] = masked[c] * grads[d]
        table = square_ref[...]
        for q in range(6):
            total = contract(table, part_ref[pl.ds(q * wide, wide), :])
            value = total[0:32] + total[32:64]
            for first in range(0, 32, 8):
                rows = pl.ds((q * 32 + first) * stride_x + x, 8, stride=stride_x)
                hess_ref[rows, :] = value[first : first + 8]
        return carry

    lax.fori_loop(0, tile_x, hessian_row, 0)
    table_copy.wait()
    arrive(y_copies())

    def convert(i, carry):
        put_sides(BOUND + i, gx >= 0)
        return carry

    lax.fori_loop(0, tile_x, convert, 0)
    head = tile_x - 2 * BOUND - 1
    turned = tile_x - BOUND

    def load_row(turn, carry):
        @pl.when(both(turn >= head - BOUND - 1, turn < head))
        def _():
            k = turn - (head - BOUND - 1)
            arrive(after_parts(k, edges))
            begin(after_corners(k))

        @pl.when(both(turn >= head - BOUND, turn < head))
        def _():
            k = head - 1 - turn
            arrive(before_parts(k, edges))
            begin(before_corners(k))

        @pl.when(both(turn >= head, turn < turned))
        def _():
            k = turn - head
            arrive(after_parts(k, rest) + after_corners(k))
            put_band(after_ref, k, BOUND + tile_x + k, not_last_x)

        @pl.when(turn >= turned)
        def _():
            k = tile_x - 1 - turn
            arrive(before_parts(k, rest) + before_corners(k))
            put_band(before_ref, k, k, not_first_x)

        x = row_of(turn, tile_x)
        for one in second_copies(x):
            one.wait()

        def fetch(block, inner_carry):
            for inner in range(4):
                y = block * 4 + inner
                for layer in range(depth):
                    row = source_ref[x, layer, y]
                    rows = pl.ds(y * stride_f + layer * 8, 8)
                    fetched_ref[rows, :] = wide_ref[pl.ds(row, 8), :]
            return inner_carry

        lax.fori_loop(0, tile_y // 4, fetch, 0)
        for layer in range(depth):
            for chunk in range(4):
                lanes = pl.ds(layer * 512 + chunk * 128, 128)
                part = pl.ds(chunk * 128, 128)
                near = fetched_ref[pl.ds(layer * 8 + chunk, tile_y, stride=stride_f), :]
                far = fetched_ref[pl.ds(layer * 8 + 4 + chunk, tile_y, stride=stride_f), :]
                weight = weight_ref[x, :, lanes].astype(jnp.float32)
                warped = weight * near + (1.0 - weight) * far
                image = image_ref[x, :, lanes].astype(jnp.float32) - warped
                image = image.astype(jnp.bfloat16).astype(jnp.float32)
                for c in range(3):
                    rows = pl.ds(c * wide + layer * tile_y, tile_y)
                    value = image * grad_ref[c, x, :, lanes].astype(jnp.float32)
                    high = value.astype(jnp.bfloat16)
                    high_ref[rows, part] = high
                    low_ref[rows, part] = (value - high.astype(jnp.float32)).astype(jnp.bfloat16)
        table = shape_ref[...]
        for c in range(3):
            rows = pl.ds(c * wide, wide)
            total = contract(table, high_ref[rows, :]) + contract(table, low_ref[rows, :])
            load_ref[pl.ds(c * 8 * stride_x + x, 8, stride=stride_x), :] = total[0:8] + total[8:16]
        return carry

    lax.fori_loop(0, tile_x, load_row, 0)

    width = wide
    lane = lax.broadcasted_iota(jnp.int32, (tile_x, width), 1)
    row = lax.broadcasted_iota(jnp.int32, (tile_x, width), 0)
    in_tile = lane % tile_y
    first_y = in_tile == 0
    last_y = in_tile == tile_y - 1
    first_x = row == 0
    last_x = row == tile_x - 1
    topmost = lane >= width - tile_y
    above = lane >= tile_y
    first_8, last_8 = (first_y[0:8], last_y[0:8])
    turn_y = tile_y - 1
    body, tail = (pl.ds(0, tile_x), pl.ds(tile_x, 8))
    upper, lower = (pl.ds(0, 8), pl.ds(8, 8))

    def roll(value, shift, axis):
        return pltpu.roll(value, shift % value.shape[axis], axis)

    def shift_x(value):
        return jnp.where(first_x, 0.0, roll(value, 1, 0))

    def copies(phase):
        table = [
            (out_e, None, in_w, 1, 0),
            (out_n, None, in_s, 0, 1),
            (out_e, lower, in_sw, 1, 1),
            (out_w, None, in_e, -1, 0),
            (out_s, None, in_n, 0, -1),
            (out_w, upper, in_ne, -1, -1),
            (out_e, upper, in_nw, 1, -1),
            (out_w, lower, in_se, -1, 1),
        ]
        if phase == PHASES - 1:
            table = table[:3]
        found = []
        for k, (src, rows, dst, dx, dy) in enumerate(table):
            send_ok, recv_ok = (gx >= 0, gx >= 0)
            if dx:
                send_ok = not_last_x if dx > 0 else not_first_x
                recv_ok = not_first_x if dx > 0 else not_last_x
            if dy:
                send_ok = both(send_ok, not_last_y if dy > 0 else not_first_y)
                recv_ok = both(recv_ok, not_first_y if dy > 0 else not_last_y)
            source = src.at[phase] if rows is None else src.at[phase, rows]
            one = remote(
                source,
                dst.at[phase],
                send_sems.at[phase, k],
                recv_sems.at[phase, k],
                (gx + dx, gy + dy),
            )
            found.append((one, send_ok, recv_ok))
        return found

    def assemble(phase, partial, meanwhile):
        folded = {}
        for i in range(2):
            for j in range(2):
                found = []
                for c in range(3):
                    under = partial((4 * i + 2 * j) * 3 + c)
                    over = partial((4 * i + 2 * j + 1) * 3 + c)
                    found.append(under + jnp.where(above, roll(over, tile_y, 1), 0.0))
                    folded[i, j, 3 + c] = jnp.where(topmost, over, 0.0)
                for c in range(3):
                    folded[i, j, c] = found[c]
        total, right = ([], [])
        north = jnp.zeros((tile_x, width), jnp.float32)
        south = jnp.zeros((tile_x, width), jnp.float32)
        for a in range(6):
            kept = [
                folded[i, 0, a] + jnp.where(first_y, 0.0, roll(folded[i, 1, a], 1, 1))
                for i in range(2)
            ]
            mine = kept[0] + shift_x(kept[1])
            side = folded[0, 1, a] + shift_x(folded[1, 1, a])
            edge_x = kept[1][tile_x - 1 :]
            edge_c = folded[1, 1, a][tile_x - 1 :]
            out_e[phase, a : a + 1, :] = edge_x
            out_e[phase, 8 + a : 9 + a, :] = edge_c
            out_w[phase, a : a + 1, :] = mine[0:1]
            out_w[phase, 8 + a : 9 + a, :] = side[0:1]
            out_n[phase, tile_x + a : tile_x + a + 1, :] = edge_c
            out_s[phase, tile_x + a : tile_x + a + 1, :] = edge_x
            north = jnp.where(in_tile == a, roll(side, a + 1, 1), north)
            south = jnp.where(in_tile == a, roll(mine, a, 1), south)
            total.append(mine)
            right.append(side)
        out_n[phase, body, :] = north
        out_s[phase, body, :] = south
        begin(copies(phase))
        meanwhile()
        arrive(copies(phase))
        line = in_w[phase, upper, :] + jnp.where(
            first_8, roll(in_sw[phase], -turn_y, 1), 0.0
        )
        from_s = in_s[phase, body, :]
        whole = [
            total[a]
            + jnp.where(first_x, line[a : a + 1], 0.0)
            + jnp.where(first_y, roll(from_s, -(tile_y + a), 1), 0.0)
            for a in range(6)
        ]
        if phase == PHASES - 1:
            return whole
        side_x = in_s[phase, tail, :] + in_se[phase]
        side_x = jnp.where(first_8, roll(side_x, -turn_y, 1), 0.0)
        side_x = jnp.where(not_last_x, out_e[phase, upper, :] + in_e[phase, upper, :] + side_x, 0.0)
        line = in_w[phase, lower, :] + roll(in_nw[phase], turn_y, 1)
        corner = in_n[phase, tail, :] + in_ne[phase]
        corner = out_e[phase, lower, :] + in_e[phase, lower, :] + roll(corner, turn_y, 1)
        corner = jnp.where(both(not_last_x, not_last_y), corner, 0.0)
        corner = jnp.where(last_8, corner, roll(side_x, -1, 1))
        from_n = in_n[phase, body, :]
        for a in range(6):
            side = right[a] + jnp.where(first_x, line[a : a + 1], 0.0)
            side = side + roll(from_n, turn_y - a, 1)
            side = jnp.where(not_last_y, side, 0.0)
            next_x = jnp.where(last_x, side_x[a : a + 1], roll(whole[a], -1, 0))
            next_y = jnp.where(last_y, side, roll(whole[a], -1, 1))
            next_c = jnp.where(last_x, corner[a : a + 1], roll(next_y, -1, 0))
            for k, value in enumerate((whole[a], next_y, next_x, next_c)):
                if a < 3:
                    field_ref[6 * k + a] = value
                    field_ref[6 * k + 3 + a] = roll(value, -tile_y, 1)
                else:
                    above_it = field_ref[6 * k + a]
                    field_ref[6 * k + a] = jnp.where(topmost, value, above_it)
        return whole

    def apply():
        for half in range(0, tile_x, 8):
            rows = pl.ds(half, 8)
            fields = [field_ref[k, rows, :] for k in range(24)]
            for n, (i, j, l) in enumerate(NODES):
                for c in range(3):
                    total = None
                    for m, (p, q, r) in enumerate(NODES):
                        kind = (i + p) * 9 + (j + q) * 3 + l + r
                        for d in range(3):
                            index = (PAIR_OF[c, d] * 32 + kind) * stride_x + half
                            term = hess_ref[pl.ds(index, 8), :] * fields[3 * m + d]
                            total = term if total is None else total + term
                    value_ref[3 * n + c, rows, :] = total

    def exchange(own, got, sends, receives, index, count, target):
        return [
            remote(
                own,
                got.at[k - 1],
                sends.at[k - 1],
                receives.at[k - 1],
                target((index + k) % count),
            )
            for k in range(1, count)
        ]

    def along_x():
        return exchange(own_x, got_x, send_x, recv_x, gx, n_gx, lambda t: (t, gy))

    def along_y():
        return exchange(own_y, got_y, send_y, recv_y, gy, n_gy, lambda t: (gx, t))

    def gather(found, own, got, count):
        for one in found:
            one.wait_recv()
        total = own[...]
        for k in range(1, count):
            total = total + got[k - 1]
        return total

    def inner(left, right):
        total = left[0] * right[0]
        for one, other in zip(left[1:], right[1:]):
            total = total + one * other
        return jnp.sum(total, axis=0, keepdims=True)

    def nothing():
        return None

    def load_part(k):
        start = ((k % 3) * 8 + k // 3) * stride_x
        return load_ref[pl.ds(start, tile_x), :]

    def value_part(k):
        return value_ref[k]

    base = [assemble(0, load_part, nothing)]
    for phase in range(1, ITERS):
        apply()
        base.append(assemble(phase, value_part, nothing))
    apply()
    last = inner([field_ref[k] for k in range(24)], [value_ref[k] for k in range(24)])
    rows = [
        inner(base[0], base[0]),
        inner(base[0], base[1]),
        inner(base[1], base[1]),
        inner(base[1], base[2]),
        inner(base[2], base[2]),
        last,
    ]
    for k in range(6):
        own_x[k : k + 1, :] = rows[k]
    own_x[6:8, :] = jnp.zeros((2, width), jnp.float32)
    for one in along_x():
        one.start()

    def pass_on():
        own_y[...] = gather(along_x(), own_x, got_x, n_gx)
        for one in along_y():
            one.start()

    base.append(assemble(ITERS, value_part, pass_on))
    sums = gather(along_y(), own_y, got_y, n_gy)
    sums = jnp.sum(sums, axis=1, keepdims=True)
    h = [sums[k : k + 1] for k in range(6)]
    sigma = tikhonov / UNIT
    a0 = h[1] / h[0]
    n1 = h[2] - a0 * h[1]
    a1 = (h[3] - 2.0 * a0 * h[2] + a0 * a0 * h[1]) / n1
    s = a0 + a1
    q = a0 * a1 - n1 / h[0]
    n2 = h[4] - s * h[3] + q * h[2]
    a2 = (h[5] - s * h[4] + q * h[3] - s * n2) / n2
    b2 = n2 / n1
    p2 = -(s + a2)
    p1 = q + a2 * s - b2
    p0 = b2 * a0 - a2 * q
    scale = 1.0 / (sigma * (sigma * (p2 - sigma) - p1) + p0)
    r2, r1, r0 = (p2 * scale, p1 * scale, p0 * scale)
    turn_back = -scale / UNIT
    i1 = (p2 - sigma) * turn_back
    i0 = (p1 - sigma * p2 + sigma * sigma) * turn_back
    for a in range(6):
        inc = turn_back * base[2][a] + i1 * base[1][a] + i0 * base[0][a]
        res = scale * base[3][a] + r2 * base[2][a] + r1 * base[1][a] + r0 * base[0][a]
        out_ref[a] = inc
        out_ref[6 + a] = res
    for phase in range(PHASES):
        sent(copies(phase))
    for one in along_x() + along_y():
        one.wait_send()
    sent(y_copies())
    for k in range(BOUND + 1):
        sent(after_parts(k, whole_row) + after_corners(k))
    for k in range(BOUND):
        sent(before_parts(k, whole_row) + before_corners(k))


def format_kernel(depth, value_ref, inc_ref, res_ref):
    tile_y = inc_ref.shape[3]
    width = value_ref.shape[2]
    for out, first in ((inc_ref, 0), (res_ref, 6)):
        for c in range(3):
            value = value_ref[first + c]
            for layer in range(depth):
                out[c, layer] = value[:, layer * tile_y : (layer + 1) * tile_y]
            out[c, depth] = value_ref[first + 3 + c][:, width - tile_y :]


def per_device(
    reference_scan, ref_gradient, deformed_scan, interp_weights, sample_mask, block_list, offsets
):
    tile_x, tile_y, column = reference_scan.shape
    depth = column // 512
    width = depth * tile_y
    square_table, shape_table = tables()
    n_gx, n_gy = (lax.axis_size("gx"), lax.axis_size("gy"))
    span_x, span_y = (tile_x + 2 * BOUND + 1, tile_y + 2 * BOUND)
    f32, bf16, vmem, dma = (jnp.float32, jnp.bfloat16, pltpu.VMEM, pltpu.SemaphoreType.DMA)
    part = jax.ShapeDtypeStruct((3, depth + 1, tile_x, tile_y), f32)
    halos = 2 + 5 * (2 * BOUND + 1)
    whole = pl.BlockSpec(memory_space=pltpu.VMEM)
    anywhere = pl.BlockSpec(memory_space=pl.ANY)
    packed = pl.pallas_call(
        functools.partial(step_kernel, (n_gx, n_gy), tile_x, tile_y, depth),
        out_shape=jax.ShapeDtypeStruct((12, tile_x, width), f32),
        in_specs=[whole] * 3 + [anywhere] * 5,
        out_specs=whole,
        scratch_shapes=[
            vmem((3, tile_x, tile_y, column), bf16),
            vmem((tile_x, tile_y, column), jnp.int32),
            vmem((tile_x, tile_y, column), bf16),
            vmem((tile_x, tile_y, column), bf16),
            vmem((tile_x, tile_y, column), bf16),
            vmem((BOUND, tile_y, column), bf16),
            vmem((BOUND + 1, tile_y, column), bf16),
            vmem((span_x, EDGE, column), bf16),
            vmem((span_x, EDGE, column), bf16),
            vmem((span_y * spread_stride(depth * span_x * 4), 128), f32),
            vmem((6 * width, 512), bf16),
            vmem((tile_y * spread_stride(8 * depth), 128), f32),
            vmem((3 * width, 512), bf16),
            vmem((3 * width, 512), bf16),
            vmem((6 * 32 * spread_stride(tile_x), width), f32),
            vmem((3 * 8 * spread_stride(tile_x), width), f32),
            vmem((24, tile_x, width), f32),
            vmem((24, tile_x, width), f32),
        ]
        + [
            vmem((PHASES, rows, width), f32)
            for rows in (16, 16, tile_x + 8, tile_x + 8) * 2 + (8, 8, 8, 8)
        ]
        + [
            vmem((8, width), f32),
            vmem((n_gx - 1, 8, width), f32),
            vmem((8, width), f32),
            vmem((n_gy - 1, 8, width), f32),
            vmem((tile_x, depth, tile_y), jnp.int32),
            pltpu.SMEM((tile_x, depth, tile_y), jnp.int32),
            dma((6, tile_x)),
            dma((halos,)),
            dma((halos,)),
            dma((PHASES, 8)),
            dma((PHASES, 8)),
            dma((n_gx - 1,)),
            dma((n_gx - 1,)),
            dma((n_gy - 1,)),
            dma((n_gy - 1,)),
        ],
        compiler_params=pltpu.CompilerParams(collective_id=0, has_side_effects=True),
        name="step",
    )(
        jnp.transpose(offsets, (0, 1, 3, 2)),
        jnp.asarray(square_table),
        jnp.asarray(shape_table),
        ref_gradient,
        sample_mask,
        deformed_scan,
        reference_scan,
        interp_weights,
    )
    increment, residual = pl.pallas_call(
        functools.partial(format_kernel, depth),
        out_shape=(part, part),
        in_specs=[whole],
        out_specs=(whole, whole),
        name="format",
    )(packed)

    def nodal(value):
        return jnp.transpose(value, (0, 2, 3, 1))

    return (nodal(increment), nodal(residual))


def solution(mesh):
    return jax.shard_map(
        per_device,
        mesh=mesh,
        in_specs=(
            P("gx", "gy", None),
            P(None, "gx", "gy", None),
            P("gx", "gy", None),
            P("gx", "gy", None),
            P("gx", "gy", None),
            P("gx", "gy"),
            P(None, "gx", "gy", None),
        ),
        out_specs=(P(None, "gx", "gy", None), P(None, "gx", "gy", None)),
        check_vma=False,
    )
```

```python
import functools

import jax
import jax.numpy as jnp
import ml_dtypes
import numpy as np
from jax import lax
from jax.experimental import pallas as pl
from jax.experimental.pallas import tpu as pltpu
from jax.sharding import PartitionSpec as P

BOUND = 4
ITERS = 3
PHASES = ITERS + 1
EDGE = 8

tikhonov = 8.0
UNIT = 64.0

NODES = [(n >> 2 & 1, n >> 1 & 1, n & 1) for n in range(8)]
PAIRS = [(c, d) for c in range(3) for d in range(c, 3)]
PAIR_OF = {(c, d): PAIRS.index((min(c, d), max(c, d))) for c in range(3) for d in range(3)}
MESH = pl.DeviceIdType.MESH


def split(table, count):
    parts = []
    for _ in range(count):
        part = table.astype(ml_dtypes.bfloat16)
        parts.append(part)
        table = table - part.astype(np.float32)
    return parts


def tables():
    voxel = np.arange(512)
    coords = [
        ((voxel // 64).astype(np.float32) + np.float32(0.5)) / np.float32(8.0),
        ((voxel // 8 % 8).astype(np.float32) + np.float32(0.5)) / np.float32(8.0),
        ((voxel % 8).astype(np.float32) + np.float32(0.5)) / np.float32(8.0),
    ]
    linear = [[np.float32(1.0) - t, t] for t in coords]
    quad = [[s[0] * s[0], s[0] * s[1], s[1] * s[1]] for s in linear]
    shapes = np.stack([linear[0][i] * linear[1][j] * linear[2][l] for i, j, l in NODES])
    squares = np.stack(
        [quad[0][a] * quad[1][b] * quad[2][c] for a in range(3) for b in range(3) for c in range(3)]
    )
    squares = np.pad(squares, ((0, 5), (0, 0))) / np.float32(UNIT)
    square_table = np.concatenate(split(squares.astype(np.float32), 2), axis=0)
    shape_table = np.concatenate(split(shapes.astype(np.float32), 2), axis=0)
    return (square_table, shape_table)


def spread_stride(rows):
    return rows + 4 if rows % 8 == 0 else rows


def contract(table, part):
    return lax.dot_general(
        table, part, (((1,), (1,)), ((), ())), preferred_element_type=jnp.float32
    )


def row_of(turn, tile_x):
    return jnp.where(turn < tile_x - BOUND, turn + BOUND, tile_x - 1 - turn)


def step_kernel(
    sizes,
    tile_x,
    tile_y,
    depth,
    offset_hbm,
    square_hbm,
    shape_hbm,
    grad_hbm,
    mask_hbm,
    scan_ref,
    image_hbm,
    weight_hbm,
    out_ref,
    grad_ref,
    mask_ref,
    own_ref,
    image_ref,
    weight_ref,
    before_ref,
    after_ref,
    beyond_ref,
    ahead_ref,
    wide_ref,
    part_ref,
    fetched_ref,
    high_ref,
    low_ref,
    hess_ref,
    load_ref,
    field_ref,
    value_ref,
    out_e,
    out_w,
    out_n,
    out_s,
    in_w,
    in_e,
    in_s,
    in_n,
    in_sw,
    in_ne,
    in_nw,
    in_se,
    own_x,
    got_x,
    own_y,
    got_y,
    offset_ref,
    square_ref,
    shape_ref,
    table_ref,
    source_ref,
    local_sems,
    halo_send,
    halo_recv,
    send_sems,
    recv_sems,
    send_x,
    recv_x,
    send_y,
    recv_y,
):
    n_gx, n_gy = sizes
    gx = lax.axis_index("gx")
    gy = lax.axis_index("gy")
    not_first_x, not_last_x = (gx > 0, gx < n_gx - 1)
    not_first_y, not_last_y = (gy > 0, gy < n_gy - 1)
    both = jnp.logical_and
    wide = depth * tile_y
    span_x = tile_x + 2 * BOUND + 1
    stride_y = spread_stride(depth * span_x * 4)
    stride_x = spread_stride(tile_x)
    stride_f = spread_stride(8 * depth)

    def remote(source, target, sends, receives, device):
        return pltpu.make_async_remote_copy(
            src_ref=source,
            dst_ref=target,
            send_sem=sends,
            recv_sem=receives,
            device_id=device,
            device_id_type=MESH,
        )

    def halo(k, source, target, device):
        return remote(source, target, halo_send.at[k], halo_recv.at[k], device)

    every = slice(None)
    low_y, high_y = (pl.ds(0, EDGE), pl.ds(tile_y - EDGE, EDGE))
    near_y, far_y = ((gx, gy - 1), (gx, gy + 1))
    middle = pl.ds(BOUND, tile_x)

    def y_copies():
        return [
            (halo(0, scan_ref.at[every, low_y], beyond_ref.at[middle], near_y), not_first_y, not_last_y),
            (halo(1, scan_ref.at[every, high_y], ahead_ref.at[middle], far_y), not_last_y, not_first_y),
        ]

    inner_y = pl.ds(EDGE, tile_y - 2 * EDGE)
    bands = 2 * BOUND + 1

    def after_parts(k, parts):
        return [
            (
                halo(2 + 3 * k + p, scan_ref.at[k, cut], after_ref.at[k, cut], (gx - 1, gy)),
                not_first_x,
                not_last_x,
            )
            for p, cut in enumerate((low_y, high_y, inner_y))
            if p in parts
        ]

    def before_parts(k, parts):
        row = tile_x - BOUND + k
        first = 5 + 3 * BOUND + 3 * k
        return [
            (
                halo(first + p, scan_ref.at[row, cut], before_ref.at[k, cut], (gx + 1, gy)),
                not_last_x,
                not_first_x,
            )
            for p, cut in enumerate((low_y, high_y, inner_y))
            if p in parts
        ]

    edges, rest, whole_row = ((0, 1), (2,), (0, 1, 2))

    def corner_copies(first, band, k, row, present):
        return [
            (
                halo(first, band.at[k, low_y], beyond_ref.at[row], near_y),
                both(present, not_first_y),
                both(present, not_last_y),
            ),
            (
                halo(first + 1, band.at[k, high_y], ahead_ref.at[row], far_y),
                both(present, not_last_y),
                both(present, not_first_y),
            ),
        ]

    def after_corners(k):
        first = 2 + 3 * bands + 2 * k
        return corner_copies(first, after_ref, k, BOUND + tile_x + k, not_last_x)

    def before_corners(k):
        first = 4 + 3 * bands + 2 * BOUND + 2 * k
        return corner_copies(first, before_ref, k, k, not_first_x)

    def begin(copies):
        for one, sends, _ in copies:
            pl.when(sends)(one.start)

    def arrive(copies):
        for one, _, receives in copies:
            pl.when(receives)(one.wait_recv)

    def sent(copies):
        for one, sends, _ in copies:
            pl.when(sends)(one.wait_send)

    def put_wide(value, at_x, at_y):
        count = value.shape[0]
        for layer in range(depth):
            for chunk in range(4):
                lanes = slice(layer * 512 + chunk * 128, layer * 512 + chunk * 128 + 128)
                start = at_y * stride_y + (layer * span_x + at_x) * 4 + chunk
                wide_ref[pl.ds(start, count, stride=stride_y), :] = value[:, lanes]

    def put_sides(row, inside):
        value = beyond_ref[row].astype(jnp.float32)[0:BOUND]
        put_wide(jnp.where(both(inside, not_last_y), value, 0.0), row, BOUND + tile_y)
        value = ahead_ref[row].astype(jnp.float32)[EDGE - BOUND :]
        put_wide(jnp.where(both(inside, not_first_y), value, 0.0), row, 0)

    def put_band(band, k, row, inside):
        for first in range(0, tile_y, 16):
            value = band[k, pl.ds(first, 16), :].astype(jnp.float32)
            put_wide(jnp.where(inside, value, 0.0), row, BOUND + first)
        put_sides(row, inside)

    def first_copies(x):
        return [
            pltpu.make_async_copy(grad_hbm.at[:, x], grad_ref.at[:, x], local_sems.at[0, x]),
            pltpu.make_async_copy(mask_hbm.at[x], mask_ref.at[x], local_sems.at[1, x]),
            pltpu.make_async_copy(scan_ref.at[x], own_ref.at[x], local_sems.at[2, x]),
        ]

    def second_copies(x):
        return [
            pltpu.make_async_copy(image_hbm.at[x], image_ref.at[x], local_sems.at[3, x]),
            pltpu.make_async_copy(weight_hbm.at[x], weight_ref.at[x], local_sems.at[4, x]),
        ]

    def start_first(x, carry):
        for one in first_copies(x):
            one.start()
        return carry

    def start_second(turn, carry):
        for one in second_copies(row_of(turn, tile_x)):
            one.start()
        return carry

    for buffer in (in_w, in_e, in_s, in_n, in_sw, in_ne, in_nw, in_se):
        buffer[...] = jnp.zeros_like(buffer)
    for buffer in (out_e, out_w, out_n, out_s):
        buffer[...] = jnp.zeros_like(buffer)
    barrier = pltpu.get_barrier_semaphore()
    for k in range(1, n_gx):
        pl.semaphore_signal(
            barrier, inc=1, device_id=((gx + k) % n_gx, gy), device_id_type=MESH
        )
    for k in range(1, n_gy):
        pl.semaphore_signal(
            barrier, inc=1, device_id=(gx, (gy + k) % n_gy), device_id_type=MESH
        )
    corners = 0
    for dx, there_x in ((-1, not_first_x), (1, not_last_x)):
        for dy, there_y in ((-1, not_first_y), (1, not_last_y)):
            present = both(there_x, there_y)
            corners = corners + jnp.where(present, 1, 0)

            @pl.when(present)
            def _(dx=dx, dy=dy):
                pl.semaphore_signal(
                    barrier, inc=1, device_id=(gx + dx, gy + dy), device_id_type=MESH
                )

    lax.fori_loop(0, 2, start_first, 0)
    small_copies = [
        pltpu.make_async_copy(one, other, local_sems.at[5, k])
        for k, (one, other) in enumerate(
            ((square_hbm, square_ref), (offset_hbm, offset_ref), (shape_hbm, shape_ref))
        )
    ]
    for one in small_copies:
        one.start()
    pl.semaphore_wait(barrier, n_gx - 1 + n_gy - 1 + corners)
    begin(y_copies())
    for parts in (edges, rest):
        for k in range(BOUND + 1):
            begin(after_parts(k, parts))
        for k in range(BOUND):
            begin(before_parts(BOUND - 1 - k, parts))
    lax.fori_loop(2, tile_x, start_first, 0)
    lax.fori_loop(0, tile_x, start_second, 0)

    def hessian_row(x, carry):
        for one in first_copies(x):
            one.wait()
        for first in range(0, tile_y, 16):
            value = own_ref[x, pl.ds(first, 16), :].astype(jnp.float32)
            put_wide(value, BOUND + x, BOUND + first)
        for layer in range(depth):
            lanes = pl.ds(layer * 512, 512)
            mask = mask_ref[x, :, lanes].astype(jnp.float32).astype(jnp.bfloat16)
            grads = [grad_ref[c, x, :, lanes] for c in range(3)]
            masked = [mask * g for g in grads]
            for c in range(3):
                grad_ref[c, x, :, lanes] = masked[c]
            for q, (c, d) in enumerate(PAIRS):
                part_ref[pl.ds(q * wide + layer * tile_y, tile_y), :] = masked[c] * grads[d]
        table = square_ref[...]
        for q in range(6):
            total = contract(table, part_ref[pl.ds(q * wide, wide), :])
            value = total[0:32] + total[32:64]
            for first in range(0, 32, 8):
                rows = pl.ds((q * 32 + first) * stride_x + x, 8, stride=stride_x)
                hess_ref[rows, :] = value[first : first + 8]
        return carry

    for one in small_copies:
        one.wait()
    extent = (tile_x, depth, tile_y)
    pos_x, layers, pos_y = [lax.broadcasted_iota(jnp.int32, extent, k) for k in range(3)]
    table = (pos_y + offset_ref[1] + BOUND) * stride_y
    table_ref[...] = table + (layers * span_x + pos_x + offset_ref[0] + BOUND) * 4
    table_copy = pltpu.make_async_copy(table_ref, source_ref, local_sems.at[5, 3])
    table_copy.start()
    lax.fori_loop(0, tile_x, hessian_row, 0)
    table_copy.wait()
    arrive(y_copies())

    def convert(i, carry):
        put_sides(BOUND + i, gx >= 0)
        return carry

    lax.fori_loop(0, tile_x, convert, 0)
    head = tile_x - 2 * BOUND - 1
    turned = tile_x - BOUND

    def load_row(turn, carry):
        @pl.when(both(turn >= head - BOUND - 1, turn < head))
        def _():
            k = turn - (head - BOUND - 1)
            arrive(after_parts(k, edges))
            begin(after_corners(k))

        @pl.when(both(turn >= head - BOUND, turn < head))
        def _():
            k = head - 1 - turn
            arrive(before_parts(k, edges))
            begin(before_corners(k))

        @pl.when(both(turn >= head, turn < turned))
        def _():
            k = turn - head
            arrive(after_parts(k, rest) + after_corners(k))
            put_band(after_ref, k, BOUND + tile_x + k, not_last_x)

        @pl.when(turn >= turned)
        def _():
            k = tile_x - 1 - turn
            arrive(before_parts(k, rest) + before_corners(k))
            put_band(before_ref, k, k, not_first_x)

        x = row_of(turn, tile_x)
        for one in second_copies(x):
            one.wait()

        for y in range(tile_y):
            for layer in range(depth):
                row = source_ref[x, layer, y]
                fetched_ref[pl.ds(y * stride_f + layer * 8, 8), :] = wide_ref[pl.ds(row, 8), :]
        for layer in range(depth):
            for chunk in range(4):
                lanes = pl.ds(layer * 512 + chunk * 128, 128)
                part = pl.ds(chunk * 128, 128)
                near = fetched_ref[pl.ds(layer * 8 + chunk, tile_y, stride=stride_f), :]
                far = fetched_ref[pl.ds(layer * 8 + 4 + chunk, tile_y, stride=stride_f), :]
                weight = weight_ref[x, :, lanes].astype(jnp.float32)
                warped = weight * near + (1.0 - weight) * far
                image = image_ref[x, :, lanes].astype(jnp.float32) - warped
                image = image.astype(jnp.bfloat16).astype(jnp.float32)
                for c in range(3):
                    rows = pl.ds(c * wide + layer * tile_y, tile_y)
                    value = image * grad_ref[c, x, :, lanes].astype(jnp.float32)
                    high = value.astype(jnp.bfloat16)
                    high_ref[rows, part] = high
                    low_ref[rows, part] = (value - high.astype(jnp.float32)).astype(jnp.bfloat16)
        table = shape_ref[...]
        for c in range(3):
            rows = pl.ds(c * wide, wide)
            total = contract(table, high_ref[rows, :]) + contract(table, low_ref[rows, :])
            load_ref[pl.ds(c * 8 * stride_x + x, 8, stride=stride_x), :] = total[0:8] + total[8:16]
        return carry

    lax.fori_loop(0, tile_x, load_row, 0)

    width = wide
    lane = lax.broadcasted_iota(jnp.int32, (tile_x, width), 1)
    row = lax.broadcasted_iota(jnp.int32, (tile_x, width), 0)
    in_tile = lane % tile_y
    first_y = in_tile == 0
    last_y = in_tile == tile_y - 1
    first_x = row == 0
    last_x = row == tile_x - 1
    topmost = lane >= width - tile_y
    above = lane >= tile_y
    first_8, last_8 = (first_y[0:8], last_y[0:8])
    turn_y = tile_y - 1
    body, tail = (pl.ds(0, tile_x), pl.ds(tile_x, 8))
    upper, lower = (pl.ds(0, 8), pl.ds(8, 8))

    def roll(value, shift, axis):
        return pltpu.roll(value, shift % value.shape[axis], axis)

    def shift_x(value):
        return jnp.where(first_x, 0.0, roll(value, 1, 0))

    def copies(phase):
        table = [
            (out_e, None, in_w, 1, 0),
            (out_n, None, in_s, 0, 1),
            (out_e, lower, in_sw, 1, 1),
            (out_w, None, in_e, -1, 0),
            (out_s, None, in_n, 0, -1),
            (out_w, upper, in_ne, -1, -1),
            (out_e, upper, in_nw, 1, -1),
            (out_w, lower, in_se, -1, 1),
        ]
        if phase == PHASES - 1:
            table = table[:3]
        found = []
        for k, (src, rows, dst, dx, dy) in enumerate(table):
            send_ok, recv_ok = (gx >= 0, gx >= 0)
            if dx:
                send_ok = not_last_x if dx > 0 else not_first_x
                recv_ok = not_first_x if dx > 0 else not_last_x
            if dy:
                send_ok = both(send_ok, not_last_y if dy > 0 else not_first_y)
                recv_ok = both(recv_ok, not_first_y if dy > 0 else not_last_y)
            source = src.at[phase] if rows is None else src.at[phase, rows]
            one = remote(
                source,
                dst.at[phase],
                send_sems.at[phase, k],
                recv_sems.at[phase, k],
                (gx + dx, gy + dy),
            )
            found.append((one, send_ok, recv_ok))
        return found

    def assemble(phase, partial, meanwhile):
        folded = {}
        for i in range(2):
            for j in range(2):
                found = []
                for c in range(3):
                    under = partial((4 * i + 2 * j) * 3 + c)
                    over = partial((4 * i + 2 * j + 1) * 3 + c)
                    found.append(under + jnp.where(above, roll(over, tile_y, 1), 0.0))
                    folded[i, j, 3 + c] = jnp.where(topmost, over, 0.0)
                for c in range(3):
                    folded[i, j, c] = found[c]
        total, right = ([], [])
        north = jnp.zeros((tile_x, width), jnp.float32)
        south = jnp.zeros((tile_x, width), jnp.float32)
        for a in range(6):
            kept = [
                folded[i, 0, a] + jnp.where(first_y, 0.0, roll(folded[i, 1, a], 1, 1))
                for i in range(2)
            ]
            mine = kept[0] + shift_x(kept[1])
            side = folded[0, 1, a] + shift_x(folded[1, 1, a])
            edge_x = kept[1][tile_x - 1 :]
            edge_c = folded[1, 1, a][tile_x - 1 :]
            out_e[phase, a : a + 1, :] = edge_x
            out_e[phase, 8 + a : 9 + a, :] = edge_c
            out_w[phase, a : a + 1, :] = mine[0:1]
            out_w[phase, 8 + a : 9 + a, :] = side[0:1]
            out_n[phase, tile_x + a : tile_x + a + 1, :] = edge_c
            out_s[phase, tile_x + a : tile_x + a + 1, :] = edge_x
            north = jnp.where(in_tile == a, roll(side, a + 1, 1), north)
            south = jnp.where(in_tile == a, roll(mine, a, 1), south)
            total.append(mine)
            right.append(side)
        out_n[phase, body, :] = north
        out_s[phase, body, :] = south
        begin(copies(phase))
        meanwhile()
        arrive(copies(phase))
        line = in_w[phase, upper, :] + jnp.where(
            first_8, roll(in_sw[phase], -turn_y, 1), 0.0
        )
        from_s = in_s[phase, body, :]
        whole = [
            total[a]
            + jnp.where(first_x, line[a : a + 1], 0.0)
            + jnp.where(first_y, roll(from_s, -(tile_y + a), 1), 0.0)
            for a in range(6)
        ]
        if phase == PHASES - 1:
            return whole
        side_x = in_s[phase, tail, :] + in_se[phase]
        side_x = jnp.where(first_8, roll(side_x, -turn_y, 1), 0.0)
        side_x = jnp.where(not_last_x, out_e[phase, upper, :] + in_e[phase, upper, :] + side_x, 0.0)
        line = in_w[phase, lower, :] + roll(in_nw[phase], turn_y, 1)
        corner = in_n[phase, tail, :] + in_ne[phase]
        corner = out_e[phase, lower, :] + in_e[phase, lower, :] + roll(corner, turn_y, 1)
        corner = jnp.where(both(not_last_x, not_last_y), corner, 0.0)
        corner = jnp.where(last_8, corner, roll(side_x, -1, 1))
        from_n = in_n[phase, body, :]
        for a in range(6):
            side = right[a] + jnp.where(first_x, line[a : a + 1], 0.0)
            side = side + roll(from_n, turn_y - a, 1)
            side = jnp.where(not_last_y, side, 0.0)
            next_x = jnp.where(last_x, side_x[a : a + 1], roll(whole[a], -1, 0))
            next_y = jnp.where(last_y, side, roll(whole[a], -1, 1))
            next_c = jnp.where(last_x, corner[a : a + 1], roll(next_y, -1, 0))
            for k, value in enumerate((whole[a], next_y, next_x, next_c)):
                if a < 3:
                    field_ref[6 * k + a] = value
                    field_ref[6 * k + 3 + a] = roll(value, -tile_y, 1)
                else:
                    above_it = field_ref[6 * k + a]
                    field_ref[6 * k + a] = jnp.where(topmost, value, above_it)
        return whole

    def apply():
        for half in range(0, tile_x, 8):
            rows = pl.ds(half, 8)
            fields = [field_ref[k, rows, :] for k in range(24)]
            for n, (i, j, l) in enumerate(NODES):
                for c in range(3):
                    total = None
                    for m, (p, q, r) in enumerate(NODES):
                        kind = (i + p) * 9 + (j + q) * 3 + l + r
                        for d in range(3):
                            index = (PAIR_OF[c, d] * 32 + kind) * stride_x + half
                            term = hess_ref[pl.ds(index, 8), :] * fields[3 * m + d]
                            total = term if total is None else total + term
                    value_ref[3 * n + c, rows, :] = total

    def exchange(own, got, sends, receives, index, count, target):
        return [
            remote(
                own,
                got.at[k - 1],
                sends.at[k - 1],
                receives.at[k - 1],
                target((index + k) % count),
            )
            for k in range(1, count)
        ]

    def along_x():
        return exchange(own_x, got_x, send_x, recv_x, gx, n_gx, lambda t: (t, gy))

    def along_y():
        return exchange(own_y, got_y, send_y, recv_y, gy, n_gy, lambda t: (gx, t))

    def gather(found, own, got, count):
        for one in found:
            one.wait_recv()
        total = own[...]
        for k in range(1, count):
            total = total + got[k - 1]
        return total

    def inner(left, right):
        total = left[0] * right[0]
        for one, other in zip(left[1:], right[1:]):
            total = total + one * other
        return jnp.sum(total, axis=0, keepdims=True)

    def nothing():
        return None

    def load_part(k):
        start = ((k % 3) * 8 + k // 3) * stride_x
        return load_ref[pl.ds(start, tile_x), :]

    def value_part(k):
        return value_ref[k]

    base = [assemble(0, load_part, nothing)]
    for phase in range(1, ITERS):
        apply()
        base.append(assemble(phase, value_part, nothing))
    apply()
    last = inner([field_ref[k] for k in range(24)], [value_ref[k] for k in range(24)])
    rows = [
        inner(base[0], base[0]),
        inner(base[0], base[1]),
        inner(base[1], base[1]),
        inner(base[1], base[2]),
        inner(base[2], base[2]),
        last,
    ]
    for k in range(6):
        own_x[k : k + 1, :] = rows[k]
    own_x[6:8, :] = jnp.zeros((2, width), jnp.float32)
    for one in along_x():
        one.start()

    def pass_on():
        own_y[...] = gather(along_x(), own_x, got_x, n_gx)
        for one in along_y():
            one.start()

    base.append(assemble(ITERS, value_part, pass_on))
    sums = gather(along_y(), own_y, got_y, n_gy)
    sums = jnp.sum(sums, axis=1, keepdims=True)
    h = [sums[k : k + 1] for k in range(6)]
    sigma = tikhonov / UNIT
    a0 = h[1] / h[0]
    n1 = h[2] - a0 * h[1]
    a1 = (h[3] - 2.0 * a0 * h[2] + a0 * a0 * h[1]) / n1
    s = a0 + a1
    q = a0 * a1 - n1 / h[0]
    n2 = h[4] - s * h[3] + q * h[2]
    a2 = (h[5] - s * h[4] + q * h[3] - s * n2) / n2
    b2 = n2 / n1
    p2 = -(s + a2)
    p1 = q + a2 * s - b2
    p0 = b2 * a0 - a2 * q
    scale = 1.0 / (sigma * (sigma * (p2 - sigma) - p1) + p0)
    r2, r1, r0 = (p2 * scale, p1 * scale, p0 * scale)
    turn_back = -scale / UNIT
    i1 = (p2 - sigma) * turn_back
    i0 = (p1 - sigma * p2 + sigma * sigma) * turn_back
    for a in range(6):
        inc = turn_back * base[2][a] + i1 * base[1][a] + i0 * base[0][a]
        res = scale * base[3][a] + r2 * base[2][a] + r1 * base[1][a] + r0 * base[0][a]
        out_ref[a] = inc
        out_ref[6 + a] = res
    for phase in range(PHASES):
        sent(copies(phase))
    for one in along_x() + along_y():
        one.wait_send()
    sent(y_copies())
    for k in range(BOUND + 1):
        sent(after_parts(k, whole_row) + after_corners(k))
    for k in range(BOUND):
        sent(before_parts(k, whole_row) + before_corners(k))


def format_kernel(depth, value_ref, inc_ref, res_ref):
    tile_y = inc_ref.shape[3]
    width = value_ref.shape[2]
    for out, first in ((inc_ref, 0), (res_ref, 6)):
        for c in range(3):
            value = value_ref[first + c]
            for layer in range(depth):
                out[c, layer] = value[:, layer * tile_y : (layer + 1) * tile_y]
            out[c, depth] = value_ref[first + 3 + c][:, width - tile_y :]


def per_device(
    reference_scan, ref_gradient, deformed_scan, interp_weights, sample_mask, block_list, offsets
):
    tile_x, tile_y, column = reference_scan.shape
    depth = column // 512
    width = depth * tile_y
    square_table, shape_table = tables()
    n_gx, n_gy = (lax.axis_size("gx"), lax.axis_size("gy"))
    span_x, span_y = (tile_x + 2 * BOUND + 1, tile_y + 2 * BOUND)
    f32, bf16, vmem, dma = (jnp.float32, jnp.bfloat16, pltpu.VMEM, pltpu.SemaphoreType.DMA)
    part = jax.ShapeDtypeStruct((3, depth + 1, tile_x, tile_y), f32)
    halos = 2 + 5 * (2 * BOUND + 1)
    whole = pl.BlockSpec(memory_space=pltpu.VMEM)
    anywhere = pl.BlockSpec(memory_space=pl.ANY)
    packed = pl.pallas_call(
        functools.partial(step_kernel, (n_gx, n_gy), tile_x, tile_y, depth),
        out_shape=vmem((12, tile_x, width), f32),
        in_specs=[anywhere] * 8,
        out_specs=whole,
        scratch_shapes=[
            vmem((3, tile_x, tile_y, column), bf16),
            vmem((tile_x, tile_y, column), jnp.int32),
            vmem((tile_x, tile_y, column), bf16),
            vmem((tile_x, tile_y, column), bf16),
            vmem((tile_x, tile_y, column), bf16),
            vmem((BOUND, tile_y, column), bf16),
            vmem((BOUND + 1, tile_y, column), bf16),
            vmem((span_x, EDGE, column), bf16),
            vmem((span_x, EDGE, column), bf16),
            vmem((span_y * spread_stride(depth * span_x * 4), 128), f32),
            vmem((6 * width, 512), bf16),
            vmem((tile_y * spread_stride(8 * depth), 128), f32),
            vmem((3 * width, 512), bf16),
            vmem((3 * width, 512), bf16),
            vmem((6 * 32 * spread_stride(tile_x), width), f32),
            vmem((3 * 8 * spread_stride(tile_x), width), f32),
            vmem((24, tile_x, width), f32),
            vmem((24, tile_x, width), f32),
        ]
        + [
            vmem((PHASES, rows, width), f32)
            for rows in (16, 16, tile_x + 8, tile_x + 8) * 2 + (8, 8, 8, 8)
        ]
        + [
            vmem((8, width), f32),
            vmem((n_gx - 1, 8, width), f32),
            vmem((8, width), f32),
            vmem((n_gy - 1, 8, width), f32),
            vmem((2, tile_x, depth, tile_y), jnp.int32),
            vmem(square_table.shape, bf16),
            vmem(shape_table.shape, bf16),
            vmem((tile_x, depth, tile_y), jnp.int32),
            pltpu.SMEM((tile_x, depth, tile_y), jnp.int32),
            dma((6, tile_x)),
            dma((halos,)),
            dma((halos,)),
            dma((PHASES, 8)),
            dma((PHASES, 8)),
            dma((n_gx - 1,)),
            dma((n_gx - 1,)),
            dma((n_gy - 1,)),
            dma((n_gy - 1,)),
        ],
        compiler_params=pltpu.CompilerParams(collective_id=0, has_side_effects=True),
        name="step",
    )(
        jnp.transpose(offsets, (0, 1, 3, 2)),
        jnp.asarray(square_table),
        jnp.asarray(shape_table),
        ref_gradient,
        sample_mask,
        deformed_scan,
        reference_scan,
        interp_weights,
    )
    increment, residual = pl.pallas_call(
        functools.partial(format_kernel, depth),
        out_shape=(part, part),
        in_specs=[whole],
        out_specs=(whole, whole),
        compiler_params=pltpu.CompilerParams(vmem_limit_bytes=2**21),
        name="format",
    )(packed)

    def nodal(value):
        return jnp.transpose(value, (0, 2, 3, 1))

    return (nodal(increment), nodal(residual))


def solution(mesh):
    return jax.shard_map(
        per_device,
        mesh=mesh,
        in_specs=(
            P("gx", "gy", None),
            P(None, "gx", "gy", None),
            P("gx", "gy", None),
            P("gx", "gy", None),
            P("gx", "gy", None),
            P("gx", "gy"),
            P(None, "gx", "gy", None),
        ),
        out_specs=(P(None, "gx", "gy", None), P(None, "gx", "gy", None)),
        check_vma=False,
    )
```

```python
import functools

import jax
import jax.numpy as jnp
import ml_dtypes
import numpy as np
from jax import lax
from jax.experimental import pallas as pl
from jax.experimental.pallas import tpu as pltpu
from jax.sharding import PartitionSpec as P

BOUND = 4
ITERS = 3
PHASES = ITERS + 1
EDGE = 8

tikhonov = 8.0
UNIT = 64.0

NODES = [(n >> 2 & 1, n >> 1 & 1, n & 1) for n in range(8)]
PAIRS = [(c, d) for c in range(3) for d in range(c, 3)]
PAIR_OF = {(c, d): PAIRS.index((min(c, d), max(c, d))) for c in range(3) for d in range(3)}
MESH = pl.DeviceIdType.MESH


def split(table, count):
    parts = []
    for _ in range(count):
        part = table.astype(ml_dtypes.bfloat16)
        parts.append(part)
        table = table - part.astype(np.float32)
    return parts


def tables():
    voxel = np.arange(512)
    coords = [
        ((voxel // 64).astype(np.float32) + np.float32(0.5)) / np.float32(8.0),
        ((voxel // 8 % 8).astype(np.float32) + np.float32(0.5)) / np.float32(8.0),
        ((voxel % 8).astype(np.float32) + np.float32(0.5)) / np.float32(8.0),
    ]
    linear = [[np.float32(1.0) - t, t] for t in coords]
    quad = [[s[0] * s[0], s[0] * s[1], s[1] * s[1]] for s in linear]
    shapes = np.stack([linear[0][i] * linear[1][j] * linear[2][l] for i, j, l in NODES])
    squares = np.stack(
        [quad[0][a] * quad[1][b] * quad[2][c] for a in range(3) for b in range(3) for c in range(3)]
    )
    squares = np.pad(squares, ((0, 5), (0, 0))) / np.float32(UNIT)
    square_table = np.concatenate(split(squares.astype(np.float32), 2), axis=0)
    shape_table = np.concatenate(split(shapes.astype(np.float32), 2), axis=0)
    return (square_table, shape_table)


def spread_stride(rows):
    return rows + 4 if rows % 8 == 0 else rows


def contract(table, part):
    return lax.dot_general(
        table, part, (((1,), (1,)), ((), ())), preferred_element_type=jnp.float32
    )


def row_of(turn, tile_x):
    place = turn - (tile_x - 2 * BOUND - 1)
    upper = tile_x - BOUND - 1 + place // 2
    edge = jnp.where(place % 2 == 0, upper, BOUND - 1 - place // 2)
    return jnp.where(place < 0, turn + BOUND, edge)


def step_kernel(
    sizes,
    tile_x,
    tile_y,
    depth,
    offset_hbm,
    square_hbm,
    shape_hbm,
    grad_hbm,
    mask_hbm,
    scan_ref,
    image_hbm,
    weight_hbm,
    out_ref,
    grad_ref,
    mask_ref,
    own_ref,
    image_ref,
    weight_ref,
    before_ref,
    after_ref,
    beyond_ref,
    ahead_ref,
    wide_ref,
    part_ref,
    fetched_ref,
    high_ref,
    low_ref,
    hess_ref,
    load_ref,
    field_ref,
    value_ref,
    out_e,
    out_w,
    out_n,
    out_s,
    in_w,
    in_e,
    in_s,
    in_n,
    in_sw,
    in_ne,
    in_nw,
    in_se,
    own_x,
    got_x,
    own_y,
    got_y,
    offset_ref,
    square_ref,
    shape_ref,
    table_ref,
    source_ref,
    local_sems,
    halo_send,
    halo_recv,
    send_sems,
    recv_sems,
    send_x,
    recv_x,
    send_y,
    recv_y,
):
    n_gx, n_gy = sizes
    gx = lax.axis_index("gx")
    gy = lax.axis_index("gy")
    not_first_x, not_last_x = (gx > 0, gx < n_gx - 1)
    not_first_y, not_last_y = (gy > 0, gy < n_gy - 1)
    both = jnp.logical_and
    wide = depth * tile_y
    span_x = tile_x + 2 * BOUND + 1
    stride_y = spread_stride(depth * span_x * 4)
    stride_x = spread_stride(tile_x)
    stride_f = spread_stride(8 * depth)

    def remote(source, target, sends, receives, device):
        return pltpu.make_async_remote_copy(
            src_ref=source,
            dst_ref=target,
            send_sem=sends,
            recv_sem=receives,
            device_id=device,
            device_id_type=MESH,
        )

    def halo(k, source, target, device):
        return remote(source, target, halo_send.at[k], halo_recv.at[k], device)

    every = slice(None)
    low_y, high_y = (pl.ds(0, EDGE), pl.ds(tile_y - EDGE, EDGE))
    near_y, far_y = ((gx, gy - 1), (gx, gy + 1))
    middle = pl.ds(BOUND, tile_x)

    def y_copies():
        return [
            (halo(0, scan_ref.at[every, low_y], beyond_ref.at[middle], near_y), not_first_y, not_last_y),
            (halo(1, scan_ref.at[every, high_y], ahead_ref.at[middle], far_y), not_last_y, not_first_y),
        ]

    inner_y = pl.ds(EDGE, tile_y - 2 * EDGE)
    bands = 2 * BOUND + 1

    def after_parts(k, parts):
        return [
            (
                halo(2 + 3 * k + p, scan_ref.at[k, cut], after_ref.at[k, cut], (gx - 1, gy)),
                not_first_x,
                not_last_x,
            )
            for p, cut in enumerate((low_y, high_y, inner_y))
            if p in parts
        ]

    def before_parts(k, parts):
        row = tile_x - BOUND + k
        first = 5 + 3 * BOUND + 3 * k
        return [
            (
                halo(first + p, scan_ref.at[row, cut], before_ref.at[k, cut], (gx + 1, gy)),
                not_last_x,
                not_first_x,
            )
            for p, cut in enumerate((low_y, high_y, inner_y))
            if p in parts
        ]

    edges, rest, whole_row = ((0, 1), (2,), (0, 1, 2))

    def corner_copies(first, band, k, row, present):
        return [
            (
                halo(first, band.at[k, low_y], beyond_ref.at[row], near_y),
                both(present, not_first_y),
                both(present, not_last_y),
            ),
            (
                halo(first + 1, band.at[k, high_y], ahead_ref.at[row], far_y),
                both(present, not_last_y),
                both(present, not_first_y),
            ),
        ]

    def after_corners(k):
        first = 2 + 3 * bands + 2 * k
        return corner_copies(first, after_ref, k, BOUND + tile_x + k, not_last_x)

    def before_corners(k):
        first = 4 + 3 * bands + 2 * BOUND + 2 * k
        return corner_copies(first, before_ref, k, k, not_first_x)

    def begin(copies):
        for one, sends, _ in copies:
            pl.when(sends)(one.start)

    def arrive(copies):
        for one, _, receives in copies:
            pl.when(receives)(one.wait_recv)

    def sent(copies):
        for one, sends, _ in copies:
            pl.when(sends)(one.wait_send)

    def put_wide(value, at_x, at_y):
        count = value.shape[0]
        for layer in range(depth):
            for chunk in range(4):
                lanes = slice(layer * 512 + chunk * 128, layer * 512 + chunk * 128 + 128)
                start = at_y * stride_y + (layer * span_x + at_x) * 4 + chunk
                wide_ref[pl.ds(start, count, stride=stride_y), :] = value[:, lanes]

    def put_sides(row, inside):
        value = beyond_ref[row].astype(jnp.float32)[0:BOUND]
        put_wide(jnp.where(both(inside, not_last_y), value, 0.0), row, BOUND + tile_y)
        value = ahead_ref[row].astype(jnp.float32)[EDGE - BOUND :]
        put_wide(jnp.where(both(inside, not_first_y), value, 0.0), row, 0)

    def put_band(band, k, row, inside):
        for first in range(0, tile_y, 16):
            value = band[k, pl.ds(first, 16), :].astype(jnp.float32)
            put_wide(jnp.where(inside, value, 0.0), row, BOUND + first)
        put_sides(row, inside)

    def first_copies(x):
        return [
            pltpu.make_async_copy(grad_hbm.at[:, x], grad_ref.at[:, x], local_sems.at[0, x]),
            pltpu.make_async_copy(mask_hbm.at[x], mask_ref.at[x], local_sems.at[1, x]),
            pltpu.make_async_copy(scan_ref.at[x], own_ref.at[x], local_sems.at[2, x]),
        ]

    def second_copies(x):
        return [
            pltpu.make_async_copy(image_hbm.at[x], image_ref.at[x], local_sems.at[3, x]),
            pltpu.make_async_copy(weight_hbm.at[x], weight_ref.at[x], local_sems.at[4, x]),
        ]

    def start_first(x, carry):
        for one in first_copies(x):
            one.start()
        return carry

    def start_second(turn, carry):
        for one in second_copies(row_of(turn, tile_x)):
            one.start()
        return carry

    barrier = pltpu.get_barrier_semaphore()
    there_x = {-1: not_first_x, 0: gx >= 0, 1: not_last_x}
    there_y = {-1: not_first_y, 0: gy >= 0, 1: not_last_y}

    def greet(target, steps):
        found = 0
        for dx, dy in steps:
            present = both(there_x[dx], there_y[dy])
            found = found + jnp.where(present, 1, 0)

            @pl.when(present)
            def _(dx=dx, dy=dy):
                pl.semaphore_signal(
                    target, inc=1, device_id=(gx + dx, gy + dy), device_id_type=MESH
                )

        return found

    for k in range(1, n_gx):
        pl.semaphore_signal(
            barrier, inc=1, device_id=((gx + k) % n_gx, gy), device_id_type=MESH
        )
    for k in range(1, n_gy):
        pl.semaphore_signal(
            barrier, inc=1, device_id=(gx, (gy + k) % n_gy), device_id_type=MESH
        )
    corners = greet(barrier, [(dx, dy) for dx in (-1, 1) for dy in (-1, 1)])
    lax.fori_loop(0, 2, start_first, 0)
    small_copies = [
        pltpu.make_async_copy(one, other, local_sems.at[5, k])
        for k, (one, other) in enumerate(
            ((square_hbm, square_ref), (offset_hbm, offset_ref), (shape_hbm, shape_ref))
        )
    ]
    for one in small_copies:
        one.start()
    pl.semaphore_wait(barrier, n_gx - 1 + n_gy - 1 + corners)
    begin(y_copies())
    for parts in (edges, rest):
        for k in range(BOUND + 1):
            begin(after_parts(k, parts))
            if k < BOUND:
                begin(before_parts(BOUND - 1 - k, parts))
    lax.fori_loop(2, tile_x, start_first, 0)
    lax.fori_loop(0, tile_x, start_second, 0)
    for buffer, dx, dy in (
        (in_w, -1, 0),
        (in_e, 1, 0),
        (in_s, 0, -1),
        (in_n, 0, 1),
        (in_sw, -1, -1),
        (in_ne, 1, 1),
        (in_nw, -1, 1),
        (in_se, 1, -1),
    ):

        @pl.when(jnp.logical_not(both(there_x[dx], there_y[dy])))
        def _(buffer=buffer):
            buffer[...] = jnp.zeros_like(buffer)

    for buffer in (out_e, out_w, out_n, out_s):
        buffer[...] = jnp.zeros_like(buffer)

    def hessian_row(x, carry):
        for one in first_copies(x):
            one.wait()
        for first in range(0, tile_y, 16):
            value = own_ref[x, pl.ds(first, 16), :].astype(jnp.float32)
            put_wide(value, BOUND + x, BOUND + first)
        for layer in range(depth):
            lanes = pl.ds(layer * 512, 512)
            mask = mask_ref[x, :, lanes].astype(jnp.float32).astype(jnp.bfloat16)
            grads = [grad_ref[c, x, :, lanes] for c in range(3)]
            masked = [mask * g for g in grads]
            for c in range(3):
                grad_ref[c, x, :, lanes] = masked[c]
            for q, (c, d) in enumerate(PAIRS):
                part_ref[pl.ds(q * wide + layer * tile_y, tile_y), :] = masked[c] * grads[d]
        table = square_ref[...]
        for q in range(6):
            total = contract(table, part_ref[pl.ds(q * wide, wide), :])
            value = total[0:32] + total[32:64]
            for first in range(0, 32, 8):
                rows = pl.ds((q * 32 + first) * stride_x + x, 8, stride=stride_x)
                hess_ref[rows, :] = value[first : first + 8]
        return carry

    for one in small_copies:
        one.wait()
    extent = (tile_x, depth, tile_y)
    pos_x, layers, pos_y = [lax.broadcasted_iota(jnp.int32, extent, k) for k in range(3)]
    table = (pos_y + offset_ref[1] + BOUND) * stride_y
    table_ref[...] = table + (layers * span_x + pos_x + offset_ref[0] + BOUND) * 4
    table_copy = pltpu.make_async_copy(table_ref, source_ref, local_sems.at[5, 3])
    table_copy.start()
    lax.fori_loop(0, tile_x, hessian_row, 0)
    table_copy.wait()
    arrive(y_copies())

    def convert(i, carry):
        put_sides(BOUND + i, gx >= 0)
        return carry

    lax.fori_loop(0, tile_x, convert, 0)
    head = tile_x - 2 * BOUND - 1

    def load_row(turn, carry):
        @pl.when(both(turn >= head - BOUND - 1, turn < head))
        def _():
            k = turn - (head - BOUND - 1)
            arrive(after_parts(k, edges))
            begin(after_corners(k))

        @pl.when(both(turn >= head - BOUND, turn < head))
        def _():
            k = head - 1 - turn
            arrive(before_parts(k, edges))
            begin(before_corners(k))

        place = turn - head

        @pl.when(both(place >= 0, place % 2 == 0))
        def _():
            k = place // 2
            arrive(after_parts(k, rest) + after_corners(k))
            put_band(after_ref, k, BOUND + tile_x + k, not_last_x)

        @pl.when(both(place >= 0, place % 2 == 1))
        def _():
            k = BOUND - 1 - place // 2
            arrive(before_parts(k, rest) + before_corners(k))
            put_band(before_ref, k, k, not_first_x)

        x = row_of(turn, tile_x)
        for one in second_copies(x):
            one.wait()

        for y in range(tile_y):
            for layer in range(depth):
                row = source_ref[x, layer, y]
                fetched_ref[pl.ds(y * stride_f + layer * 8, 8), :] = wide_ref[pl.ds(row, 8), :]
        for layer in range(depth):
            for chunk in range(4):
                lanes = pl.ds(layer * 512 + chunk * 128, 128)
                part = pl.ds(chunk * 128, 128)
                near = fetched_ref[pl.ds(layer * 8 + chunk, tile_y, stride=stride_f), :]
                far = fetched_ref[pl.ds(layer * 8 + 4 + chunk, tile_y, stride=stride_f), :]
                weight = weight_ref[x, :, lanes].astype(jnp.float32)
                warped = weight * near + (1.0 - weight) * far
                image = image_ref[x, :, lanes].astype(jnp.float32) - warped
                image = image.astype(jnp.bfloat16).astype(jnp.float32)
                for c in range(3):
                    rows = pl.ds(c * wide + layer * tile_y, tile_y)
                    value = image * grad_ref[c, x, :, lanes].astype(jnp.float32)
                    high = value.astype(jnp.bfloat16)
                    high_ref[rows, part] = high
                    low_ref[rows, part] = (value - high.astype(jnp.float32)).astype(jnp.bfloat16)
        table = shape_ref[...]
        for c in range(3):
            rows = pl.ds(c * wide, wide)
            total = contract(table, high_ref[rows, :]) + contract(table, low_ref[rows, :])
            load_ref[pl.ds(c * 8 * stride_x + x, 8, stride=stride_x), :] = total[0:8] + total[8:16]
        return carry

    lax.fori_loop(0, tile_x, load_row, 0)

    width = wide
    lane = lax.broadcasted_iota(jnp.int32, (tile_x, width), 1)
    row = lax.broadcasted_iota(jnp.int32, (tile_x, width), 0)
    in_tile = lane % tile_y
    first_y = in_tile == 0
    last_y = in_tile == tile_y - 1
    first_x = row == 0
    last_x = row == tile_x - 1
    topmost = lane >= width - tile_y
    above = lane >= tile_y
    first_8, last_8 = (first_y[0:8], last_y[0:8])
    turn_y = tile_y - 1
    body, tail = (pl.ds(0, tile_x), pl.ds(tile_x, 8))
    upper, lower = (pl.ds(0, 8), pl.ds(8, 8))

    def roll(value, shift, axis):
        return pltpu.roll(value, shift % value.shape[axis], axis)

    def shift_x(value):
        return jnp.where(first_x, 0.0, roll(value, 1, 0))

    def copies(phase):
        table = [
            (out_e, lower, in_sw, 1, 1),
            (out_e, None, in_w, 1, 0),
            (out_n, None, in_s, 0, 1),
            (out_w, upper, in_ne, -1, -1),
            (out_e, upper, in_nw, 1, -1),
            (out_w, lower, in_se, -1, 1),
            (out_w, None, in_e, -1, 0),
            (out_s, None, in_n, 0, -1),
        ]
        if phase == PHASES - 1:
            table = table[:3]
        far, near = ([], [])
        for k, (src, rows, dst, dx, dy) in enumerate(table):
            send_ok, recv_ok = (gx >= 0, gx >= 0)
            if dx:
                send_ok = not_last_x if dx > 0 else not_first_x
                recv_ok = not_first_x if dx > 0 else not_last_x
            if dy:
                send_ok = both(send_ok, not_last_y if dy > 0 else not_first_y)
                recv_ok = both(recv_ok, not_first_y if dy > 0 else not_last_y)
            source = src.at[phase] if rows is None else src.at[phase, rows]
            one = remote(
                source,
                dst.at[phase],
                send_sems.at[phase, k],
                recv_sems.at[phase, k],
                (gx + dx, gy + dy),
            )
            (far if dx else near).append((one, send_ok, recv_ok))
        return (far, near)

    def assemble(phase, partial, meanwhile):
        folded = {}
        for i in range(2):
            for j in range(2):
                found = []
                for c in range(3):
                    under = partial((4 * i + 2 * j) * 3 + c)
                    over = partial((4 * i + 2 * j + 1) * 3 + c)
                    found.append(under + jnp.where(above, roll(over, tile_y, 1), 0.0))
                    folded[i, j, 3 + c] = jnp.where(topmost, over, 0.0)
                for c in range(3):
                    folded[i, j, c] = found[c]
        total, right, edge_x, edge_c = ([], [], [], [])
        for a in range(6):
            kept = [
                folded[i, 0, a] + jnp.where(first_y, 0.0, roll(folded[i, 1, a], 1, 1))
                for i in range(2)
            ]
            total.append(kept[0] + shift_x(kept[1]))
            right.append(folded[0, 1, a] + shift_x(folded[1, 1, a]))
            edge_x.append(kept[1][tile_x - 1 :])
            edge_c.append(folded[1, 1, a][tile_x - 1 :])
            out_e[phase, a : a + 1, :] = edge_x[a]
            out_e[phase, 8 + a : 9 + a, :] = edge_c[a]
            out_w[phase, a : a + 1, :] = total[a][0:1]
            out_w[phase, 8 + a : 9 + a, :] = right[a][0:1]
        far, near = copies(phase)
        begin(far)
        north = jnp.zeros((tile_x, width), jnp.float32)
        south = jnp.zeros((tile_x, width), jnp.float32)
        for a in range(6):
            north = jnp.where(in_tile == a, roll(right[a], a + 1, 1), north)
            south = jnp.where(in_tile == a, roll(total[a], a, 1), south)
            out_n[phase, tile_x + a : tile_x + a + 1, :] = edge_c[a]
            out_s[phase, tile_x + a : tile_x + a + 1, :] = edge_x[a]
        out_n[phase, body, :] = north
        out_s[phase, body, :] = south
        begin(near)
        meanwhile()
        arrive(near)
        from_s = in_s[phase, body, :]
        whole = [
            total[a] + jnp.where(first_y, roll(from_s, -(tile_y + a), 1), 0.0) for a in range(6)
        ]
        if phase < PHASES - 1:
            from_n = in_n[phase, body, :]
            right = [right[a] + roll(from_n, turn_y - a, 1) for a in range(6)]
        arrive(far)
        line = in_w[phase, upper, :] + jnp.where(
            first_8, roll(in_sw[phase], -turn_y, 1), 0.0
        )
        whole = [
            whole[a] + jnp.where(first_x, line[a : a + 1], 0.0)
            for a in range(6)
        ]
        if phase == PHASES - 1:
            return whole
        side_x = in_s[phase, tail, :] + in_se[phase]
        side_x = jnp.where(first_8, roll(side_x, -turn_y, 1), 0.0)
        side_x = jnp.where(not_last_x, out_e[phase, upper, :] + in_e[phase, upper, :] + side_x, 0.0)
        line = in_w[phase, lower, :] + roll(in_nw[phase], turn_y, 1)
        corner = in_n[phase, tail, :] + in_ne[phase]
        corner = out_e[phase, lower, :] + in_e[phase, lower, :] + roll(corner, turn_y, 1)
        corner = jnp.where(both(not_last_x, not_last_y), corner, 0.0)
        corner = jnp.where(last_8, corner, roll(side_x, -1, 1))
        for a in range(6):
            side = right[a] + jnp.where(first_x, line[a : a + 1], 0.0)
            side = jnp.where(not_last_y, side, 0.0)
            next_x = jnp.where(last_x, side_x[a : a + 1], roll(whole[a], -1, 0))
            next_y = jnp.where(last_y, side, roll(whole[a], -1, 1))
            next_c = jnp.where(last_x, corner[a : a + 1], roll(next_y, -1, 0))
            for k, value in enumerate((whole[a], next_y, next_x, next_c)):
                if a < 3:
                    field_ref[6 * k + a] = value
                    field_ref[6 * k + 3 + a] = roll(value, -tile_y, 1)
                else:
                    above_it = field_ref[6 * k + a]
                    field_ref[6 * k + a] = jnp.where(topmost, value, above_it)
        return whole

    def apply():
        for half in range(0, tile_x, 8):
            rows = pl.ds(half, 8)
            fields = [field_ref[k, rows, :] for k in range(24)]
            for n, (i, j, l) in enumerate(NODES):
                for c in range(3):
                    total = None
                    for m, (p, q, r) in enumerate(NODES):
                        kind = (i + p) * 9 + (j + q) * 3 + l + r
                        for d in range(3):
                            index = (PAIR_OF[c, d] * 32 + kind) * stride_x + half
                            term = hess_ref[pl.ds(index, 8), :] * fields[3 * m + d]
                            total = term if total is None else total + term
                    value_ref[3 * n + c, rows, :] = total

    def exchange(own, got, sends, receives, index, count, target):
        return [
            remote(
                own,
                got.at[k - 1],
                sends.at[k - 1],
                receives.at[k - 1],
                target((index + k) % count),
            )
            for k in range(1, count)
        ]

    def along_x():
        return exchange(own_x, got_x, send_x, recv_x, gx, n_gx, lambda t: (t, gy))

    def along_y():
        return exchange(own_y, got_y, send_y, recv_y, gy, n_gy, lambda t: (gx, t))

    def gather(found, own, got, count):
        for one in found:
            one.wait_recv()
        total = own[...]
        for k in range(1, count):
            total = total + got[k - 1]
        return total

    def inner(left, right):
        total = left[0] * right[0]
        for one, other in zip(left[1:], right[1:]):
            total = total + one * other
        return jnp.sum(total, axis=0, keepdims=True)

    def nothing():
        return None

    def load_part(k):
        start = ((k % 3) * 8 + k // 3) * stride_x
        return load_ref[pl.ds(start, tile_x), :]

    def value_part(k):
        return value_ref[k]

    base = [assemble(0, load_part, nothing)]
    for phase in range(1, ITERS):
        apply()
        base.append(assemble(phase, value_part, nothing))
    apply()
    last = inner([field_ref[k] for k in range(24)], [value_ref[k] for k in range(24)])
    rows = [
        inner(base[0], base[0]),
        inner(base[0], base[1]),
        inner(base[1], base[1]),
        inner(base[1], base[2]),
        inner(base[2], base[2]),
        last,
    ]
    for k in range(6):
        own_x[k : k + 1, :] = rows[k]
    own_x[6:8, :] = jnp.zeros((2, width), jnp.float32)
    for one in along_x():
        one.start()

    def pass_on():
        own_y[...] = gather(along_x(), own_x, got_x, n_gx)
        for one in along_y():
            one.start()

    base.append(assemble(ITERS, value_part, pass_on))
    sums = gather(along_y(), own_y, got_y, n_gy)
    sums = jnp.sum(sums, axis=1, keepdims=True)
    h = [sums[k : k + 1] for k in range(6)]
    sigma = tikhonov / UNIT
    a0 = h[1] / h[0]
    n1 = h[2] - a0 * h[1]
    a1 = (h[3] - 2.0 * a0 * h[2] + a0 * a0 * h[1]) / n1
    s = a0 + a1
    q = a0 * a1 - n1 / h[0]
    n2 = h[4] - s * h[3] + q * h[2]
    a2 = (h[5] - s * h[4] + q * h[3] - s * n2) / n2
    b2 = n2 / n1
    p2 = -(s + a2)
    p1 = q + a2 * s - b2
    p0 = b2 * a0 - a2 * q
    scale = 1.0 / (sigma * (sigma * (p2 - sigma) - p1) + p0)
    r2, r1, r0 = (p2 * scale, p1 * scale, p0 * scale)
    turn_back = -scale / UNIT
    i1 = (p2 - sigma) * turn_back
    i0 = (p1 - sigma * p2 + sigma * sigma) * turn_back
    for a in range(6):
        inc = turn_back * base[2][a] + i1 * base[1][a] + i0 * base[0][a]
        res = scale * base[3][a] + r2 * base[2][a] + r1 * base[1][a] + r0 * base[0][a]
        out_ref[a] = inc
        out_ref[6 + a] = res
    for phase in range(PHASES):
        for group in copies(phase):
            sent(group)
    for one in along_x() + along_y():
        one.wait_send()
    sent(y_copies())
    for k in range(BOUND + 1):
        sent(after_parts(k, whole_row) + after_corners(k))
    for k in range(BOUND):
        sent(before_parts(k, whole_row) + before_corners(k))


def format_kernel(depth, value_ref, inc_ref, res_ref):
    tile_y = inc_ref.shape[3]
    width = value_ref.shape[2]
    for out, first in ((inc_ref, 0), (res_ref, 6)):
        for c in range(3):
            value = value_ref[first + c]
            for layer in range(depth):
                out[c, layer] = value[:, layer * tile_y : (layer + 1) * tile_y]
            out[c, depth] = value_ref[first + 3 + c][:, width - tile_y :]


def per_device(
    reference_scan, ref_gradient, deformed_scan, interp_weights, sample_mask, block_list, offsets
):
    tile_x, tile_y, column = reference_scan.shape
    depth = column // 512
    width = depth * tile_y
    square_table, shape_table = tables()
    n_gx, n_gy = (lax.axis_size("gx"), lax.axis_size("gy"))
    span_x, span_y = (tile_x + 2 * BOUND + 1, tile_y + 2 * BOUND)
    f32, bf16, vmem, dma = (jnp.float32, jnp.bfloat16, pltpu.VMEM, pltpu.SemaphoreType.DMA)
    part = jax.ShapeDtypeStruct((3, depth + 1, tile_x, tile_y), f32)
    halos = 2 + 5 * (2 * BOUND + 1)
    whole = pl.BlockSpec(memory_space=pltpu.VMEM)
    anywhere = pl.BlockSpec(memory_space=pl.ANY)
    packed = pl.pallas_call(
        functools.partial(step_kernel, (n_gx, n_gy), tile_x, tile_y, depth),
        out_shape=vmem((12, tile_x, width), f32),
        in_specs=[anywhere] * 8,
        out_specs=whole,
        scratch_shapes=[
            vmem((3, tile_x, tile_y, column), bf16),
            vmem((tile_x, tile_y, column), jnp.int32),
            vmem((tile_x, tile_y, column), bf16),
            vmem((tile_x, tile_y, column), bf16),
            vmem((tile_x, tile_y, column), bf16),
            vmem((BOUND, tile_y, column), bf16),
            vmem((BOUND + 1, tile_y, column), bf16),
            vmem((span_x, EDGE, column), bf16),
            vmem((span_x, EDGE, column), bf16),
            vmem((span_y * spread_stride(depth * span_x * 4), 128), f32),
            vmem((6 * width, 512), bf16),
            vmem((tile_y * spread_stride(8 * depth), 128), f32),
            vmem((3 * width, 512), bf16),
            vmem((3 * width, 512), bf16),
            vmem((6 * 32 * spread_stride(tile_x), width), f32),
            vmem((3 * 8 * spread_stride(tile_x), width), f32),
            vmem((24, tile_x, width), f32),
            vmem((24, tile_x, width), f32),
        ]
        + [
            vmem((PHASES, rows, width), f32)
            for rows in (16, 16, tile_x + 8, tile_x + 8) * 2 + (8, 8, 8, 8)
        ]
        + [
            vmem((8, width), f32),
            vmem((n_gx - 1, 8, width), f32),
            vmem((8, width), f32),
            vmem((n_gy - 1, 8, width), f32),
            vmem((2, tile_x, depth, tile_y), jnp.int32),
            vmem(square_table.shape, bf16),
            vmem(shape_table.shape, bf16),
            vmem((tile_x, depth, tile_y), jnp.int32),
            pltpu.SMEM((tile_x, depth, tile_y), jnp.int32),
            dma((6, tile_x)),
            dma((halos,)),
            dma((halos,)),
            dma((PHASES, 8)),
            dma((PHASES, 8)),
            dma((n_gx - 1,)),
            dma((n_gx - 1,)),
            dma((n_gy - 1,)),
            dma((n_gy - 1,)),
        ],
        compiler_params=pltpu.CompilerParams(collective_id=0, has_side_effects=True),
        name="step",
    )(
        jnp.transpose(offsets, (0, 1, 3, 2)),
        jnp.asarray(square_table),
        jnp.asarray(shape_table),
        ref_gradient,
        sample_mask,
        deformed_scan,
        reference_scan,
        interp_weights,
    )
    increment, residual = pl.pallas_call(
        functools.partial(format_kernel, depth),
        out_shape=(part, part),
        in_specs=[whole],
        out_specs=(whole, whole),
        compiler_params=pltpu.CompilerParams(vmem_limit_bytes=2**21),
        name="format",
    )(packed)

    def nodal(value):
        return jnp.transpose(value, (0, 2, 3, 1))

    return (nodal(increment), nodal(residual))


def solution(mesh):
    return jax.shard_map(
        per_device,
        mesh=mesh,
        in_specs=(
            P("gx", "gy", None),
            P(None, "gx", "gy", None),
            P("gx", "gy", None),
            P("gx", "gy", None),
            P("gx", "gy", None),
            P("gx", "gy"),
            P(None, "gx", "gy", None),
        ),
        out_specs=(P(None, "gx", "gy", None), P(None, "gx", "gy", None)),
        check_vma=False,
    )
```

```python
import functools

import jax
import jax.numpy as jnp
import ml_dtypes
import numpy as np
from jax import lax
from jax.experimental import pallas as pl
from jax.experimental.pallas import tpu as pltpu
from jax.sharding import PartitionSpec as P

BOUND = 4
ITERS = 3
PHASES = ITERS + 1
EDGE = 8

tikhonov = 8.0
UNIT = 64.0

NODES = [(n >> 2 & 1, n >> 1 & 1, n & 1) for n in range(8)]
PAIRS = [(c, d) for c in range(3) for d in range(c, 3)]
PAIR_OF = {(c, d): PAIRS.index((min(c, d), max(c, d))) for c in range(3) for d in range(3)}
MESH = pl.DeviceIdType.MESH


def split(table, count):
    parts = []
    for _ in range(count):
        part = table.astype(ml_dtypes.bfloat16)
        parts.append(part)
        table = table - part.astype(np.float32)
    return parts


def tables():
    voxel = np.arange(512)
    coords = [
        ((voxel // 64).astype(np.float32) + np.float32(0.5)) / np.float32(8.0),
        ((voxel // 8 % 8).astype(np.float32) + np.float32(0.5)) / np.float32(8.0),
        ((voxel % 8).astype(np.float32) + np.float32(0.5)) / np.float32(8.0),
    ]
    linear = [[np.float32(1.0) - t, t] for t in coords]
    quad = [[s[0] * s[0], s[0] * s[1], s[1] * s[1]] for s in linear]
    shapes = np.stack([linear[0][i] * linear[1][j] * linear[2][l] for i, j, l in NODES])
    squares = np.stack(
        [quad[0][a] * quad[1][b] * quad[2][c] for a in range(3) for b in range(3) for c in range(3)]
    )
    squares = np.pad(squares, ((0, 5), (0, 0))) / np.float32(UNIT)
    square_table = np.concatenate(split(squares.astype(np.float32), 2), axis=0)
    shape_table = np.concatenate(split(shapes.astype(np.float32), 2), axis=0)
    return (square_table, shape_table)


def spread_stride(rows):
    return rows + 4 if rows % 8 == 0 else rows


def contract(table, part):
    return lax.dot_general(
        table, part, (((1,), (1,)), ((), ())), preferred_element_type=jnp.float32
    )


def row_of(turn, tile_x):
    place = turn - (tile_x - 2 * BOUND - 1)
    upper = tile_x - BOUND - 1 + place // 2
    edge = jnp.where(place % 2 == 0, upper, BOUND - 1 - place // 2)
    return jnp.where(place < 0, turn + BOUND, edge)


def step_kernel(
    sizes,
    tile_x,
    tile_y,
    depth,
    offset_hbm,
    square_hbm,
    shape_hbm,
    grad_hbm,
    mask_hbm,
    scan_ref,
    image_hbm,
    weight_hbm,
    out_ref,
    grad_ref,
    mask_ref,
    own_ref,
    image_ref,
    weight_ref,
    before_ref,
    after_ref,
    beyond_ref,
    ahead_ref,
    wide_ref,
    part_ref,
    fetched_ref,
    high_ref,
    low_ref,
    hess_ref,
    load_ref,
    field_ref,
    value_ref,
    out_e,
    out_w,
    out_n,
    out_s,
    in_w,
    in_e,
    in_s,
    in_n,
    in_sw,
    in_ne,
    in_nw,
    in_se,
    own_x,
    got_x,
    offset_ref,
    square_ref,
    shape_ref,
    table_ref,
    source_ref,
    local_sems,
    halo_send,
    halo_recv,
    send_sems,
    recv_sems,
    send_x,
    recv_x,
):
    n_gx, n_gy = sizes
    gx = lax.axis_index("gx")
    gy = lax.axis_index("gy")
    not_first_x, not_last_x = (gx > 0, gx < n_gx - 1)
    not_first_y, not_last_y = (gy > 0, gy < n_gy - 1)
    both = jnp.logical_and
    wide = depth * tile_y
    span_x = tile_x + 2 * BOUND + 1
    stride_y = spread_stride(depth * span_x * 4)
    stride_x = spread_stride(tile_x)
    stride_f = spread_stride(8 * depth)

    def remote(source, target, sends, receives, device):
        return pltpu.make_async_remote_copy(
            src_ref=source,
            dst_ref=target,
            send_sem=sends,
            recv_sem=receives,
            device_id=device,
            device_id_type=MESH,
        )

    def halo(k, source, target, device):
        return remote(source, target, halo_send.at[k], halo_recv.at[k], device)

    every = slice(None)
    low_y, high_y = (pl.ds(0, EDGE), pl.ds(tile_y - EDGE, EDGE))
    near_y, far_y = ((gx, gy - 1), (gx, gy + 1))
    middle = pl.ds(BOUND, tile_x)

    def y_copies():
        return [
            (halo(0, scan_ref.at[every, low_y], beyond_ref.at[middle], near_y), not_first_y, not_last_y),
            (halo(1, scan_ref.at[every, high_y], ahead_ref.at[middle], far_y), not_last_y, not_first_y),
        ]

    inner_y = pl.ds(EDGE, tile_y - 2 * EDGE)
    bands = 2 * BOUND + 1

    def after_parts(k, parts):
        return [
            (
                halo(2 + 3 * k + p, scan_ref.at[k, cut], after_ref.at[k, cut], (gx - 1, gy)),
                not_first_x,
                not_last_x,
            )
            for p, cut in enumerate((low_y, high_y, inner_y))
            if p in parts
        ]

    def before_parts(k, parts):
        row = tile_x - BOUND + k
        first = 5 + 3 * BOUND + 3 * k
        return [
            (
                halo(first + p, scan_ref.at[row, cut], before_ref.at[k, cut], (gx + 1, gy)),
                not_last_x,
                not_first_x,
            )
            for p, cut in enumerate((low_y, high_y, inner_y))
            if p in parts
        ]

    edges, rest, whole_row = ((0, 1), (2,), (0, 1, 2))

    def corner_copies(first, band, k, row, present):
        return [
            (
                halo(first, band.at[k, low_y], beyond_ref.at[row], near_y),
                both(present, not_first_y),
                both(present, not_last_y),
            ),
            (
                halo(first + 1, band.at[k, high_y], ahead_ref.at[row], far_y),
                both(present, not_last_y),
                both(present, not_first_y),
            ),
        ]

    def after_corners(k):
        first = 2 + 3 * bands + 2 * k
        return corner_copies(first, after_ref, k, BOUND + tile_x + k, not_last_x)

    def before_corners(k):
        first = 4 + 3 * bands + 2 * BOUND + 2 * k
        return corner_copies(first, before_ref, k, k, not_first_x)

    def begin(copies):
        for one, sends, _ in copies:
            pl.when(sends)(one.start)

    def arrive(copies):
        for one, _, receives in copies:
            pl.when(receives)(one.wait_recv)

    def sent(copies):
        for one, sends, _ in copies:
            pl.when(sends)(one.wait_send)

    def put_wide(value, at_x, at_y):
        count = value.shape[0]
        for layer in range(depth):
            for chunk in range(4):
                lanes = slice(layer * 512 + chunk * 128, layer * 512 + chunk * 128 + 128)
                start = at_y * stride_y + (layer * span_x + at_x) * 4 + chunk
                wide_ref[pl.ds(start, count, stride=stride_y), :] = value[:, lanes]

    def put_sides(row, inside):
        value = beyond_ref[row].astype(jnp.float32)[0:BOUND]
        put_wide(jnp.where(both(inside, not_last_y), value, 0.0), row, BOUND + tile_y)
        value = ahead_ref[row].astype(jnp.float32)[EDGE - BOUND :]
        put_wide(jnp.where(both(inside, not_first_y), value, 0.0), row, 0)

    def put_band(band, k, row, inside):
        for first in range(0, tile_y, 16):
            value = band[k, pl.ds(first, 16), :].astype(jnp.float32)
            put_wide(jnp.where(inside, value, 0.0), row, BOUND + first)
        put_sides(row, inside)

    def first_copies(x):
        return [
            pltpu.make_async_copy(grad_hbm.at[:, x], grad_ref.at[:, x], local_sems.at[0, x]),
            pltpu.make_async_copy(mask_hbm.at[x], mask_ref.at[x], local_sems.at[1, x]),
            pltpu.make_async_copy(scan_ref.at[x], own_ref.at[x], local_sems.at[2, x]),
        ]

    def second_copies(x):
        return [
            pltpu.make_async_copy(image_hbm.at[x], image_ref.at[x], local_sems.at[3, x]),
            pltpu.make_async_copy(weight_hbm.at[x], weight_ref.at[x], local_sems.at[4, x]),
        ]

    def start_first(x, carry):
        for one in first_copies(x):
            one.start()
        return carry

    def start_second(turn, carry):
        for one in second_copies(row_of(turn, tile_x)):
            one.start()
        return carry

    barrier = pltpu.get_barrier_semaphore()
    there_x = {-1: not_first_x, 0: gx >= 0, 1: not_last_x}
    there_y = {-1: not_first_y, 0: gy >= 0, 1: not_last_y}

    for k in range(1, n_gx * n_gy):
        other = (gx * n_gy + gy + k) % (n_gx * n_gy)
        pl.semaphore_signal(
            barrier,
            inc=1,
            device_id=(other // n_gy, other % n_gy),
            device_id_type=MESH,
        )
    lax.fori_loop(0, 2, start_first, 0)
    small_copies = [
        pltpu.make_async_copy(one, other, local_sems.at[5, k])
        for k, (one, other) in enumerate(
            ((square_hbm, square_ref), (offset_hbm, offset_ref), (shape_hbm, shape_ref))
        )
    ]
    for one in small_copies:
        one.start()
    pl.semaphore_wait(barrier, n_gx * n_gy - 1)
    begin(y_copies())
    for parts in (edges, rest):
        for k in range(BOUND + 1):
            begin(after_parts(k, parts))
            if k < BOUND:
                begin(before_parts(BOUND - 1 - k, parts))
    lax.fori_loop(2, tile_x, start_first, 0)
    lax.fori_loop(0, tile_x, start_second, 0)
    for buffer, dx, dy in (
        (in_w, -1, 0),
        (in_e, 1, 0),
        (in_s, 0, -1),
        (in_n, 0, 1),
        (in_sw, -1, -1),
        (in_ne, 1, 1),
        (in_nw, -1, 1),
        (in_se, 1, -1),
    ):

        @pl.when(jnp.logical_not(both(there_x[dx], there_y[dy])))
        def _(buffer=buffer):
            buffer[...] = jnp.zeros_like(buffer)

    for buffer in (out_e, out_w, out_n, out_s):
        buffer[...] = jnp.zeros_like(buffer)

    def hessian_row(x, carry):
        for one in first_copies(x):
            one.wait()
        for first in range(0, tile_y, 16):
            value = own_ref[x, pl.ds(first, 16), :].astype(jnp.float32)
            put_wide(value, BOUND + x, BOUND + first)
        for layer in range(depth):
            lanes = pl.ds(layer * 512, 512)
            mask = mask_ref[x, :, lanes].astype(jnp.float32).astype(jnp.bfloat16)
            grads = [grad_ref[c, x, :, lanes] for c in range(3)]
            masked = [mask * g for g in grads]
            for c in range(3):
                grad_ref[c, x, :, lanes] = masked[c]
            for q, (c, d) in enumerate(PAIRS):
                part_ref[pl.ds(q * wide + layer * tile_y, tile_y), :] = masked[c] * grads[d]
        table = square_ref[...]
        for q in range(6):
            total = contract(table, part_ref[pl.ds(q * wide, wide), :])
            value = total[0:32] + total[32:64]
            for first in range(0, 32, 8):
                rows = pl.ds((q * 32 + first) * stride_x + x, 8, stride=stride_x)
                hess_ref[rows, :] = value[first : first + 8]
        return carry

    for one in small_copies:
        one.wait()
    extent = (tile_x, depth, tile_y)
    pos_x, layers, pos_y = [lax.broadcasted_iota(jnp.int32, extent, k) for k in range(3)]
    table = (pos_y + offset_ref[1] + BOUND) * stride_y
    table_ref[...] = table + (layers * span_x + pos_x + offset_ref[0] + BOUND) * 4
    table_copy = pltpu.make_async_copy(table_ref, source_ref, local_sems.at[5, 3])
    table_copy.start()
    lax.fori_loop(0, tile_x, hessian_row, 0)
    table_copy.wait()
    arrive(y_copies())

    def convert(i, carry):
        put_sides(BOUND + i, gx >= 0)
        return carry

    lax.fori_loop(0, tile_x, convert, 0)
    head = tile_x - 2 * BOUND - 1

    def load_row(turn, carry):
        @pl.when(both(turn >= head - BOUND - 1, turn < head))
        def _():
            k = turn - (head - BOUND - 1)
            arrive(after_parts(k, edges))
            begin(after_corners(k))

        @pl.when(both(turn >= head - BOUND, turn < head))
        def _():
            k = head - 1 - turn
            arrive(before_parts(k, edges))
            begin(before_corners(k))

        place = turn - head

        @pl.when(both(place >= 0, place % 2 == 0))
        def _():
            k = place // 2
            arrive(after_parts(k, rest) + after_corners(k))
            put_band(after_ref, k, BOUND + tile_x + k, not_last_x)

        @pl.when(both(place >= 0, place % 2 == 1))
        def _():
            k = BOUND - 1 - place // 2
            arrive(before_parts(k, rest) + before_corners(k))
            put_band(before_ref, k, k, not_first_x)

        x = row_of(turn, tile_x)
        for one in second_copies(x):
            one.wait()

        for y in range(tile_y):
            for layer in range(depth):
                row = source_ref[x, layer, y]
                fetched_ref[pl.ds(y * stride_f + layer * 8, 8), :] = wide_ref[pl.ds(row, 8), :]
        for layer in range(depth):
            for chunk in range(4):
                lanes = pl.ds(layer * 512 + chunk * 128, 128)
                part = pl.ds(chunk * 128, 128)
                near = fetched_ref[pl.ds(layer * 8 + chunk, tile_y, stride=stride_f), :]
                far = fetched_ref[pl.ds(layer * 8 + 4 + chunk, tile_y, stride=stride_f), :]
                weight = weight_ref[x, :, lanes].astype(jnp.float32)
                warped = weight * near + (1.0 - weight) * far
                image = image_ref[x, :, lanes].astype(jnp.float32) - warped
                image = image.astype(jnp.bfloat16).astype(jnp.float32)
                for c in range(3):
                    rows = pl.ds(c * wide + layer * tile_y, tile_y)
                    value = image * grad_ref[c, x, :, lanes].astype(jnp.float32)
                    high = value.astype(jnp.bfloat16)
                    high_ref[rows, part] = high
                    low_ref[rows, part] = (value - high.astype(jnp.float32)).astype(jnp.bfloat16)
        table = shape_ref[...]
        for c in range(3):
            rows = pl.ds(c * wide, wide)
            total = contract(table, high_ref[rows, :]) + contract(table, low_ref[rows, :])
            load_ref[pl.ds(c * 8 * stride_x + x, 8, stride=stride_x), :] = total[0:8] + total[8:16]
        return carry

    lax.fori_loop(0, tile_x, load_row, 0)

    width = wide
    lane = lax.broadcasted_iota(jnp.int32, (tile_x, width), 1)
    row = lax.broadcasted_iota(jnp.int32, (tile_x, width), 0)
    in_tile = lane % tile_y
    first_y = in_tile == 0
    last_y = in_tile == tile_y - 1
    first_x = row == 0
    last_x = row == tile_x - 1
    topmost = lane >= width - tile_y
    above = lane >= tile_y
    first_8, last_8 = (first_y[0:8], last_y[0:8])
    turn_y = tile_y - 1
    body, tail = (pl.ds(0, tile_x), pl.ds(tile_x, 8))
    upper, lower = (pl.ds(0, 8), pl.ds(8, 8))

    def roll(value, shift, axis):
        return pltpu.roll(value, shift % value.shape[axis], axis)

    def shift_x(value):
        return jnp.where(first_x, 0.0, roll(value, 1, 0))

    def copies(phase):
        table = [
            (out_e, lower, in_sw, 1, 1),
            (out_e, None, in_w, 1, 0),
            (out_n, None, in_s, 0, 1),
            (out_w, upper, in_ne, -1, -1),
            (out_e, upper, in_nw, 1, -1),
            (out_w, lower, in_se, -1, 1),
            (out_w, None, in_e, -1, 0),
            (out_s, None, in_n, 0, -1),
        ]
        if phase == PHASES - 1:
            table = table[:3]
        far, near = ([], [])
        for k, (src, rows, dst, dx, dy) in enumerate(table):
            send_ok, recv_ok = (gx >= 0, gx >= 0)
            if dx:
                send_ok = not_last_x if dx > 0 else not_first_x
                recv_ok = not_first_x if dx > 0 else not_last_x
            if dy:
                send_ok = both(send_ok, not_last_y if dy > 0 else not_first_y)
                recv_ok = both(recv_ok, not_first_y if dy > 0 else not_last_y)
            source = src.at[phase] if rows is None else src.at[phase, rows]
            one = remote(
                source,
                dst.at[phase],
                send_sems.at[phase, k],
                recv_sems.at[phase, k],
                (gx + dx, gy + dy),
            )
            (far if dx else near).append((one, send_ok, recv_ok))
        return (far, near)

    def assemble(phase, partial, meanwhile):
        folded = {}
        for i in range(2):
            for j in range(2):
                found = []
                for c in range(3):
                    under = partial((4 * i + 2 * j) * 3 + c)
                    over = partial((4 * i + 2 * j + 1) * 3 + c)
                    found.append(under + jnp.where(above, roll(over, tile_y, 1), 0.0))
                    folded[i, j, 3 + c] = jnp.where(topmost, over, 0.0)
                for c in range(3):
                    folded[i, j, c] = found[c]
        total, right, edge_x, edge_c = ([], [], [], [])
        for a in range(6):
            kept = [
                folded[i, 0, a] + jnp.where(first_y, 0.0, roll(folded[i, 1, a], 1, 1))
                for i in range(2)
            ]
            total.append(kept[0] + shift_x(kept[1]))
            right.append(folded[0, 1, a] + shift_x(folded[1, 1, a]))
            edge_x.append(kept[1][tile_x - 1 :])
            edge_c.append(folded[1, 1, a][tile_x - 1 :])
            out_e[phase, a : a + 1, :] = edge_x[a]
            out_e[phase, 8 + a : 9 + a, :] = edge_c[a]
            out_w[phase, a : a + 1, :] = total[a][0:1]
            out_w[phase, 8 + a : 9 + a, :] = right[a][0:1]
        far, near = copies(phase)
        begin(far)
        north = jnp.zeros((tile_x, width), jnp.float32)
        south = jnp.zeros((tile_x, width), jnp.float32)
        for a in range(6):
            north = jnp.where(in_tile == a, roll(right[a], a + 1, 1), north)
            south = jnp.where(in_tile == a, roll(total[a], a, 1), south)
            out_n[phase, tile_x + a : tile_x + a + 1, :] = edge_c[a]
            out_s[phase, tile_x + a : tile_x + a + 1, :] = edge_x[a]
        out_n[phase, body, :] = north
        out_s[phase, body, :] = south
        begin(near)
        meanwhile()
        arrive(near)
        from_s = in_s[phase, body, :]
        whole = [
            total[a] + jnp.where(first_y, roll(from_s, -(tile_y + a), 1), 0.0) for a in range(6)
        ]
        if phase < PHASES - 1:
            from_n = in_n[phase, body, :]
            right = [right[a] + roll(from_n, turn_y - a, 1) for a in range(6)]
        arrive(far)
        line = in_w[phase, upper, :] + jnp.where(
            first_8, roll(in_sw[phase], -turn_y, 1), 0.0
        )
        whole = [
            whole[a] + jnp.where(first_x, line[a : a + 1], 0.0)
            for a in range(6)
        ]
        if phase == PHASES - 1:
            return whole
        side_x = in_s[phase, tail, :] + in_se[phase]
        side_x = jnp.where(first_8, roll(side_x, -turn_y, 1), 0.0)
        side_x = jnp.where(not_last_x, out_e[phase, upper, :] + in_e[phase, upper, :] + side_x, 0.0)
        line = in_w[phase, lower, :] + roll(in_nw[phase], turn_y, 1)
        corner = in_n[phase, tail, :] + in_ne[phase]
        corner = out_e[phase, lower, :] + in_e[phase, lower, :] + roll(corner, turn_y, 1)
        corner = jnp.where(both(not_last_x, not_last_y), corner, 0.0)
        corner = jnp.where(last_8, corner, roll(side_x, -1, 1))
        for a in range(6):
            side = right[a] + jnp.where(first_x, line[a : a + 1], 0.0)
            side = jnp.where(not_last_y, side, 0.0)
            next_x = jnp.where(last_x, side_x[a : a + 1], roll(whole[a], -1, 0))
            next_y = jnp.where(last_y, side, roll(whole[a], -1, 1))
            next_c = jnp.where(last_x, corner[a : a + 1], roll(next_y, -1, 0))
            for k, value in enumerate((whole[a], next_y, next_x, next_c)):
                if a < 3:
                    field_ref[6 * k + a] = value
                    field_ref[6 * k + 3 + a] = roll(value, -tile_y, 1)
                else:
                    above_it = field_ref[6 * k + a]
                    field_ref[6 * k + a] = jnp.where(topmost, value, above_it)
        return whole

    def apply():
        for half in range(0, tile_x, 8):
            rows = pl.ds(half, 8)
            fields = [field_ref[k, rows, :] for k in range(24)]
            for n, (i, j, l) in enumerate(NODES):
                for c in range(3):
                    total = None
                    for m, (p, q, r) in enumerate(NODES):
                        kind = (i + p) * 9 + (j + q) * 3 + l + r
                        for d in range(3):
                            index = (PAIR_OF[c, d] * 32 + kind) * stride_x + half
                            term = hess_ref[pl.ds(index, 8), :] * fields[3 * m + d]
                            total = term if total is None else total + term
                    value_ref[3 * n + c, rows, :] = total

    def everyone():
        place = gx * n_gy + gy
        found = []
        for k in range(1, n_gx * n_gy):
            other = (place + k) % (n_gx * n_gy)
            found.append(
                remote(
                    own_x,
                    got_x.at[k - 1],
                    send_x.at[k - 1],
                    recv_x.at[k - 1],
                    (other // n_gy, other % n_gy),
                )
            )
        return found

    def gather(found, own, got, count):
        for one in found:
            one.wait_recv()
        total = own[...]
        for k in range(1, count):
            total = total + got[k - 1]
        return total

    def inner(left, right):
        total = left[0] * right[0]
        for one, other in zip(left[1:], right[1:]):
            total = total + one * other
        return jnp.sum(total, axis=0, keepdims=True)

    def nothing():
        return None

    def load_part(k):
        start = ((k % 3) * 8 + k // 3) * stride_x
        return load_ref[pl.ds(start, tile_x), :]

    def value_part(k):
        return value_ref[k]

    base = [assemble(0, load_part, nothing)]
    for phase in range(1, ITERS):
        apply()
        base.append(assemble(phase, value_part, nothing))
    apply()
    last = inner([field_ref[k] for k in range(24)], [value_ref[k] for k in range(24)])
    rows = [
        inner(base[0], base[0]),
        inner(base[0], base[1]),
        inner(base[1], base[1]),
        inner(base[1], base[2]),
        inner(base[2], base[2]),
        last,
    ]
    spot = lane[0:1]
    packed = jnp.zeros((1, width), jnp.float32)
    for k in range(6):
        packed = jnp.where(spot == k, jnp.sum(rows[k], axis=1, keepdims=True), packed)
    own_x[...] = packed
    for one in everyone():
        one.start()

    base.append(assemble(ITERS, value_part, nothing))
    sums = gather(everyone(), own_x, got_x, n_gx * n_gy)
    h = [sums[:, k : k + 1] for k in range(6)]
    sigma = tikhonov / UNIT
    a0 = h[1] / h[0]
    n1 = h[2] - a0 * h[1]
    a1 = (h[3] - 2.0 * a0 * h[2] + a0 * a0 * h[1]) / n1
    s = a0 + a1
    q = a0 * a1 - n1 / h[0]
    n2 = h[4] - s * h[3] + q * h[2]
    a2 = (h[5] - s * h[4] + q * h[3] - s * n2) / n2
    b2 = n2 / n1
    p2 = -(s + a2)
    p1 = q + a2 * s - b2
    p0 = b2 * a0 - a2 * q
    scale = 1.0 / (sigma * (sigma * (p2 - sigma) - p1) + p0)
    r2, r1, r0 = (p2 * scale, p1 * scale, p0 * scale)
    turn_back = -scale / UNIT
    i1 = (p2 - sigma) * turn_back
    i0 = (p1 - sigma * p2 + sigma * sigma) * turn_back
    for a in range(6):
        inc = turn_back * base[2][a] + i1 * base[1][a] + i0 * base[0][a]
        res = scale * base[3][a] + r2 * base[2][a] + r1 * base[1][a] + r0 * base[0][a]
        out_ref[a] = inc
        out_ref[6 + a] = res
    for phase in range(PHASES):
        for group in copies(phase):
            sent(group)
    for one in everyone():
        one.wait_send()
    sent(y_copies())
    for k in range(BOUND + 1):
        sent(after_parts(k, whole_row) + after_corners(k))
    for k in range(BOUND):
        sent(before_parts(k, whole_row) + before_corners(k))


def format_kernel(depth, value_ref, inc_ref, res_ref):
    tile_y = inc_ref.shape[3]
    width = value_ref.shape[2]
    for out, first in ((inc_ref, 0), (res_ref, 6)):
        for c in range(3):
            value = value_ref[first + c]
            for layer in range(depth):
                out[c, layer] = value[:, layer * tile_y : (layer + 1) * tile_y]
            out[c, depth] = value_ref[first + 3 + c][:, width - tile_y :]


def per_device(
    reference_scan, ref_gradient, deformed_scan, interp_weights, sample_mask, block_list, offsets
):
    tile_x, tile_y, column = reference_scan.shape
    depth = column // 512
    width = depth * tile_y
    square_table, shape_table = tables()
    n_gx, n_gy = (lax.axis_size("gx"), lax.axis_size("gy"))
    span_x, span_y = (tile_x + 2 * BOUND + 1, tile_y + 2 * BOUND)
    f32, bf16, vmem, dma = (jnp.float32, jnp.bfloat16, pltpu.VMEM, pltpu.SemaphoreType.DMA)
    part = jax.ShapeDtypeStruct((3, depth + 1, tile_x, tile_y), f32)
    halos = 2 + 5 * (2 * BOUND + 1)
    whole = pl.BlockSpec(memory_space=pltpu.VMEM)
    anywhere = pl.BlockSpec(memory_space=pl.ANY)
    packed = pl.pallas_call(
        functools.partial(step_kernel, (n_gx, n_gy), tile_x, tile_y, depth),
        out_shape=vmem((12, tile_x, width), f32),
        in_specs=[anywhere] * 8,
        out_specs=whole,
        scratch_shapes=[
            vmem((3, tile_x, tile_y, column), bf16),
            vmem((tile_x, tile_y, column), jnp.int32),
            vmem((tile_x, tile_y, column), bf16),
            vmem((tile_x, tile_y, column), bf16),
            vmem((tile_x, tile_y, column), bf16),
            vmem((BOUND, tile_y, column), bf16),
            vmem((BOUND + 1, tile_y, column), bf16),
            vmem((span_x, EDGE, column), bf16),
            vmem((span_x, EDGE, column), bf16),
            vmem((span_y * spread_stride(depth * span_x * 4), 128), f32),
            vmem((6 * width, 512), bf16),
            vmem((tile_y * spread_stride(8 * depth), 128), f32),
            vmem((3 * width, 512), bf16),
            vmem((3 * width, 512), bf16),
            vmem((6 * 32 * spread_stride(tile_x), width), f32),
            vmem((3 * 8 * spread_stride(tile_x), width), f32),
            vmem((24, tile_x, width), f32),
            vmem((24, tile_x, width), f32),
        ]
        + [
            vmem((PHASES, rows, width), f32)
            for rows in (16, 16, tile_x + 8, tile_x + 8) * 2 + (8, 8, 8, 8)
        ]
        + [
            vmem((1, width), f32),
            vmem((n_gx * n_gy - 1, 1, width), f32),
            vmem((2, tile_x, depth, tile_y), jnp.int32),
            vmem(square_table.shape, bf16),
            vmem(shape_table.shape, bf16),
            vmem((tile_x, depth, tile_y), jnp.int32),
            pltpu.SMEM((tile_x, depth, tile_y), jnp.int32),
            dma((6, tile_x)),
            dma((halos,)),
            dma((halos,)),
            dma((PHASES, 8)),
            dma((PHASES, 8)),
            dma((n_gx * n_gy - 1,)),
            dma((n_gx * n_gy - 1,)),
        ],
        compiler_params=pltpu.CompilerParams(collective_id=0, has_side_effects=True),
        name="step",
    )(
        jnp.transpose(offsets, (0, 1, 3, 2)),
        jnp.asarray(square_table),
        jnp.asarray(shape_table),
        ref_gradient,
        sample_mask,
        deformed_scan,
        reference_scan,
        interp_weights,
    )
    increment, residual = pl.pallas_call(
        functools.partial(format_kernel, depth),
        out_shape=(part, part),
        in_specs=[whole],
        out_specs=(whole, whole),
        compiler_params=pltpu.CompilerParams(vmem_limit_bytes=2**21),
        name="format",
    )(packed)

    def nodal(value):
        return jnp.transpose(value, (0, 2, 3, 1))

    return (nodal(increment), nodal(residual))


def solution(mesh):
    return jax.shard_map(
        per_device,
        mesh=mesh,
        in_specs=(
            P("gx", "gy", None),
            P(None, "gx", "gy", None),
            P("gx", "gy", None),
            P("gx", "gy", None),
            P("gx", "gy", None),
            P("gx", "gy"),
            P(None, "gx", "gy", None),
        ),
        out_specs=(P(None, "gx", "gy", None), P(None, "gx", "gy", None)),
        check_vma=False,
    )
```

```python
import functools

import jax
import jax.numpy as jnp
import ml_dtypes
import numpy as np
from jax import lax
from jax.experimental import pallas as pl
from jax.experimental.pallas import tpu as pltpu
from jax.sharding import PartitionSpec as P

BOUND = 4
ITERS = 3
PHASES = ITERS + 1
EDGE = 8

tikhonov = 8.0
UNIT = 64.0

NODES = [(n >> 2 & 1, n >> 1 & 1, n & 1) for n in range(8)]
PAIRS = [(c, d) for c in range(3) for d in range(c, 3)]
PAIR_OF = {(c, d): PAIRS.index((min(c, d), max(c, d))) for c in range(3) for d in range(3)}
MESH = pl.DeviceIdType.MESH


def split(table, count):
    parts = []
    for _ in range(count):
        part = table.astype(ml_dtypes.bfloat16)
        parts.append(part)
        table = table - part.astype(np.float32)
    return parts


def tables():
    voxel = np.arange(512)
    coords = [
        ((voxel // 64).astype(np.float32) + np.float32(0.5)) / np.float32(8.0),
        ((voxel // 8 % 8).astype(np.float32) + np.float32(0.5)) / np.float32(8.0),
        ((voxel % 8).astype(np.float32) + np.float32(0.5)) / np.float32(8.0),
    ]
    linear = [[np.float32(1.0) - t, t] for t in coords]
    quad = [[s[0] * s[0], s[0] * s[1], s[1] * s[1]] for s in linear]
    shapes = np.stack([linear[0][i] * linear[1][j] * linear[2][l] for i, j, l in NODES])
    squares = np.stack(
        [quad[0][a] * quad[1][b] * quad[2][c] for a in range(3) for b in range(3) for c in range(3)]
    )
    squares = np.pad(squares, ((0, 5), (0, 0))) / np.float32(UNIT)
    square_table = np.concatenate(split(squares.astype(np.float32), 2), axis=0)
    shape_table = np.concatenate(split(shapes.astype(np.float32), 2), axis=0)
    return (square_table, shape_table)


def spread_stride(rows):
    return rows + 4 if rows % 8 == 0 else rows


def contract(table, part):
    return lax.dot_general(
        table, part, (((1,), (1,)), ((), ())), preferred_element_type=jnp.float32
    )


def row_of(turn, tile_x):
    place = turn - (tile_x - 2 * BOUND - 1)
    upper = tile_x - BOUND - 1 + place // 2
    edge = jnp.where(place % 2 == 0, upper, BOUND - 1 - place // 2)
    return jnp.where(place < 0, turn + BOUND, edge)


def step_kernel(
    sizes,
    tile_x,
    tile_y,
    depth,
    offset_hbm,
    square_hbm,
    shape_hbm,
    grad_hbm,
    mask_hbm,
    scan_ref,
    image_hbm,
    weight_hbm,
    out_ref,
    grad_ref,
    mask_ref,
    own_ref,
    image_ref,
    weight_ref,
    before_ref,
    after_ref,
    beyond_ref,
    ahead_ref,
    wide_ref,
    part_ref,
    fetched_ref,
    high_ref,
    low_ref,
    hess_ref,
    load_ref,
    field_ref,
    value_ref,
    out_e,
    out_w,
    out_n,
    out_s,
    in_w,
    in_e,
    in_s,
    in_n,
    in_sw,
    in_ne,
    in_nw,
    in_se,
    own_x,
    got_x,
    offset_ref,
    square_ref,
    shape_ref,
    table_ref,
    source_ref,
    local_sems,
    halo_send,
    halo_recv,
    send_sems,
    recv_sems,
    send_x,
    recv_x,
):
    n_gx, n_gy = sizes
    gx = lax.axis_index("gx")
    gy = lax.axis_index("gy")
    not_first_x, not_last_x = (gx > 0, gx < n_gx - 1)
    not_first_y, not_last_y = (gy > 0, gy < n_gy - 1)
    both = jnp.logical_and
    wide = depth * tile_y
    span_x = tile_x + 2 * BOUND + 1
    stride_y = spread_stride(depth * span_x * 4)
    stride_x = spread_stride(tile_x)
    stride_f = spread_stride(8 * depth)

    def remote(source, target, sends, receives, device):
        return pltpu.make_async_remote_copy(
            src_ref=source,
            dst_ref=target,
            send_sem=sends,
            recv_sem=receives,
            device_id=device,
            device_id_type=MESH,
        )

    def halo(k, source, target, device):
        return remote(source, target, halo_send.at[k], halo_recv.at[k], device)

    every = slice(None)
    low_y, high_y = (pl.ds(0, EDGE), pl.ds(tile_y - EDGE, EDGE))
    near_y, far_y = ((gx, gy - 1), (gx, gy + 1))
    middle = pl.ds(BOUND, tile_x)

    def y_copies():
        return [
            (halo(0, scan_ref.at[every, low_y], beyond_ref.at[middle], near_y), not_first_y, not_last_y),
            (halo(1, scan_ref.at[every, high_y], ahead_ref.at[middle], far_y), not_last_y, not_first_y),
        ]

    inner_y = pl.ds(EDGE, tile_y - 2 * EDGE)
    bands = 2 * BOUND + 1

    def after_parts(k, parts):
        return [
            (
                halo(2 + 3 * k + p, scan_ref.at[k, cut], after_ref.at[k, cut], (gx - 1, gy)),
                not_first_x,
                not_last_x,
            )
            for p, cut in enumerate((low_y, high_y, inner_y))
            if p in parts
        ]

    def before_parts(k, parts):
        row = tile_x - BOUND + k
        first = 5 + 3 * BOUND + 3 * k
        return [
            (
                halo(first + p, scan_ref.at[row, cut], before_ref.at[k, cut], (gx + 1, gy)),
                not_last_x,
                not_first_x,
            )
            for p, cut in enumerate((low_y, high_y, inner_y))
            if p in parts
        ]

    edges, rest, whole_row = ((0, 1), (2,), (0, 1, 2))

    def corner_copies(first, band, k, row, present):
        return [
            (
                halo(first, band.at[k, low_y], beyond_ref.at[row], near_y),
                both(present, not_first_y),
                both(present, not_last_y),
            ),
            (
                halo(first + 1, band.at[k, high_y], ahead_ref.at[row], far_y),
                both(present, not_last_y),
                both(present, not_first_y),
            ),
        ]

    def after_corners(k):
        first = 2 + 3 * bands + 2 * k
        return corner_copies(first, after_ref, k, BOUND + tile_x + k, not_last_x)

    def before_corners(k):
        first = 4 + 3 * bands + 2 * BOUND + 2 * k
        return corner_copies(first, before_ref, k, k, not_first_x)

    def begin(copies):
        for one, sends, _ in copies:
            pl.when(sends)(one.start)

    def arrive(copies):
        for one, _, receives in copies:
            pl.when(receives)(one.wait_recv)

    def sent(copies):
        for one, sends, _ in copies:
            pl.when(sends)(one.wait_send)

    def put_wide(value, at_x, at_y):
        count = value.shape[0]
        for layer in range(depth):
            for chunk in range(4):
                lanes = slice(layer * 512 + chunk * 128, layer * 512 + chunk * 128 + 128)
                start = at_y * stride_y + (layer * span_x + at_x) * 4 + chunk
                wide_ref[pl.ds(start, count, stride=stride_y), :] = value[:, lanes]

    def put_sides(row, inside):
        value = beyond_ref[row].astype(jnp.float32)[0:BOUND]
        put_wide(jnp.where(both(inside, not_last_y), value, 0.0), row, BOUND + tile_y)
        value = ahead_ref[row].astype(jnp.float32)[EDGE - BOUND :]
        put_wide(jnp.where(both(inside, not_first_y), value, 0.0), row, 0)

    def put_band(band, k, row, inside):
        for first in range(0, tile_y, 16):
            value = band[k, pl.ds(first, 16), :].astype(jnp.float32)
            put_wide(jnp.where(inside, value, 0.0), row, BOUND + first)
        put_sides(row, inside)

    def first_copies(x):
        return [
            pltpu.make_async_copy(grad_hbm.at[:, x], grad_ref.at[:, x], local_sems.at[0, x]),
            pltpu.make_async_copy(mask_hbm.at[x], mask_ref.at[x], local_sems.at[1, x]),
            pltpu.make_async_copy(scan_ref.at[x], own_ref.at[x], local_sems.at[2, x]),
        ]

    def second_copies(x):
        return [
            pltpu.make_async_copy(image_hbm.at[x], image_ref.at[x], local_sems.at[3, x]),
            pltpu.make_async_copy(weight_hbm.at[x], weight_ref.at[x], local_sems.at[4, x]),
        ]

    def start_first(x, carry):
        for one in first_copies(x):
            one.start()
        return carry

    def start_second(turn, carry):
        for one in second_copies(row_of(turn, tile_x)):
            one.start()
        return carry

    barrier = pltpu.get_barrier_semaphore()
    there_x = {-1: not_first_x, 0: gx >= 0, 1: not_last_x}
    there_y = {-1: not_first_y, 0: gy >= 0, 1: not_last_y}

    for k in range(1, n_gx * n_gy):
        other = (gx * n_gy + gy + k) % (n_gx * n_gy)
        pl.semaphore_signal(
            barrier,
            inc=1,
            device_id=(other // n_gy, other % n_gy),
            device_id_type=MESH,
        )
    lax.fori_loop(0, 2, start_first, 0)
    small_copies = [
        pltpu.make_async_copy(one, other, local_sems.at[5, k])
        for k, (one, other) in enumerate(
            ((square_hbm, square_ref), (offset_hbm, offset_ref), (shape_hbm, shape_ref))
        )
    ]
    for one in small_copies:
        one.start()
    pl.semaphore_wait(barrier, n_gx * n_gy - 1)
    begin(y_copies())
    for parts in (edges, rest):
        for k in range(BOUND + 1):
            begin(after_parts(k, parts))
            if k < BOUND:
                begin(before_parts(BOUND - 1 - k, parts))
    lax.fori_loop(2, tile_x, start_first, 0)
    lax.fori_loop(0, tile_x, start_second, 0)
    for buffer, dx, dy in (
        (in_w, -1, 0),
        (in_e, 1, 0),
        (in_s, 0, -1),
        (in_n, 0, 1),
        (in_sw, -1, -1),
        (in_ne, 1, 1),
        (in_nw, -1, 1),
        (in_se, 1, -1),
    ):

        @pl.when(jnp.logical_not(both(there_x[dx], there_y[dy])))
        def _(buffer=buffer):
            buffer[...] = jnp.zeros_like(buffer)

    for buffer in (out_e, out_w, out_n, out_s):
        buffer[...] = jnp.zeros_like(buffer)

    def hessian_row(x, carry):
        for one in first_copies(x):
            one.wait()
        for first in range(0, tile_y, 16):
            value = own_ref[x, pl.ds(first, 16), :].astype(jnp.float32)
            put_wide(value, BOUND + x, BOUND + first)
        for layer in range(depth):
            lanes = pl.ds(layer * 512, 512)
            mask = mask_ref[x, :, lanes].astype(jnp.float32).astype(jnp.bfloat16)
            grads = [grad_ref[c, x, :, lanes] for c in range(3)]
            masked = [mask * g for g in grads]
            for c in range(3):
                grad_ref[c, x, :, lanes] = masked[c]
            for q, (c, d) in enumerate(PAIRS):
                part_ref[pl.ds(q * wide + layer * tile_y, tile_y), :] = masked[c] * grads[d]
        table = square_ref[...]
        for q in range(6):
            total = contract(table, part_ref[pl.ds(q * wide, wide), :])
            value = total[0:32] + total[32:64]
            for first in range(0, 32, 8):
                rows = pl.ds((q * 32 + first) * stride_x + x, 8, stride=stride_x)
                hess_ref[rows, :] = value[first : first + 8]
        return carry

    for one in small_copies:
        one.wait()
    extent = (tile_x, depth, tile_y)
    pos_x, layers, pos_y = [lax.broadcasted_iota(jnp.int32, extent, k) for k in range(3)]
    table = (pos_y + offset_ref[1] + BOUND) * stride_y
    table_ref[...] = table + (layers * span_x + pos_x + offset_ref[0] + BOUND) * 4
    table_copy = pltpu.make_async_copy(table_ref, source_ref, local_sems.at[5, 3])
    table_copy.start()
    lax.fori_loop(0, tile_x, hessian_row, 0)
    table_copy.wait()
    arrive(y_copies())

    def convert(i, carry):
        put_sides(BOUND + i, gx >= 0)
        return carry

    lax.fori_loop(0, tile_x, convert, 0)
    head = tile_x - 2 * BOUND - 1

    def load_row(turn, carry):
        @pl.when(both(turn >= head - BOUND - 1, turn < head))
        def _():
            k = turn - (head - BOUND - 1)
            arrive(after_parts(k, edges))
            begin(after_corners(k))

        @pl.when(both(turn >= head - BOUND, turn < head))
        def _():
            k = head - 1 - turn
            arrive(before_parts(k, edges))
            begin(before_corners(k))

        place = turn - head

        @pl.when(both(place >= 0, place % 2 == 0))
        def _():
            k = place // 2
            arrive(after_parts(k, rest) + after_corners(k))
            put_band(after_ref, k, BOUND + tile_x + k, not_last_x)

        @pl.when(both(place >= 0, place % 2 == 1))
        def _():
            k = BOUND - 1 - place // 2
            arrive(before_parts(k, rest) + before_corners(k))
            put_band(before_ref, k, k, not_first_x)

        x = row_of(turn, tile_x)
        for one in second_copies(x):
            one.wait()

        for y in range(tile_y):
            for layer in range(depth):
                row = source_ref[x, layer, y]
                fetched_ref[pl.ds(y * stride_f + layer * 8, 8), :] = wide_ref[pl.ds(row, 8), :]
        for layer in range(depth):
            for chunk in range(4):
                lanes = pl.ds(layer * 512 + chunk * 128, 128)
                part = pl.ds(chunk * 128, 128)
                near = fetched_ref[pl.ds(layer * 8 + chunk, tile_y, stride=stride_f), :]
                far = fetched_ref[pl.ds(layer * 8 + 4 + chunk, tile_y, stride=stride_f), :]
                weight = weight_ref[x, :, lanes].astype(jnp.float32)
                warped = weight * near + (1.0 - weight) * far
                image = image_ref[x, :, lanes].astype(jnp.float32) - warped
                image = image.astype(jnp.bfloat16).astype(jnp.float32)
                for c in range(3):
                    rows = pl.ds(c * wide + layer * tile_y, tile_y)
                    value = image * grad_ref[c, x, :, lanes].astype(jnp.float32)
                    high = value.astype(jnp.bfloat16)
                    high_ref[rows, part] = high
                    low_ref[rows, part] = (value - high.astype(jnp.float32)).astype(jnp.bfloat16)
        table = shape_ref[...]
        for c in range(3):
            rows = pl.ds(c * wide, wide)
            total = contract(table, high_ref[rows, :]) + contract(table, low_ref[rows, :])
            load_ref[pl.ds(c * 8 * stride_x + x, 8, stride=stride_x), :] = total[0:8] + total[8:16]
        return carry

    lax.fori_loop(0, tile_x, load_row, 0)

    width = wide
    lane = lax.broadcasted_iota(jnp.int32, (tile_x, width), 1)
    row = lax.broadcasted_iota(jnp.int32, (tile_x, width), 0)
    in_tile = lane % tile_y
    first_y = in_tile == 0
    last_y = in_tile == tile_y - 1
    first_x = row == 0
    last_x = row == tile_x - 1
    topmost = lane >= width - tile_y
    above = lane >= tile_y
    first_8, last_8 = (first_y[0:8], last_y[0:8])
    turn_y = tile_y - 1
    body, tail = (pl.ds(0, tile_x), pl.ds(tile_x, 8))
    upper, lower = (pl.ds(0, 8), pl.ds(8, 8))

    def roll(value, shift, axis):
        return pltpu.roll(value, shift % value.shape[axis], axis)

    def shift_x(value):
        return jnp.where(first_x, 0.0, roll(value, 1, 0))

    def copies(phase):
        table = [
            (out_e, lower, in_sw, 1, 1),
            (out_e, None, in_w, 1, 0),
            (out_n, None, in_s, 0, 1),
            (out_w, upper, in_ne, -1, -1),
            (out_e, upper, in_nw, 1, -1),
            (out_w, lower, in_se, -1, 1),
            (out_w, None, in_e, -1, 0),
            (out_s, None, in_n, 0, -1),
        ]
        if phase == PHASES - 1:
            table = table[:3]
        far, near = ([], [])
        for k, (src, rows, dst, dx, dy) in enumerate(table):
            send_ok, recv_ok = (gx >= 0, gx >= 0)
            if dx:
                send_ok = not_last_x if dx > 0 else not_first_x
                recv_ok = not_first_x if dx > 0 else not_last_x
            if dy:
                send_ok = both(send_ok, not_last_y if dy > 0 else not_first_y)
                recv_ok = both(recv_ok, not_first_y if dy > 0 else not_last_y)
            source = src.at[phase] if rows is None else src.at[phase, rows]
            one = remote(
                source,
                dst.at[phase],
                send_sems.at[phase, k],
                recv_sems.at[phase, k],
                (gx + dx, gy + dy),
            )
            (far if dx else near).append((one, send_ok, recv_ok))
        return (far, near)

    def assemble(phase, partial, meanwhile):
        folded = {}
        for i in range(2):
            for j in range(2):
                found = []
                for c in range(3):
                    under = partial((4 * i + 2 * j) * 3 + c)
                    over = partial((4 * i + 2 * j + 1) * 3 + c)
                    found.append(under + jnp.where(above, roll(over, tile_y, 1), 0.0))
                    folded[i, j, 3 + c] = jnp.where(topmost, over, 0.0)
                for c in range(3):
                    folded[i, j, c] = found[c]
        total, right, edge_x, edge_c = ([], [], [], [])
        for a in range(6):
            kept = [
                folded[i, 0, a] + jnp.where(first_y, 0.0, roll(folded[i, 1, a], 1, 1))
                for i in range(2)
            ]
            total.append(kept[0] + shift_x(kept[1]))
            right.append(folded[0, 1, a] + shift_x(folded[1, 1, a]))
            edge_x.append(kept[1][tile_x - 1 :])
            edge_c.append(folded[1, 1, a][tile_x - 1 :])
            out_e[phase, a : a + 1, :] = edge_x[a]
            out_e[phase, 8 + a : 9 + a, :] = edge_c[a]
            out_w[phase, a : a + 1, :] = total[a][0:1]
            out_w[phase, 8 + a : 9 + a, :] = right[a][0:1]
        far, near = copies(phase)
        begin(far)
        north = jnp.zeros((tile_x, width), jnp.float32)
        south = jnp.zeros((tile_x, width), jnp.float32)
        for a in range(6):
            north = jnp.where(in_tile == a, roll(right[a], a + 1, 1), north)
            south = jnp.where(in_tile == a, roll(total[a], a, 1), south)
            out_n[phase, tile_x + a : tile_x + a + 1, :] = edge_c[a]
            out_s[phase, tile_x + a : tile_x + a + 1, :] = edge_x[a]
        out_n[phase, body, :] = north
        out_s[phase, body, :] = south
        begin(near)
        meanwhile()
        arrive(near)
        from_s = in_s[phase, body, :]
        whole = [
            total[a] + jnp.where(first_y, roll(from_s, -(tile_y + a), 1), 0.0) for a in range(6)
        ]
        if phase < PHASES - 1:
            from_n = in_n[phase, body, :]
            right = [right[a] + roll(from_n, turn_y - a, 1) for a in range(6)]
        arrive(far)
        line = in_w[phase, upper, :] + jnp.where(
            first_8, roll(in_sw[phase], -turn_y, 1), 0.0
        )
        whole = [
            whole[a] + jnp.where(first_x, line[a : a + 1], 0.0)
            for a in range(6)
        ]
        if phase == PHASES - 1:
            return whole
        side_x = in_s[phase, tail, :] + in_se[phase]
        side_x = jnp.where(first_8, roll(side_x, -turn_y, 1), 0.0)
        side_x = jnp.where(not_last_x, out_e[phase, upper, :] + in_e[phase, upper, :] + side_x, 0.0)
        line = in_w[phase, lower, :] + roll(in_nw[phase], turn_y, 1)
        corner = in_n[phase, tail, :] + in_ne[phase]
        corner = out_e[phase, lower, :] + in_e[phase, lower, :] + roll(corner, turn_y, 1)
        corner = jnp.where(both(not_last_x, not_last_y), corner, 0.0)
        corner = jnp.where(last_8, corner, roll(side_x, -1, 1))
        for a in range(6):
            side = right[a] + jnp.where(first_x, line[a : a + 1], 0.0)
            side = jnp.where(not_last_y, side, 0.0)
            next_x = jnp.where(last_x, side_x[a : a + 1], roll(whole[a], -1, 0))
            next_y = jnp.where(last_y, side, roll(whole[a], -1, 1))
            next_c = jnp.where(last_x, corner[a : a + 1], roll(next_y, -1, 0))
            for k, value in enumerate((whole[a], next_y, next_x, next_c)):
                if a < 3:
                    field_ref[6 * k + a] = value
                    field_ref[6 * k + 3 + a] = roll(value, -tile_y, 1)
                else:
                    above_it = field_ref[6 * k + a]
                    field_ref[6 * k + a] = jnp.where(topmost, value, above_it)
        return whole

    def apply():
        for half in range(0, tile_x, 8):
            rows = pl.ds(half, 8)
            fields = [field_ref[k, rows, :] for k in range(24)]
            for n, (i, j, l) in enumerate(NODES):
                for c in range(3):
                    total = None
                    for m, (p, q, r) in enumerate(NODES):
                        kind = (i + p) * 9 + (j + q) * 3 + l + r
                        for d in range(3):
                            index = (PAIR_OF[c, d] * 32 + kind) * stride_x + half
                            term = hess_ref[pl.ds(index, 8), :] * fields[3 * m + d]
                            total = term if total is None else total + term
                    value_ref[3 * n + c, rows, :] = total

    def everyone():
        place = gx * n_gy + gy
        found = []
        for k in range(1, n_gx * n_gy):
            other = (place + k) % (n_gx * n_gy)
            found.append(
                remote(
                    own_x,
                    got_x.at[k - 1],
                    send_x.at[k - 1],
                    recv_x.at[k - 1],
                    (other // n_gy, other % n_gy),
                )
            )
        return found

    def gather(found, own, got, count):
        for one in found:
            one.wait_recv()
        total = own[...]
        for k in range(1, count):
            total = total + got[k - 1]
        return total

    def inner(left, right):
        total = left[0] * right[0]
        for one, other in zip(left[1:], right[1:]):
            total = total + one * other
        return jnp.sum(total, axis=0, keepdims=True)

    def nothing():
        return None

    def load_part(k):
        start = ((k % 3) * 8 + k // 3) * stride_x
        return load_ref[pl.ds(start, tile_x), :]

    def value_part(k):
        return value_ref[k]

    base = [assemble(0, load_part, nothing)]
    for phase in range(1, ITERS):
        apply()
        base.append(assemble(phase, value_part, nothing))
    apply()
    last = inner([field_ref[k] for k in range(24)], [value_ref[k] for k in range(24)])
    rows = [
        inner(base[0], base[0]),
        inner(base[0], base[1]),
        inner(base[1], base[1]),
        inner(base[1], base[2]),
        inner(base[2], base[2]),
        last,
    ]
    spot = lane[0:1]
    packed = jnp.zeros((1, width), jnp.float32)
    for k in range(6):
        packed = jnp.where(spot == k, jnp.sum(rows[k], axis=1, keepdims=True), packed)
    own_x[...] = packed
    for one in everyone():
        one.start()

    base.append(assemble(ITERS, value_part, nothing))
    sums = gather(everyone(), own_x, got_x, n_gx * n_gy)
    h = [sums[:, k : k + 1] for k in range(6)]
    sigma = tikhonov / UNIT
    a0 = h[1] / h[0]
    n1 = h[2] - a0 * h[1]
    a1 = (h[3] - 2.0 * a0 * h[2] + a0 * a0 * h[1]) / n1
    s = a0 + a1
    q = a0 * a1 - n1 / h[0]
    n2 = h[4] - s * h[3] + q * h[2]
    a2 = (h[5] - s * h[4] + q * h[3] - s * n2) / n2
    b2 = n2 / n1
    p2 = -(s + a2)
    p1 = q + a2 * s - b2
    p0 = b2 * a0 - a2 * q
    scale = 1.0 / (sigma * (sigma * (p2 - sigma) - p1) + p0)
    r2, r1, r0 = (p2 * scale, p1 * scale, p0 * scale)
    turn_back = -scale / UNIT
    i1 = (p2 - sigma) * turn_back
    i0 = (p1 - sigma * p2 + sigma * sigma) * turn_back
    for a in range(6):
        inc = turn_back * base[2][a] + i1 * base[1][a] + i0 * base[0][a]
        res = scale * base[3][a] + r2 * base[2][a] + r1 * base[1][a] + r0 * base[0][a]
        out_ref[a] = inc
        out_ref[6 + a] = res
    for phase in range(PHASES):
        for group in copies(phase):
            sent(group)
    for one in everyone():
        one.wait_send()
    sent(y_copies())
    for k in range(BOUND + 1):
        sent(after_parts(k, whole_row) + after_corners(k))
    for k in range(BOUND):
        sent(before_parts(k, whole_row) + before_corners(k))


def format_kernel(depth, value_ref, inc_ref, res_ref):
    tile_y = inc_ref.shape[3]
    width = value_ref.shape[2]
    for out, first in ((inc_ref, 0), (res_ref, 6)):
        for c in range(3):
            value = value_ref[first + c]
            for layer in range(depth):
                out[c, layer] = value[:, layer * tile_y : (layer + 1) * tile_y]
            out[c, depth] = value_ref[first + 3 + c][:, width - tile_y :]


def per_device(
    reference_scan, ref_gradient, deformed_scan, interp_weights, sample_mask, block_list, offsets
):
    tile_x, tile_y, column = reference_scan.shape
    depth = column // 512
    width = depth * tile_y
    square_table, shape_table = tables()
    n_gx, n_gy = (lax.axis_size("gx"), lax.axis_size("gy"))
    span_x, span_y = (tile_x + 2 * BOUND + 1, tile_y + 2 * BOUND)
    f32, bf16, vmem, dma = (jnp.float32, jnp.bfloat16, pltpu.VMEM, pltpu.SemaphoreType.DMA)
    part = jax.ShapeDtypeStruct((3, depth + 1, tile_x, tile_y), f32)
    halos = 2 + 5 * (2 * BOUND + 1)
    whole = pl.BlockSpec(memory_space=pltpu.VMEM)
    anywhere = pl.BlockSpec(memory_space=pl.ANY)
    packed = pl.pallas_call(
        functools.partial(step_kernel, (n_gx, n_gy), tile_x, tile_y, depth),
        out_shape=vmem((12, tile_x, width), f32),
        in_specs=[anywhere] * 8,
        out_specs=whole,
        scratch_shapes=[
            vmem((3, tile_x, tile_y, column), bf16),
            vmem((tile_x, tile_y, column), jnp.int32),
            vmem((tile_x, tile_y, column), bf16),
            vmem((tile_x, tile_y, column), bf16),
            vmem((tile_x, tile_y, column), bf16),
            vmem((BOUND, tile_y, column), bf16),
            vmem((BOUND + 1, tile_y, column), bf16),
            vmem((span_x, EDGE, column), bf16),
            vmem((span_x, EDGE, column), bf16),
            vmem(((span_y + 1) * spread_stride(depth * span_x * 4), 128), f32),
            vmem((6 * width, 512), bf16),
            vmem(((tile_y + 1) * spread_stride(8 * depth), 128), f32),
            vmem((3 * width, 512), bf16),
            vmem((3 * width, 512), bf16),
            vmem(((6 * 32 + 1) * spread_stride(tile_x), width), f32),
            vmem(((3 * 8 + 1) * spread_stride(tile_x), width), f32),
            vmem((24, tile_x, width), f32),
            vmem((24, tile_x, width), f32),
        ]
        + [
            vmem((PHASES, rows, width), f32)
            for rows in (16, 16, tile_x + 8, tile_x + 8) * 2 + (8, 8, 8, 8)
        ]
        + [
            vmem((1, width), f32),
            vmem((n_gx * n_gy - 1, 1, width), f32),
            vmem((2, tile_x, depth, tile_y), jnp.int32),
            vmem(square_table.shape, bf16),
            vmem(shape_table.shape, bf16),
            vmem((tile_x, depth, tile_y), jnp.int32),
            pltpu.SMEM((tile_x, depth, tile_y), jnp.int32),
            dma((6, tile_x)),
            dma((halos,)),
            dma((halos,)),
            dma((PHASES, 8)),
            dma((PHASES, 8)),
            dma((n_gx * n_gy - 1,)),
            dma((n_gx * n_gy - 1,)),
        ],
        compiler_params=pltpu.CompilerParams(collective_id=0, has_side_effects=True),
        name="step",
    )(
        jnp.transpose(offsets, (0, 1, 3, 2)),
        jnp.asarray(square_table),
        jnp.asarray(shape_table),
        ref_gradient,
        sample_mask,
        deformed_scan,
        reference_scan,
        interp_weights,
    )
    increment, residual = pl.pallas_call(
        functools.partial(format_kernel, depth),
        out_shape=(part, part),
        in_specs=[whole],
        out_specs=(whole, whole),
        compiler_params=pltpu.CompilerParams(vmem_limit_bytes=2**21),
        name="format",
    )(packed)

    def nodal(value):
        return jnp.transpose(value, (0, 2, 3, 1))

    return (nodal(increment), nodal(residual))


def solution(mesh):
    return jax.shard_map(
        per_device,
        mesh=mesh,
        in_specs=(
            P("gx", "gy", None),
            P(None, "gx", "gy", None),
            P("gx", "gy", None),
            P("gx", "gy", None),
            P("gx", "gy", None),
            P("gx", "gy"),
            P(None, "gx", "gy", None),
        ),
        out_specs=(P(None, "gx", "gy", None), P(None, "gx", "gy", None)),
        check_vma=False,
    )
```

```python
import functools

import jax
import jax.numpy as jnp
import ml_dtypes
import numpy as np
from jax import lax
from jax.experimental import pallas as pl
from jax.experimental.pallas import tpu as pltpu
from jax.sharding import PartitionSpec as P

BOUND = 4
ITERS = 3
PHASES = ITERS + 1
EDGE = 8

tikhonov = 8.0
UNIT = 64.0

NODES = [(n >> 2 & 1, n >> 1 & 1, n & 1) for n in range(8)]
PAIRS = [(c, d) for c in range(3) for d in range(c, 3)]
PAIR_OF = {(c, d): PAIRS.index((min(c, d), max(c, d))) for c in range(3) for d in range(3)}
MESH = pl.DeviceIdType.MESH


def split(table, count):
    parts = []
    for _ in range(count):
        part = table.astype(ml_dtypes.bfloat16)
        parts.append(part)
        table = table - part.astype(np.float32)
    return parts


def tables():
    voxel = np.arange(512)
    coords = [
        ((voxel // 64).astype(np.float32) + np.float32(0.5)) / np.float32(8.0),
        ((voxel // 8 % 8).astype(np.float32) + np.float32(0.5)) / np.float32(8.0),
        ((voxel % 8).astype(np.float32) + np.float32(0.5)) / np.float32(8.0),
    ]
    linear = [[np.float32(1.0) - t, t] for t in coords]
    quad = [[s[0] * s[0], s[0] * s[1], s[1] * s[1]] for s in linear]
    shapes = np.stack([linear[0][i] * linear[1][j] * linear[2][l] for i, j, l in NODES])
    squares = np.stack(
        [quad[0][a] * quad[1][b] * quad[2][c] for a in range(3) for b in range(3) for c in range(3)]
    )
    squares = np.pad(squares, ((0, 5), (0, 0))) / np.float32(UNIT)
    square_table = np.concatenate(split(squares.astype(np.float32), 2), axis=0)
    shape_table = np.concatenate(split(shapes.astype(np.float32), 2), axis=0)
    return (square_table, shape_table)


def spread_stride(rows):
    return rows + 4 if rows % 8 == 0 else rows


def contract(table, part):
    return lax.dot_general(
        table, part, (((1,), (1,)), ((), ())), preferred_element_type=jnp.float32
    )


def row_of(turn, tile_x):
    place = turn - (tile_x - 2 * BOUND - 1)
    upper = tile_x - BOUND - 1 + place // 2
    edge = jnp.where(place % 2 == 0, upper, BOUND - 1 - place // 2)
    return jnp.where(place < 0, turn + BOUND, edge)


def step_kernel(
    sizes,
    tile_x,
    tile_y,
    depth,
    offset_hbm,
    square_hbm,
    shape_hbm,
    grad_hbm,
    mask_hbm,
    scan_ref,
    image_hbm,
    weight_hbm,
    out_ref,
    grad_ref,
    mask_ref,
    own_ref,
    image_ref,
    weight_ref,
    before_ref,
    after_ref,
    beyond_ref,
    ahead_ref,
    wide_ref,
    part_ref,
    fetched_ref,
    high_ref,
    low_ref,
    hess_ref,
    load_ref,
    field_ref,
    value_ref,
    out_e,
    out_w,
    out_n,
    out_s,
    in_w,
    in_e,
    in_s,
    in_n,
    in_sw,
    in_ne,
    in_nw,
    in_se,
    own_x,
    got_x,
    offset_ref,
    square_ref,
    shape_ref,
    table_ref,
    source_ref,
    local_sems,
    halo_send,
    halo_recv,
    send_sems,
    recv_sems,
    send_x,
    recv_x,
):
    n_gx, n_gy = sizes
    gx = lax.axis_index("gx")
    gy = lax.axis_index("gy")
    not_first_x, not_last_x = (gx > 0, gx < n_gx - 1)
    not_first_y, not_last_y = (gy > 0, gy < n_gy - 1)
    both = jnp.logical_and
    wide = depth * tile_y
    span_x = tile_x + 2 * BOUND + 1
    stride_y = spread_stride(depth * span_x * 4)
    stride_x = spread_stride(tile_x)
    stride_f = spread_stride(8 * depth)

    def remote(source, target, sends, receives, device):
        return pltpu.make_async_remote_copy(
            src_ref=source,
            dst_ref=target,
            send_sem=sends,
            recv_sem=receives,
            device_id=device,
            device_id_type=MESH,
        )

    def halo(k, source, target, device):
        return remote(source, target, halo_send.at[k], halo_recv.at[k], device)

    every = slice(None)
    low_y, high_y = (pl.ds(0, EDGE), pl.ds(tile_y - EDGE, EDGE))
    near_y, far_y = ((gx, gy - 1), (gx, gy + 1))
    middle = pl.ds(BOUND, tile_x)

    def y_copies():
        return [
            (halo(0, scan_ref.at[every, low_y], beyond_ref.at[middle], near_y), not_first_y, not_last_y),
            (halo(1, scan_ref.at[every, high_y], ahead_ref.at[middle], far_y), not_last_y, not_first_y),
        ]

    inner_y = pl.ds(EDGE, tile_y - 2 * EDGE)
    bands = 2 * BOUND + 1

    def after_parts(k, parts):
        return [
            (
                halo(2 + 3 * k + p, scan_ref.at[k, cut], after_ref.at[k, cut], (gx - 1, gy)),
                not_first_x,
                not_last_x,
            )
            for p, cut in enumerate((low_y, high_y, inner_y))
            if p in parts
        ]

    def before_parts(k, parts):
        row = tile_x - BOUND + k
        first = 5 + 3 * BOUND + 3 * k
        return [
            (
                halo(first + p, scan_ref.at[row, cut], before_ref.at[k, cut], (gx + 1, gy)),
                not_last_x,
                not_first_x,
            )
            for p, cut in enumerate((low_y, high_y, inner_y))
            if p in parts
        ]

    edges, rest, whole_row = ((0, 1), (2,), (0, 1, 2))

    def corner_copies(first, band, k, row, present):
        return [
            (
                halo(first, band.at[k, low_y], beyond_ref.at[row], near_y),
                both(present, not_first_y),
                both(present, not_last_y),
            ),
            (
                halo(first + 1, band.at[k, high_y], ahead_ref.at[row], far_y),
                both(present, not_last_y),
                both(present, not_first_y),
            ),
        ]

    def after_corners(k):
        first = 2 + 3 * bands + 2 * k
        return corner_copies(first, after_ref, k, BOUND + tile_x + k, not_last_x)

    def before_corners(k):
        first = 4 + 3 * bands + 2 * BOUND + 2 * k
        return corner_copies(first, before_ref, k, k, not_first_x)

    def begin(copies):
        for one, sends, _ in copies:
            pl.when(sends)(one.start)

    def arrive(copies):
        for one, _, receives in copies:
            pl.when(receives)(one.wait_recv)

    def sent(copies):
        for one, sends, _ in copies:
            pl.when(sends)(one.wait_send)

    def put_wide(value, at_x, at_y):
        count = value.shape[0]
        for layer in range(depth):
            for chunk in range(4):
                lanes = slice(layer * 512 + chunk * 128, layer * 512 + chunk * 128 + 128)
                start = at_y * stride_y + (layer * span_x + at_x) * 4 + chunk
                wide_ref[pl.ds(start, count, stride=stride_y), :] = value[:, lanes]

    def put_sides(row, inside):
        value = beyond_ref[row].astype(jnp.float32)[0:BOUND]
        put_wide(jnp.where(both(inside, not_last_y), value, 0.0), row, BOUND + tile_y)
        value = ahead_ref[row].astype(jnp.float32)[EDGE - BOUND :]
        put_wide(jnp.where(both(inside, not_first_y), value, 0.0), row, 0)

    def put_band(band, k, row, inside):
        for first in range(0, tile_y, 16):
            value = band[k, pl.ds(first, 16), :].astype(jnp.float32)
            put_wide(jnp.where(inside, value, 0.0), row, BOUND + first)
        put_sides(row, inside)

    def first_copies(x):
        return [
            pltpu.make_async_copy(grad_hbm.at[:, x], grad_ref.at[:, x], local_sems.at[0, x]),
            pltpu.make_async_copy(mask_hbm.at[x], mask_ref.at[x], local_sems.at[1, x]),
            pltpu.make_async_copy(scan_ref.at[x], own_ref.at[x], local_sems.at[2, x]),
        ]

    def second_copies(x):
        return [
            pltpu.make_async_copy(image_hbm.at[x], image_ref.at[x], local_sems.at[3, x]),
            pltpu.make_async_copy(weight_hbm.at[x], weight_ref.at[x], local_sems.at[4, x]),
        ]

    def start_first(x, carry):
        for one in first_copies(x):
            one.start()
        return carry

    def start_second(turn, carry):
        for one in second_copies(row_of(turn, tile_x)):
            one.start()
        return carry

    barrier = pltpu.get_barrier_semaphore()
    there_x = {-1: not_first_x, 0: gx >= 0, 1: not_last_x}
    there_y = {-1: not_first_y, 0: gy >= 0, 1: not_last_y}

    for k in range(1, n_gx * n_gy):
        other = (gx * n_gy + gy + k) % (n_gx * n_gy)
        pl.semaphore_signal(
            barrier,
            inc=1,
            device_id=(other // n_gy, other % n_gy),
            device_id_type=MESH,
        )
    lax.fori_loop(0, 2, start_first, 0)
    small_copies = [
        pltpu.make_async_copy(one, other, local_sems.at[5, k])
        for k, (one, other) in enumerate(
            ((square_hbm, square_ref), (offset_hbm, offset_ref), (shape_hbm, shape_ref))
        )
    ]
    for one in small_copies:
        one.start()
    pl.semaphore_wait(barrier, n_gx * n_gy - 1)
    begin(y_copies())
    for parts in (edges, rest):
        for k in range(BOUND + 1):
            begin(after_parts(k, parts))
            if k < BOUND:
                begin(before_parts(BOUND - 1 - k, parts))
    lax.fori_loop(2, tile_x, start_first, 0)
    lax.fori_loop(0, tile_x, start_second, 0)
    for buffer, dx, dy in (
        (in_w, -1, 0),
        (in_e, 1, 0),
        (in_s, 0, -1),
        (in_n, 0, 1),
        (in_sw, -1, -1),
        (in_ne, 1, 1),
        (in_nw, -1, 1),
        (in_se, 1, -1),
    ):

        @pl.when(jnp.logical_not(both(there_x[dx], there_y[dy])))
        def _(buffer=buffer):
            buffer[...] = jnp.zeros_like(buffer)

    for buffer in (out_e, out_w, out_n, out_s):
        buffer[...] = jnp.zeros_like(buffer)

    def hessian_row(x, carry):
        for one in first_copies(x):
            one.wait()
        for first in range(0, tile_y, 16):
            value = own_ref[x, pl.ds(first, 16), :].astype(jnp.float32)
            put_wide(value, BOUND + x, BOUND + first)
        for layer in range(depth):
            lanes = pl.ds(layer * 512, 512)
            mask = mask_ref[x, :, lanes].astype(jnp.float32).astype(jnp.bfloat16)
            grads = [grad_ref[c, x, :, lanes] for c in range(3)]
            masked = [mask * g for g in grads]
            for c in range(3):
                grad_ref[c, x, :, lanes] = masked[c]
            for q, (c, d) in enumerate(PAIRS):
                part_ref[pl.ds(q * wide + layer * tile_y, tile_y), :] = masked[c] * grads[d]
        table = square_ref[...]
        for q in range(6):
            total = contract(table, part_ref[pl.ds(q * wide, wide), :])
            value = total[0:32] + total[32:64]
            for first in range(0, 32, 8):
                rows = pl.ds((q * 32 + first) * stride_x + x, 8, stride=stride_x)
                hess_ref[rows, :] = value[first : first + 8]
        return carry

    for one in small_copies:
        one.wait()
    extent = (tile_x, depth, tile_y)
    pos_x, layers, pos_y = [lax.broadcasted_iota(jnp.int32, extent, k) for k in range(3)]
    table = (pos_y + offset_ref[1] + BOUND) * stride_y
    table_ref[...] = table + (layers * span_x + pos_x + offset_ref[0] + BOUND) * 4
    table_copy = pltpu.make_async_copy(table_ref, source_ref, local_sems.at[5, 3])
    table_copy.start()
    lax.fori_loop(0, tile_x, hessian_row, 0)
    table_copy.wait()
    arrive(y_copies())

    def convert(i, carry):
        put_sides(BOUND + i, gx >= 0)
        return carry

    lax.fori_loop(0, tile_x, convert, 0)
    head = tile_x - 2 * BOUND - 1

    def load_row(turn, carry):
        @pl.when(both(turn >= head - BOUND - 1, turn < head))
        def _():
            k = turn - (head - BOUND - 1)
            arrive(after_parts(k, edges))
            begin(after_corners(k))

        @pl.when(both(turn >= head - BOUND, turn < head))
        def _():
            k = head - 1 - turn
            arrive(before_parts(k, edges))
            begin(before_corners(k))

        place = turn - head

        @pl.when(both(place >= 0, place % 2 == 0))
        def _():
            k = place // 2
            arrive(after_parts(k, rest) + after_corners(k))
            put_band(after_ref, k, BOUND + tile_x + k, not_last_x)

        @pl.when(both(place >= 0, place % 2 == 1))
        def _():
            k = BOUND - 1 - place // 2
            arrive(before_parts(k, rest) + before_corners(k))
            put_band(before_ref, k, k, not_first_x)

        x = row_of(turn, tile_x)
        for one in second_copies(x):
            one.wait()

        for y in range(tile_y):
            for layer in range(depth):
                row = source_ref[x, layer, y]
                fetched_ref[pl.ds(y * stride_f + layer * 8, 8), :] = wide_ref[pl.ds(row, 8), :]
        for layer in range(depth):
            for chunk in range(4):
                lanes = pl.ds(layer * 512 + chunk * 128, 128)
                part = pl.ds(chunk * 128, 128)
                near = fetched_ref[pl.ds(layer * 8 + chunk, tile_y, stride=stride_f), :]
                far = fetched_ref[pl.ds(layer * 8 + 4 + chunk, tile_y, stride=stride_f), :]
                weight = weight_ref[x, :, lanes].astype(jnp.float32)
                warped = weight * near + (1.0 - weight) * far
                image = image_ref[x, :, lanes].astype(jnp.float32) - warped
                image = image.astype(jnp.bfloat16).astype(jnp.float32)
                for c in range(3):
                    rows = pl.ds(c * wide + layer * tile_y, tile_y)
                    value = image * grad_ref[c, x, :, lanes].astype(jnp.float32)
                    high = value.astype(jnp.bfloat16)
                    high_ref[rows, part] = high
                    low_ref[rows, part] = (value - high.astype(jnp.float32)).astype(jnp.bfloat16)
        table = shape_ref[...]
        for c in range(3):
            rows = pl.ds(c * wide, wide)
            total = contract(table, high_ref[rows, :]) + contract(table, low_ref[rows, :])
            load_ref[pl.ds(c * 8 * stride_x + x, 8, stride=stride_x), :] = total[0:8] + total[8:16]
        return carry

    lax.fori_loop(0, tile_x, load_row, 0)

    width = wide
    lane = lax.broadcasted_iota(jnp.int32, (tile_x, width), 1)
    row = lax.broadcasted_iota(jnp.int32, (tile_x, width), 0)
    in_tile = lane % tile_y
    first_y = in_tile == 0
    last_y = in_tile == tile_y - 1
    first_x = row == 0
    last_x = row == tile_x - 1
    topmost = lane >= width - tile_y
    above = lane >= tile_y
    first_8, last_8 = (first_y[0:8], last_y[0:8])
    turn_y = tile_y - 1
    body, tail = (pl.ds(0, tile_x), pl.ds(tile_x, 8))
    upper, lower = (pl.ds(0, 8), pl.ds(8, 8))

    def roll(value, shift, axis):
        return pltpu.roll(value, shift % value.shape[axis], axis)

    def shift_x(value):
        return jnp.where(first_x, 0.0, roll(value, 1, 0))

    def copies(phase):
        table = [
            (out_e, lower, in_sw, 1, 1),
            (out_e, None, in_w, 1, 0),
            (out_n, None, in_s, 0, 1),
            (out_w, upper, in_ne, -1, -1),
            (out_e, upper, in_nw, 1, -1),
            (out_w, lower, in_se, -1, 1),
            (out_w, None, in_e, -1, 0),
            (out_s, None, in_n, 0, -1),
        ]
        if phase == PHASES - 1:
            table = table[:3]
        far, near = ([], [])
        for k, (src, rows, dst, dx, dy) in enumerate(table):
            send_ok, recv_ok = (gx >= 0, gx >= 0)
            if dx:
                send_ok = not_last_x if dx > 0 else not_first_x
                recv_ok = not_first_x if dx > 0 else not_last_x
            if dy:
                send_ok = both(send_ok, not_last_y if dy > 0 else not_first_y)
                recv_ok = both(recv_ok, not_first_y if dy > 0 else not_last_y)
            source = src.at[phase] if rows is None else src.at[phase, rows]
            one = remote(
                source,
                dst.at[phase],
                send_sems.at[phase, k],
                recv_sems.at[phase, k],
                (gx + dx, gy + dy),
            )
            (far if dx else near).append((one, send_ok, recv_ok))
        return (far, near)

    def assemble(phase, partial, meanwhile):
        folded = {}
        for i in range(2):
            for j in range(2):
                found = []
                for c in range(3):
                    under = partial((4 * i + 2 * j) * 3 + c)
                    over = partial((4 * i + 2 * j + 1) * 3 + c)
                    found.append(under + jnp.where(above, roll(over, tile_y, 1), 0.0))
                    folded[i, j, 3 + c] = jnp.where(topmost, over, 0.0)
                for c in range(3):
                    folded[i, j, c] = found[c]
        total, right, edge_x, edge_c = ([], [], [], [])
        for a in range(6):
            kept = [
                folded[i, 0, a] + jnp.where(first_y, 0.0, roll(folded[i, 1, a], 1, 1))
                for i in range(2)
            ]
            total.append(kept[0] + shift_x(kept[1]))
            right.append(folded[0, 1, a] + shift_x(folded[1, 1, a]))
            edge_x.append(kept[1][tile_x - 1 :])
            edge_c.append(folded[1, 1, a][tile_x - 1 :])
            out_e[phase, a : a + 1, :] = edge_x[a]
            out_e[phase, 8 + a : 9 + a, :] = edge_c[a]
            out_w[phase, a : a + 1, :] = total[a][0:1]
            out_w[phase, 8 + a : 9 + a, :] = right[a][0:1]
        far, near = copies(phase)
        begin(far)
        north = jnp.zeros((tile_x, width), jnp.float32)
        south = jnp.zeros((tile_x, width), jnp.float32)
        for a in range(6):
            north = jnp.where(in_tile == a, roll(right[a], a + 1, 1), north)
            south = jnp.where(in_tile == a, roll(total[a], a, 1), south)
            out_n[phase, tile_x + a : tile_x + a + 1, :] = edge_c[a]
            out_s[phase, tile_x + a : tile_x + a + 1, :] = edge_x[a]
        out_n[phase, body, :] = north
        out_s[phase, body, :] = south
        begin(near)
        meanwhile()
        arrive(near)
        from_s = in_s[phase, body, :]
        whole = [
            total[a] + jnp.where(first_y, roll(from_s, -(tile_y + a), 1), 0.0) for a in range(6)
        ]
        if phase < PHASES - 1:
            from_n = in_n[phase, body, :]
            right = [right[a] + roll(from_n, turn_y - a, 1) for a in range(6)]
        arrive(far)
        line = in_w[phase, upper, :] + jnp.where(
            first_8, roll(in_sw[phase], -turn_y, 1), 0.0
        )
        whole = [
            whole[a] + jnp.where(first_x, line[a : a + 1], 0.0)
            for a in range(6)
        ]
        if phase == PHASES - 1:
            return whole
        side_x = in_s[phase, tail, :] + in_se[phase]
        side_x = jnp.where(first_8, roll(side_x, -turn_y, 1), 0.0)
        side_x = jnp.where(not_last_x, out_e[phase, upper, :] + in_e[phase, upper, :] + side_x, 0.0)
        line = in_w[phase, lower, :] + roll(in_nw[phase], turn_y, 1)
        corner = in_n[phase, tail, :] + in_ne[phase]
        corner = out_e[phase, lower, :] + in_e[phase, lower, :] + roll(corner, turn_y, 1)
        corner = jnp.where(both(not_last_x, not_last_y), corner, 0.0)
        corner = jnp.where(last_8, corner, roll(side_x, -1, 1))
        for a in range(6):
            side = right[a] + jnp.where(first_x, line[a : a + 1], 0.0)
            side = jnp.where(not_last_y, side, 0.0)
            next_x = jnp.where(last_x, side_x[a : a + 1], roll(whole[a], -1, 0))
            next_y = jnp.where(last_y, side, roll(whole[a], -1, 1))
            next_c = jnp.where(last_x, corner[a : a + 1], roll(next_y, -1, 0))
            for k, value in enumerate((whole[a], next_y, next_x, next_c)):
                if a < 3:
                    field_ref[6 * k + a] = value
                    field_ref[6 * k + 3 + a] = roll(value, -tile_y, 1)
                else:
                    above_it = field_ref[6 * k + a]
                    field_ref[6 * k + a] = jnp.where(topmost, value, above_it)
        return whole

    def apply():
        for half in range(0, tile_x, 8):
            rows = pl.ds(half, 8)
            fields = [field_ref[k, rows, :] for k in range(24)]
            for n, (i, j, l) in enumerate(NODES):
                for c in range(3):
                    total = None
                    for m, (p, q, r) in enumerate(NODES):
                        kind = (i + p) * 9 + (j + q) * 3 + l + r
                        for d in range(3):
                            index = (PAIR_OF[c, d] * 32 + kind) * stride_x + half
                            term = hess_ref[pl.ds(index, 8), :] * fields[3 * m + d]
                            total = term if total is None else total + term
                    value_ref[3 * n + c, rows, :] = total

    def everyone():
        place = gx * n_gy + gy
        found = []
        count = n_gx * n_gy
        for k in sorted(range(1, count), key=lambda k: min(k, count - k)):
            other = (place + k) % count
            found.append(
                remote(
                    own_x,
                    got_x.at[k - 1],
                    send_x.at[k - 1],
                    recv_x.at[k - 1],
                    (other // n_gy, other % n_gy),
                )
            )
        return found

    def gather(found, own, got, count):
        for one in found:
            one.wait_recv()
        total = own[...]
        for k in range(1, count):
            total = total + got[k - 1]
        return total

    def inner(left, right):
        total = left[0] * right[0]
        for one, other in zip(left[1:], right[1:]):
            total = total + one * other
        return jnp.sum(total, axis=0, keepdims=True)

    def nothing():
        return None

    def load_part(k):
        start = ((k % 3) * 8 + k // 3) * stride_x
        return load_ref[pl.ds(start, tile_x), :]

    def value_part(k):
        return value_ref[k]

    base = [assemble(0, load_part, nothing)]
    for phase in range(1, ITERS):
        apply()
        base.append(assemble(phase, value_part, nothing))
    apply()
    last = inner([field_ref[k] for k in range(24)], [value_ref[k] for k in range(24)])
    rows = [
        inner(base[0], base[0]),
        inner(base[0], base[1]),
        inner(base[1], base[1]),
        inner(base[1], base[2]),
        inner(base[2], base[2]),
        last,
    ]
    spot = lane[0:1]
    packed = jnp.zeros((1, width), jnp.float32)
    for k in range(6):
        packed = jnp.where(spot == k, jnp.sum(rows[k], axis=1, keepdims=True), packed)
    own_x[...] = packed
    for one in everyone():
        one.start()

    base.append(assemble(ITERS, value_part, nothing))
    sums = gather(everyone(), own_x, got_x, n_gx * n_gy)
    h = [sums[:, k : k + 1] for k in range(6)]
    sigma = tikhonov / UNIT
    a0 = h[1] / h[0]
    n1 = h[2] - a0 * h[1]
    a1 = (h[3] - 2.0 * a0 * h[2] + a0 * a0 * h[1]) / n1
    s = a0 + a1
    q = a0 * a1 - n1 / h[0]
    n2 = h[4] - s * h[3] + q * h[2]
    a2 = (h[5] - s * h[4] + q * h[3] - s * n2) / n2
    b2 = n2 / n1
    p2 = -(s + a2)
    p1 = q + a2 * s - b2
    p0 = b2 * a0 - a2 * q
    scale = 1.0 / (sigma * (sigma * (p2 - sigma) - p1) + p0)
    r2, r1, r0 = (p2 * scale, p1 * scale, p0 * scale)
    turn_back = -scale / UNIT
    i1 = (p2 - sigma) * turn_back
    i0 = (p1 - sigma * p2 + sigma * sigma) * turn_back
    for a in range(6):
        inc = turn_back * base[2][a] + i1 * base[1][a] + i0 * base[0][a]
        res = scale * base[3][a] + r2 * base[2][a] + r1 * base[1][a] + r0 * base[0][a]
        out_ref[a] = inc
        out_ref[6 + a] = res
    for phase in range(PHASES):
        for group in copies(phase):
            sent(group)
    for one in everyone():
        one.wait_send()
    sent(y_copies())
    for k in range(BOUND + 1):
        sent(after_parts(k, whole_row) + after_corners(k))
    for k in range(BOUND):
        sent(before_parts(k, whole_row) + before_corners(k))


def format_kernel(depth, value_ref, inc_ref, res_ref):
    tile_y = inc_ref.shape[3]
    width = value_ref.shape[2]
    for out, first in ((inc_ref, 0), (res_ref, 6)):
        for c in range(3):
            value = value_ref[first + c]
            for layer in range(depth):
                out[c, layer] = value[:, layer * tile_y : (layer + 1) * tile_y]
            out[c, depth] = value_ref[first + 3 + c][:, width - tile_y :]


def per_device(
    reference_scan, ref_gradient, deformed_scan, interp_weights, sample_mask, block_list, offsets
):
    tile_x, tile_y, column = reference_scan.shape
    depth = column // 512
    width = depth * tile_y
    square_table, shape_table = tables()
    n_gx, n_gy = (lax.axis_size("gx"), lax.axis_size("gy"))
    span_x, span_y = (tile_x + 2 * BOUND + 1, tile_y + 2 * BOUND)
    f32, bf16, vmem, dma = (jnp.float32, jnp.bfloat16, pltpu.VMEM, pltpu.SemaphoreType.DMA)
    part = jax.ShapeDtypeStruct((3, depth + 1, tile_x, tile_y), f32)
    halos = 2 + 5 * (2 * BOUND + 1)
    whole = pl.BlockSpec(memory_space=pltpu.VMEM)
    anywhere = pl.BlockSpec(memory_space=pl.ANY)
    packed = pl.pallas_call(
        functools.partial(step_kernel, (n_gx, n_gy), tile_x, tile_y, depth),
        out_shape=vmem((12, tile_x, width), f32),
        in_specs=[anywhere] * 8,
        out_specs=whole,
        scratch_shapes=[
            vmem((3, tile_x, tile_y, column), bf16),
            vmem((tile_x, tile_y, column), jnp.int32),
            vmem((tile_x, tile_y, column), bf16),
            vmem((tile_x, tile_y, column), bf16),
            vmem((tile_x, tile_y, column), bf16),
            vmem((BOUND, tile_y, column), bf16),
            vmem((BOUND + 1, tile_y, column), bf16),
            vmem((span_x, EDGE, column), bf16),
            vmem((span_x, EDGE, column), bf16),
            vmem(((span_y + 1) * spread_stride(depth * span_x * 4), 128), f32),
            vmem((6 * width, 512), bf16),
            vmem(((tile_y + 1) * spread_stride(8 * depth), 128), f32),
            vmem((3 * width, 512), bf16),
            vmem((3 * width, 512), bf16),
            vmem(((6 * 32 + 1) * spread_stride(tile_x), width), f32),
            vmem(((3 * 8 + 1) * spread_stride(tile_x), width), f32),
            vmem((24, tile_x, width), f32),
            vmem((24, tile_x, width), f32),
        ]
        + [
            vmem((PHASES, rows, width), f32)
            for rows in (16, 16, tile_x + 8, tile_x + 8) * 2 + (8, 8, 8, 8)
        ]
        + [
            vmem((1, width), f32),
            vmem((n_gx * n_gy - 1, 1, width), f32),
            vmem((2, tile_x, depth, tile_y), jnp.int32),
            vmem(square_table.shape, bf16),
            vmem(shape_table.shape, bf16),
            vmem((tile_x, depth, tile_y), jnp.int32),
            pltpu.SMEM((tile_x, depth, tile_y), jnp.int32),
            dma((6, tile_x)),
            dma((halos,)),
            dma((halos,)),
            dma((PHASES, 8)),
            dma((PHASES, 8)),
            dma((n_gx * n_gy - 1,)),
            dma((n_gx * n_gy - 1,)),
        ],
        compiler_params=pltpu.CompilerParams(collective_id=0, has_side_effects=True),
        name="step",
    )(
        jnp.transpose(offsets, (0, 1, 3, 2)),
        jnp.asarray(square_table),
        jnp.asarray(shape_table),
        ref_gradient,
        sample_mask,
        deformed_scan,
        reference_scan,
        interp_weights,
    )
    increment, residual = pl.pallas_call(
        functools.partial(format_kernel, depth),
        out_shape=(part, part),
        in_specs=[whole],
        out_specs=(whole, whole),
        compiler_params=pltpu.CompilerParams(vmem_limit_bytes=2**21),
        name="format",
    )(packed)

    def nodal(value):
        return jnp.transpose(value, (0, 2, 3, 1))

    return (nodal(increment), nodal(residual))


def solution(mesh):
    return jax.shard_map(
        per_device,
        mesh=mesh,
        in_specs=(
            P("gx", "gy", None),
            P(None, "gx", "gy", None),
            P("gx", "gy", None),
            P("gx", "gy", None),
            P("gx", "gy", None),
            P("gx", "gy"),
            P(None, "gx", "gy", None),
        ),
        out_specs=(P(None, "gx", "gy", None), P(None, "gx", "gy", None)),
        check_vma=False,
    )
```
